32 devices in a mesh: img: 4 (over z), ty: 4 (over y, core), tx: 2 (over x).
Axes of the slice: x: 2, y: 2, z: 4, core: 2. Of those that a mesh axis runs over, the one named last changes fastest.
Arguments:
- block_in: float32 [4, 64, 16, 1152], P('img', 'ty', 'tx'), may hold values from -6 to 6
- bucket: int32 [4], P('img'), may hold values from 0 to 31
- tile_anchor: int32 [4, 4, 2, 2], P('img', 'ty', 'tx'), may hold values from 0 to 255
- cond_table: float32 [32, 1152], replicated, may hold values from -6 to 6
- mod_weight: bfloat16 [1152, 6912], P(None, ('ty', 'tx')), may hold values from -0.1875 to 0.1875
- mod_bias: float32 [6912], P(('ty', 'tx')), may hold values from -3 to 3
- qkv_weight: bfloat16 [1152, 3456], replicated, may hold values from -0.1875 to 0.1875
- query_gain: float32 [72], replicated, may hold values from 0.5 to 1.5
- key_gain: float32 [72], replicated, may hold values from 0.5 to 1.5
- out_weight: bfloat16 [1152, 1152], replicated, may hold values from -3.5 to 3.5
- gate_up_weight: bfloat16 [1152, 6144], replicated, may hold values from -0.1875 to 0.1875
- down_weight: bfloat16 [3072, 1152], replicated, may hold values from -0.109375 to 0.109375
- cotangent: float32 [4, 64, 16, 1152], P('img', 'ty', 'tx'), may hold values from -6 to 6
Outputs:
- output: float32 [4, 64, 16, 1152], P('img', 'ty', 'tx')
- in_grad: float32 [4, 64, 16, 1152], P('img', 'ty', 'tx')
- table_grad: float32 [32, 1152], P(('ty', 'tx'), 'img')
- modw_grad: float32 [1152, 6912], P('img', ('ty', 'tx'))
- modb_grad: float32 [6912], P(('ty', 'tx'))
- qkv_grad: float32 [1152, 3456], P(('ty', 'tx'), 'img')
- qgain_grad: float32 [72], replicated
- kgain_grad: float32 [72], replicated
- outw_grad: float32 [1152, 1152], P(('ty', 'tx'), 'img')
- gateup_grad: float32 [1152, 6144], P(('ty', 'tx'), 'img')
- down_grad: float32 [3072, 1152], P(('ty', 'tx'), 'img')
The draws below stay inside these ranges and needn't reach their ends.
All inputs are finite; a program needn't handle non-finite values.
Results may differ from the reference program's by a relative error of at most 0.017.
Values may be sent and summed in bfloat16 or wider, within the bound.
No kernel may reach another device: no remote copies, remote signals or barrier semaphores. Data moves between devices by JAX's collectives and lax.ppermute only.
A program may use at most 256 MiB of HBM per device.

```python
import math
import jax
import jax.numpy as jnp
from jax import lax

D = 1152
HEADS = 16
HD = 72
FF = 3072
NB = 32
TH = 16
TW = 8
IMAGES = 4
H = 64
W = 16
SEQ = 1024
N_TY = 4
N_TX = 2


def place_ends(array, key, least, largest):
    longest = array.shape.index(max(array.shape))
    spots = []
    for shift in (0, 1):
        where = [jax.random.randint(jax.random.fold_in(key, axis), (), 0, length) for axis, length in enumerate(array.shape)]
        where[longest] = (where[longest] + shift) % array.shape[longest]
        spots.append(tuple(where))
    return array.at[spots[0]].set(least).at[spots[1]].set(largest)


def steps_of(rng, dims, split, low, largest):
    gain, own = 1.0, jax.random.fold_in(rng, 6)
    for dim, blocks in split:
        heights = jnp.exp(jax.random.uniform(jax.random.fold_in(own, dim), (blocks,), jnp.float32, low / len(split), largest / len(split)))
        gain = gain * jnp.repeat(heights, dims[dim] // blocks).reshape([-1 if axis == dim else 1 for axis in range(len(dims))])
    return gain


def scatter_about(stream_key, dims, spread, limit, split=(), kind=jnp.bfloat16):
    level = steps_of(stream_key, dims, split, -0.22, 0.18) if split else 1.0
    array = jax.random.normal(stream_key, dims, jnp.float32) * spread * level
    return jnp.minimum(jnp.maximum(array, -limit), limit).astype(kind)


def setup_inputs(seed: int = 0) -> dict:
    key_list = jax.random.split(jax.random.key(seed), 14)
    return {
        "block_in": scatter_about(key_list[0], (IMAGES, H, W, D), 1.0, 6.0, ((0, 4), (1, 4), (2, 2)), jnp.float32),
        "bucket": place_ends(jax.random.randint(key_list[1], (IMAGES,), 0, NB), jax.random.fold_in(key_list[1], 1), 0, NB - 1).astype(jnp.int32),
        "tile_anchor": place_ends(jax.random.randint(key_list[2], (IMAGES, N_TY, N_TX, 2), 0, 256), jax.random.fold_in(key_list[2], 1), 0, 255).astype(jnp.int32),
        "cond_table": scatter_about(key_list[3], (NB, D), 1.0, 6.0, (), jnp.float32),
        "mod_weight": scatter_about(key_list[4], (D, 6 * D), D ** -0.5, 0.1875, ((1, 8),)),
        "mod_bias": scatter_about(key_list[5], (6 * D,), 0.5, 3.0, ((0, 8),), jnp.float32),
        "qkv_weight": scatter_about(key_list[6], (D, 3 * D), D ** -0.5, 0.1875),
        "query_gain": jnp.clip(1.0 + 0.1 * jax.random.normal(key_list[7], (HD,), jnp.float32), 0.5, 1.5),
        "key_gain": jnp.clip(1.0 + 0.1 * jax.random.normal(key_list[8], (HD,), jnp.float32), 0.5, 1.5),
        "out_weight": scatter_about(key_list[9], (D, D), (max(1, 3 * D // SEQ)) ** -0.5, 3.5),
        "gate_up_weight": scatter_about(key_list[10], (D, 2 * FF), D ** -0.5, 0.1875),
        "down_weight": scatter_about(key_list[11], (FF, D), FF ** -0.5, 0.109375),
        "cotangent": scatter_about(key_list[12], (IMAGES, H, W, D), 1.0, 6.0, ((0, 4), (1, 4), (2, 2)), jnp.float32),
    }


@jax.custom_vjp
def low(v):
    return lax.optimization_barrier(v.astype(jnp.bfloat16)).astype(jnp.float32)

@jax.custom_vjp
def low_back(v):
    return v

def low_keep(v):
    return (low(v), None)

def low_pass(kept, grad):
    return (grad,)

def back_keep(v):
    return (v, None)

def back_low(kept, grad):
    return (low(grad),)
low.defvjp(low_keep, low_pass)
low_back.defvjp(back_keep, back_low)
EPS = 1e-06
PRECISE = lax.Precision.HIGHEST

def exact_dot(left, right):
    return jnp.dot(left, right, precision=PRECISE, preferred_element_type=jnp.float32)

def normed(value):
    return value * lax.rsqrt(lax.optimization_barrier(jnp.mean(value * value, axis=-1, keepdims=True)) + EPS)

def rotate(value, tables):
    row_cos, row_sin, col_cos, col_sin = tables
    quarter = value.shape[-1] // 4
    first = value[..., :quarter]
    second = value[..., quarter:2 * quarter]
    third = value[..., 2 * quarter:3 * quarter]
    fourth = value[..., 3 * quarter:]
    return jnp.concatenate([first * row_cos - second * row_sin, second * row_cos + first * row_sin, third * col_cos - fourth * col_sin, fourth * col_cos + third * col_sin], axis=-1)

def image_block(inputs, modulation, tables, params):
    qkv_weight, query_gain, key_gain, out_weight, gate_up_weight, down_weight = params
    model_width = inputs.shape[-1]
    seq_len = inputs.shape[0]
    pieces = [modulation[index * model_width:(index + 1) * model_width] for index in range(6)]
    shift_in, scale_in, gate_in, shift_mid, scale_mid, gate_mid = pieces
    hidden = low(normed(inputs) * (1.0 + scale_in) + shift_in)
    qkv = low_back(exact_dot(hidden, qkv_weight))
    query = qkv[:, :model_width].reshape(seq_len, HEADS, HD)
    keyraw = qkv[:, model_width:2 * model_width].reshape(seq_len, HEADS, HD)
    query = low(rotate(normed(query) * query_gain, tables))
    keys = low(rotate(normed(keyraw) * key_gain, tables))
    values = low(qkv[:, 2 * model_width:].reshape(seq_len, HEADS, HD))
    block = min(512, seq_len)

    def attend(query_block):
        scores = low_back(jnp.einsum('qhd,khd->hqk', query_block, keys, precision=PRECISE) * HD ** (-0.5))
        probs = jax.nn.softmax(scores, axis=-1)
        mixed = jnp.einsum('hqk,khd->qhd', low(probs), values, precision=PRECISE)
        return low_back(low(mixed.reshape(block, model_width)))
    attended = lax.map(jax.checkpoint(attend), query.reshape(seq_len // block, block, HEADS, HD))
    attended = attended.reshape(seq_len, model_width)
    middle = inputs + gate_in * low_back(exact_dot(attended, out_weight))
    hidden_mid = low(normed(middle) * (1.0 + scale_mid) + shift_mid)
    gate_up = low_back(exact_dot(hidden_mid, gate_up_weight))
    activ = low(jax.nn.silu(gate_up[:, :FF]) * gate_up[:, FF:])
    return middle + gate_mid * low_back(exact_dot(activ, down_weight))

def forward(inputs, cond_table, mod_weight, mod_bias, params, bucket, tables):
    onehot = (bucket[:, None] == jnp.arange(NB, dtype=jnp.int32)[None, :]).astype(cond_table.dtype)
    condition = exact_dot(onehot, cond_table)
    modulation = exact_dot(low(jax.nn.silu(condition)), mod_weight) + mod_bias

    def step(carry, item):
        image, mod_row, table_row = item
        return (carry, image_block(image, mod_row, table_row, params))
    unused, outputs = lax.scan(step, None, (inputs, modulation, tables))
    return outputs

def reference(block_in, bucket, tile_anchor, cond_table, mod_weight, mod_bias, qkv_weight, query_gain, key_gain, out_weight, gate_up_weight, down_weight, cotangent):
    images = block_in.shape[0]
    seq_len = TH * N_TY * TW * N_TX
    model_width = block_in.shape[-1]
    inputs = block_in.reshape(images, seq_len, model_width).astype(jnp.float32)
    full_shape = (images, N_TY, TH, N_TX, TW)
    row_pos = tile_anchor[..., 0][:, :, None, :, None] + jnp.arange(TH, dtype=jnp.int32)[None, None, :, None, None]
    col_pos = tile_anchor[..., 1][:, :, None, :, None] + jnp.arange(TW, dtype=jnp.int32)[None, None, None, None, :]
    row_pos = jnp.broadcast_to(row_pos, full_shape).reshape(images, seq_len).astype(jnp.float32)
    col_pos = jnp.broadcast_to(col_pos, full_shape).reshape(images, seq_len).astype(jnp.float32)
    quarter = HD // 4
    frequency = jnp.exp(-math.log(10000.0) * jnp.arange(quarter, dtype=jnp.float32) / quarter)
    row_angle = row_pos[:, :, None, None] * frequency
    col_angle = col_pos[:, :, None, None] * frequency
    tables = (jnp.cos(row_angle), jnp.sin(row_angle), jnp.cos(col_angle), jnp.sin(col_angle))

    def wrapped(inputs, cond_table, mod_weight, mod_bias, qkv_weight, query_gain, key_gain, out_weight, gate_up_weight, down_weight):
        params = (qkv_weight, query_gain, key_gain, out_weight, gate_up_weight, down_weight)
        return forward(inputs, cond_table, mod_weight, mod_bias, params, bucket, tables)
    output, pull = jax.vjp(wrapped, inputs, cond_table.astype(jnp.float32), mod_weight.astype(jnp.float32), mod_bias.astype(jnp.float32), qkv_weight.astype(jnp.float32), query_gain.astype(jnp.float32), key_gain.astype(jnp.float32), out_weight.astype(jnp.float32), gate_up_weight.astype(jnp.float32), down_weight.astype(jnp.float32))
    grads = pull(cotangent.reshape(images, seq_len, model_width).astype(jnp.float32))
    return (output.reshape(block_in.shape), grads[0].reshape(block_in.shape), grads[1], grads[2], grads[3], grads[4], grads[5], grads[6], grads[7], grads[8], grads[9])
```

```python
import functools
import math

import jax
import jax.numpy as jnp
from jax import lax
from jax.experimental import pallas as pl
from jax.experimental.pallas import tpu as pltpu
from jax.sharding import PartitionSpec as P

HEADS = 16
HD = 72


EPS = 1e-06
PRECISE = lax.Precision.HIGHEST


def normed(value):
    return value * lax.rsqrt(jnp.mean(value * value, axis=-1, keepdims=True) + EPS)


def norm_back(value, upstream):
    inverse = lax.rsqrt(jnp.mean(value * value, axis=-1, keepdims=True) + EPS)
    unit_value = value * inverse
    return inverse * (
        upstream - unit_value * jnp.mean(upstream * unit_value, axis=-1, keepdims=True)
    )


def rotate(value, tables, turning):
    row_cos, row_sin, col_cos, col_sin = tables
    quarter = value.shape[-1] // 4
    first = value[..., :quarter]
    second = value[..., quarter : 2 * quarter]
    third = value[..., 2 * quarter : 3 * quarter]
    fourth = value[..., 3 * quarter :]
    row_turn = turning * row_sin
    col_turn = turning * col_sin
    return jnp.concatenate(
        [
            first * row_cos - second * row_turn,
            second * row_cos + first * row_turn,
            third * col_cos - fourth * col_turn,
            fourth * col_cos + third * col_turn,
        ],
        axis=-1,
    )


def silu_slope(value):
    sigma = jax.nn.sigmoid(value)
    return sigma * (1.0 + value * (1.0 - sigma))


def product(left, right):
    return jnp.einsum("ik,kj->ij", left, right, preferred_element_type=jnp.float32)


def product_rt(left, right):
    return jnp.einsum("ik,jk->ij", left, right, preferred_element_type=jnp.float32)


def product_lt(left, right):
    return jnp.einsum("ki,kj->ij", left, right, preferred_element_type=jnp.float32)


def on_device(
    block_in,
    bucket,
    tile_anchor,
    cond_table,
    mod_weight,
    mod_bias,
    qkv_weight,
    query_gain,
    key_gain,
    out_weight,
    gate_up_weight,
    down_weight,
    cotangent,
):
    images, tile_rows, tile_cols, model_width = block_in.shape
    tokens = tile_rows * tile_cols
    all_rows = images * tokens
    head_count = HEADS
    head_size = HD
    score_scale = head_size ** (-0.5)
    hidden_units = down_weight.shape[0]
    onehot = (bucket[:, None] == jnp.arange(cond_table.shape[0], dtype=jnp.int32)[None, :]).astype(
        jnp.float32
    )
    condition = jnp.dot(onehot, cond_table, precision=PRECISE)
    cond_act = jax.nn.silu(condition).astype(jnp.bfloat16)
    mod_part = product(cond_act, mod_weight) + mod_bias[None, :]
    modulation = lax.all_gather(mod_part, ("ty", "tx"), axis=1, tiled=True)
    pieces = [
        modulation[:, None, index * model_width : (index + 1) * model_width] for index in range(6)
    ]
    shift_in, scale_in, gate_in, shift_mid, scale_mid, gate_mid = pieces
    places = jnp.arange(tokens, dtype=jnp.int32)
    row_pos = (tile_anchor[:, 0, 0, 0][:, None] + places[None, :] // tile_cols).astype(jnp.float32)
    col_pos = (tile_anchor[:, 0, 0, 1][:, None] + places[None, :] % tile_cols).astype(jnp.float32)
    quarter = head_size // 4
    frequency = jnp.exp(-math.log(10000.0) * jnp.arange(quarter, dtype=jnp.float32) / quarter)
    row_angle = row_pos[:, :, None, None] * frequency
    col_angle = col_pos[:, :, None, None] * frequency
    tables = (jnp.cos(row_angle), jnp.sin(row_angle), jnp.cos(col_angle), jnp.sin(col_angle))
    inputs = block_in.reshape(images, tokens, model_width)
    normed_in = normed(inputs)
    hidden_in = (
        (normed_in * (1.0 + scale_in) + shift_in)
        .astype(jnp.bfloat16)
        .reshape(all_rows, model_width)
    )
    qkv = product(hidden_in, qkv_weight).reshape(images, tokens, 3 * model_width)
    query_raw = qkv[..., :model_width].reshape(images, tokens, head_count, head_size)
    key_raw = qkv[..., model_width : 2 * model_width].reshape(images, tokens, head_count, head_size)
    query_unit = normed(query_raw)
    key_unit = normed(key_raw)
    query_low = rotate(query_unit * query_gain, tables, 1.0).astype(jnp.bfloat16)
    key_low = rotate(key_unit * key_gain, tables, 1.0).astype(jnp.bfloat16)
    value_low = qkv[..., 2 * model_width :].astype(jnp.bfloat16)
    keys_all, values_all = (
        lax.all_gather(
            key_low.reshape(images, tokens, model_width), ("ty", "tx"), axis=1, tiled=True
        ),
        lax.all_gather(value_low, ("ty", "tx"), axis=1, tiled=True),
    )
    key_heads = keys_all.reshape(images, -1, head_count, head_size)
    value_heads = values_all.reshape(images, -1, head_count, head_size)

    def attend(items):
        query_img, key_img, value_img = items
        scores = (
            jnp.einsum("qhd,khd->hqk", query_img, key_img, preferred_element_type=jnp.float32)
            * score_scale
        )
        row_max = jnp.max(scores, axis=-1, keepdims=True)
        expo = jnp.exp(scores - row_max)
        row_sum = jnp.sum(expo, axis=-1, keepdims=True)
        mixed = jnp.einsum(
            "hqk,khd->qhd",
            (expo / row_sum).astype(jnp.bfloat16),
            value_img,
            preferred_element_type=jnp.float32,
        )
        return (mixed, (row_max + jnp.log(row_sum))[:, :, 0])

    mixed_full, log_total = lax.map(attend, (query_low, key_heads, value_heads))
    attended = mixed_full.reshape(all_rows, model_width).astype(jnp.bfloat16)
    attn_out = product(attended, out_weight).reshape(images, tokens, model_width)
    middle = inputs + gate_in * attn_out
    normed_mid = normed(middle)
    hidden_mid = (
        (normed_mid * (1.0 + scale_mid) + shift_mid)
        .astype(jnp.bfloat16)
        .reshape(all_rows, model_width)
    )

    def feed(hidden_value):
        gate_up = product(hidden_value, gate_up_weight)
        return (gate_up[:, :hidden_units], gate_up[:, hidden_units:])

    gate_pre, up_pre = feed(hidden_mid)
    activ = (jax.nn.silu(gate_pre) * up_pre).astype(jnp.bfloat16)
    mlp_out = product(activ, down_weight).reshape(images, tokens, model_width)
    output = middle + gate_mid * mlp_out
    upstream = cotangent.reshape(images, tokens, model_width)
    gmid_grad = jnp.sum(upstream * mlp_out, axis=1)
    mlp_grad = (gate_mid * upstream).astype(jnp.bfloat16).reshape(all_rows, model_width)
    down_grad = product_lt(activ, mlp_grad)
    activ_grad = product_rt(mlp_grad, down_weight)
    gate_pre, up_pre = feed(hidden_mid)
    gu_grad = jnp.concatenate(
        [activ_grad * up_pre * silu_slope(gate_pre), activ_grad * jax.nn.silu(gate_pre)], axis=1
    ).astype(jnp.bfloat16)
    gateup_grad = product_lt(hidden_mid, gu_grad)
    mid_grad = product_rt(gu_grad, gate_up_weight).reshape(images, tokens, model_width)
    smid_grad = jnp.sum(mid_grad, axis=1)
    cmid_grad = jnp.sum(mid_grad * normed_mid, axis=1)
    middle_grad = upstream + norm_back(middle, mid_grad * (1.0 + scale_mid))
    gin_grad = jnp.sum(middle_grad * attn_out, axis=1)
    attn_grad = (gate_in * middle_grad).astype(jnp.bfloat16).reshape(all_rows, model_width)
    outw_grad = product_lt(attended, attn_grad)
    attended_grad = (
        product_rt(attn_grad, out_weight)
        .astype(jnp.bfloat16)
        .reshape(images, tokens, head_count, head_size)
    )
    row_delta = jnp.swapaxes(jnp.sum(attended_grad.astype(jnp.float32) * mixed_full, axis=-1), 1, 2)

    def score_parts(query_img, key_img, value_img, grad_img, total_img, delta_img):
        scores = (
            jnp.einsum("qhd,khd->hqk", query_img, key_img, preferred_element_type=jnp.float32)
            * score_scale
        )
        probs = jnp.exp(scores - total_img[:, :, None])
        prob_grad = jnp.einsum(
            "qhd,khd->hqk", grad_img, value_img, preferred_element_type=jnp.float32
        )
        score_grad = (probs * (prob_grad - delta_img[:, :, None])).astype(jnp.bfloat16)
        return (probs.astype(jnp.bfloat16), score_grad)

    def grads_all(items):
        query_img, key_img, value_img, grad_img, total_img, delta_img = items
        probs_low, score_grad = score_parts(
            query_img, key_img, value_img, grad_img, total_img, delta_img
        )
        query_part = (
            jnp.einsum("hqk,khd->qhd", score_grad, key_img, preferred_element_type=jnp.float32)
            * score_scale
        )
        key_part = (
            jnp.einsum("hqk,qhd->khd", score_grad, query_img, preferred_element_type=jnp.float32)
            * score_scale
        )
        value_part = jnp.einsum(
            "hqk,qhd->khd", probs_low, grad_img, preferred_element_type=jnp.float32
        )
        return (query_part, key_part.reshape(-1, model_width), value_part.reshape(-1, model_width))

    query_grad, key_full, value_full = lax.map(
        grads_all, (query_low, key_heads, value_heads, attended_grad, log_total, row_delta)
    )
    key_grad, value_grad = (
        lax.psum_scatter(
            key_full.astype(jnp.bfloat16), ("ty", "tx"), scatter_dimension=1, tiled=True
        ).astype(jnp.float32),
        lax.psum_scatter(
            value_full.astype(jnp.bfloat16), ("ty", "tx"), scatter_dimension=1, tiled=True
        ).astype(jnp.float32),
    )
    query_turned = rotate(query_grad, tables, -1.0)
    key_turned = rotate(key_grad.reshape(images, tokens, head_count, head_size), tables, -1.0)
    qgain_part = jnp.sum(query_turned * query_unit, axis=(0, 1, 2))
    kgain_part = jnp.sum(key_turned * key_unit, axis=(0, 1, 2))
    query_back = norm_back(query_raw, query_turned * query_gain).reshape(
        images, tokens, model_width
    )
    key_back = norm_back(key_raw, key_turned * key_gain).reshape(images, tokens, model_width)
    qkv_back = jnp.concatenate([query_back, key_back, value_grad], axis=-1).astype(jnp.bfloat16)
    qkv_back = qkv_back.reshape(all_rows, 3 * model_width)
    qkv_part = product_lt(hidden_in, qkv_back)
    in_back = product_rt(qkv_back, qkv_weight).reshape(images, tokens, model_width)
    sin_grad = jnp.sum(in_back, axis=1)
    cin_grad = jnp.sum(in_back * normed_in, axis=1)
    in_grad = middle_grad + norm_back(inputs, in_back * (1.0 + scale_in))
    mod_grad = jnp.concatenate(
        [sin_grad, cin_grad, gin_grad, smid_grad, cmid_grad, gmid_grad], axis=1
    )
    mod_cols = lax.psum_scatter(mod_grad, ("ty", "tx"), scatter_dimension=1, tiled=True)
    modw_part = jnp.dot(cond_act.astype(jnp.float32).T, mod_cols, precision=PRECISE)
    modb_part = jnp.sum(mod_cols, axis=0)
    act_grad = jnp.dot(mod_cols, mod_weight.astype(jnp.float32).T, precision=PRECISE)
    cond_grad = act_grad * silu_slope(condition)
    table_part = jnp.dot(onehot.T, cond_grad, precision=PRECISE)
    qkv_share, outw_share, gateup_share, down_share, table_share = (
        lax.psum_scatter(
            qkv_part.astype(jnp.bfloat16), ("ty", "tx"), scatter_dimension=0, tiled=True
        ).astype(jnp.float32),
        lax.psum_scatter(
            outw_grad.astype(jnp.bfloat16), ("ty", "tx"), scatter_dimension=0, tiled=True
        ).astype(jnp.float32),
        lax.psum_scatter(
            gateup_grad.astype(jnp.bfloat16), ("ty", "tx"), scatter_dimension=0, tiled=True
        ).astype(jnp.float32),
        lax.psum_scatter(
            down_grad.astype(jnp.bfloat16), ("ty", "tx"), scatter_dimension=0, tiled=True
        ).astype(jnp.float32),
        lax.psum_scatter(
            table_part.astype(jnp.bfloat16), ("ty", "tx"), scatter_dimension=0, tiled=True
        ).astype(jnp.float32),
    )
    qkv_total, outw_total, gateup_total, down_total, table_total = (
        lax.psum_scatter(
            qkv_share.astype(jnp.bfloat16), "img", scatter_dimension=1, tiled=True
        ).astype(jnp.float32),
        lax.psum_scatter(
            outw_share.astype(jnp.bfloat16), "img", scatter_dimension=1, tiled=True
        ).astype(jnp.float32),
        lax.psum_scatter(
            gateup_share.astype(jnp.bfloat16), "img", scatter_dimension=1, tiled=True
        ).astype(jnp.float32),
        lax.psum_scatter(
            down_share.astype(jnp.bfloat16), "img", scatter_dimension=1, tiled=True
        ).astype(jnp.float32),
        lax.psum_scatter(
            table_share.astype(jnp.bfloat16), "img", scatter_dimension=1, tiled=True
        ).astype(jnp.float32),
    )
    modw_total = lax.psum_scatter(
        modw_part.astype(jnp.bfloat16), "img", scatter_dimension=0, tiled=True
    ).astype(jnp.float32)
    modb_total = lax.psum(modb_part, "img")
    qgain_total, kgain_total = lax.psum((qgain_part, kgain_part), ("img", "ty", "tx"))
    return (
        output.reshape(block_in.shape),
        in_grad.reshape(block_in.shape),
        table_total,
        modw_total,
        modb_total,
        qkv_total,
        qgain_total,
        kgain_total,
        outw_total,
        gateup_total,
        down_total,
    )


def sigmoid(value):
    return 1.0 / (1.0 + jnp.exp(-value))


def dot_nn(left, right):
    return lax.dot_general(
        left, right, (((1,), (0,)), ((), ())), preferred_element_type=jnp.float32
    )


def dot_nt(left, right):
    return lax.dot_general(
        left, right, (((1,), (1,)), ((), ())), preferred_element_type=jnp.float32
    )


def dot_tn(left, right):
    return lax.dot_general(
        left, right, (((0,), (0,)), ((), ())), preferred_element_type=jnp.float32
    )


def column_sum(value):
    return jnp.sum(value, axis=0, keepdims=True)


EXTRA = 16
LANES = 128


def open_kernel(
    scalars, x_ref, table_ref, weight_ref, bias_ref, cot_ref, pay_ref, low_ref, wide_ref
):
    tokens, width = x_ref.shape
    columns = weight_ref.shape[1]
    x = x_ref[...]
    pay_ref[0:tokens, :] = normed(x).astype(jnp.bfloat16)
    low_ref[...] = cot_ref[...].astype(jnp.bfloat16)
    row = table_ref[pl.ds(scalars[0], 1), :]
    act = (row * sigmoid(row)).astype(jnp.bfloat16)
    mod = dot_nn(jnp.broadcast_to(act, (8, width)), weight_ref[...]) + bias_ref[...]
    wide_ref[...] = jnp.zeros_like(wide_ref)
    wide_ref[:, 0:columns] = mod
    full = wide_ref[0:1, :]
    high = full.astype(jnp.bfloat16).astype(jnp.float32)
    rest = full - high
    middle = rest.astype(jnp.bfloat16).astype(jnp.float32)
    least = rest - middle
    lane = lax.broadcasted_iota(jnp.int32, (EXTRA, width), 1)
    line = lax.broadcasted_iota(jnp.int32, (EXTRA, width), 0)
    quarter = HD // 4
    anchor = jnp.where(
        lane < 2 * quarter,
        scalars[1].astype(jnp.float32),
        jnp.where(lane < HD, scalars[2].astype(jnp.float32), 0.0),
    )
    extra = jnp.where(
        line == 0,
        high,
        jnp.where(
            line == 1, middle, jnp.where(line == 2, least, jnp.where(line == 3, anchor, 0.0))
        ),
    )
    pay_ref[tokens : tokens + EXTRA, :] = extra.astype(jnp.bfloat16)


def partner(value):
    quarter = HD // 4
    lane = lax.broadcasted_iota(jnp.int32, value.shape, 1)
    ahead = pltpu.roll(value, LANES - quarter, 1)
    behind = pltpu.roll(value, quarter, 1)
    return jnp.where((lane // quarter) % 2 == 0, ahead, behind)


def unit_rate(raw):
    return lax.rsqrt(jnp.sum(raw * raw, axis=-1, keepdims=True) * (1.0 / HD) + EPS)


def wide_gain(gain_ref, scratch):
    scratch[...] = jnp.zeros_like(scratch)
    scratch[0:1, 0:HD] = gain_ref[...]
    return scratch[0:1, :]


def attend_kernel(
    blocks,
    tile_cols,
    scalars,
    *refs,
):
    pieces, refs = refs[:10], refs[10:]
    (
        weight_ref,
        qgain_ref,
        kgain_ref,
        att_ref,
        hid_ref,
        qkv_ref,
        raw_ref,
        turn_ref,
        mod_ref,
        spread_ref,
        rows_ref,
        flat_ref,
        anchor_ref,
        gain_ref,
        vt_ref,
    ) = refs
    mine = scalars[0]
    own, core, xn, yn, d1, d2, cx, cy, cd1, cd2 = pieces
    width = own.shape[1]
    tokens = own.shape[0] - EXTRA
    columns = 6 * width // blocks
    half = d1.shape[0]
    everyone = blocks * tokens
    heads = HEADS // blocks
    extras = {
        0: own[tokens:, :],
        1: xn[tokens:, :],
        2: core[tokens:, :],
        3: cx[tokens:, :],
        4: yn[tokens:, :],
        5: d2[tokens - half :, :],
        6: cy[tokens:, :],
        7: cd2[tokens - half :, :],
    }
    for index, extra in extras.items():
        extra = extra.astype(jnp.float32)
        place = mine ^ index
        rows_ref[pl.ds(place, 1), :] = extra[0:1] + extra[1:2] + extra[2:3]
        anchor_ref[0, pl.ds(place, 1), :] = extra[3:4, 0:LANES]
    for index in range(blocks):
        flat_ref[0:1, columns * index : columns * (index + 1)] = rows_ref[
            index : index + 1, 0:columns
        ]
    mod_ref[...] = jnp.zeros_like(mod_ref)
    for index in range(6):
        mod_ref[index : index + 1, :] = flat_ref[0:1, width * index : width * (index + 1)]
    shift_in = mod_ref[0:1, :]
    scale_in = 1.0 + mod_ref[1:2, :]

    def place_tokens(index, ref, rows, offset):
        low = ref[0:rows, :].astype(jnp.float32) * scale_in + shift_in
        start = pl.multiple_of((mine ^ index) * tokens + offset, 16)
        hid_ref[pl.ds(start, rows), :] = low.astype(jnp.bfloat16)

    for index, ref in ((0, own), (1, xn), (2, core), (3, cx), (4, yn), (6, cy)):
        place_tokens(index, ref, tokens, 0)
    for index, first, second in ((5, d1, d2), (7, cd1, cd2)):
        place_tokens(index, first, half, 0)
        place_tokens(index, second, tokens - half, half)

    quarter = HD // 4
    lane = lax.broadcasted_iota(jnp.int32, (tokens, LANES), 1)
    token = lax.broadcasted_iota(jnp.int32, (tokens, LANES), 0)
    rate = jnp.where(
        lane < HD,
        jnp.exp((lane % quarter).astype(jnp.float32) * (-math.log(10000.0) / quarter)),
        0.0,
    )
    offset = jnp.where(lane < 2 * quarter, token // tile_cols, token % tile_cols)
    offset = offset.astype(jnp.float32) * rate
    offset_cos, offset_sin = jnp.cos(offset), jnp.sin(offset)
    anchor = anchor_ref[0] * rate[0:blocks]
    anchor_ref[0] = jnp.cos(anchor)
    anchor_ref[1] = jnp.sin(anchor)
    sign = jnp.where((lane // quarter) % 2 == 0, -1.0, 1.0)

    spread_ref[...] = jnp.zeros_like(spread_ref)
    for index in range(3 * heads):
        spread_ref[:, LANES * index : LANES * index + HD] = weight_ref[
            :, HD * index : HD * (index + 1)
        ]
    query_gain = wide_gain(qgain_ref, gain_ref.at[0])
    key_gain = wide_gain(kgain_ref, gain_ref.at[1])

    def project(index, carry):
        rows = pl.ds(pl.multiple_of(index * tokens, tokens), tokens)
        anchor_cos = anchor_ref[0, pl.ds(index, 1), :]
        anchor_sin = anchor_ref[1, pl.ds(index, 1), :]
        turn_cos = anchor_cos * offset_cos - anchor_sin * offset_sin
        turn_sin = (anchor_sin * offset_cos + anchor_cos * offset_sin) * sign
        turn_ref[0, rows, :] = turn_cos
        turn_ref[1, rows, :] = turn_sin
        product = dot_nn(hid_ref[rows, :], spread_ref[...])
        for part in range(2 * heads):
            raw = product[:, LANES * part : LANES * (part + 1)]
            raw_ref[part, rows, :] = raw
            unit = raw * unit_rate(raw) * (query_gain if part < heads else key_gain)
            turned = unit * turn_cos + partner(unit) * turn_sin
            qkv_ref[part, rows, :] = turned.astype(jnp.bfloat16)
        for part in range(2 * heads, 3 * heads):
            qkv_ref[part, rows, :] = product[:, LANES * part : LANES * (part + 1)].astype(
                jnp.bfloat16
            )
        return carry

    lax.fori_loop(0, blocks, project, 0)
    scale = HD ** (-0.5) * math.log2(math.e)
    chunk = 2 * tokens
    for head in range(heads):
        keys = qkv_ref[heads + head]
        vt_ref[...] = qkv_ref[2 * heads + head].T

        def attend(index, carry):
            rows = pl.ds(pl.multiple_of(index * chunk, chunk), chunk)
            scores = dot_nt(keys, qkv_ref[head, rows, :])
            expo = jnp.exp2(scores * scale)
            total = column_sum(expo)
            mixed = dot_nn(vt_ref[...], expo.astype(jnp.bfloat16)) * (1.0 / total)
            att_ref[rows, LANES * head : LANES * (head + 1)] = mixed.T.astype(jnp.bfloat16)
            return carry

        lax.fori_loop(0, everyone // chunk, attend, 0)


def middle_kernel(att_ref, weight_ref, x_ref, mod_ref, out_ref, mid_ref, hid_ref):
    blocks = att_ref.shape[0]
    heads = HEADS // blocks
    attended = jnp.concatenate(
        [
            att_ref[index, :, LANES * head : LANES * head + HD]
            for index in range(blocks)
            for head in range(heads)
        ],
        axis=1,
    )
    attn_out = dot_nn(attended, weight_ref[...])
    out_ref[...] = attn_out
    middle = x_ref[...] + mod_ref[2:3, :] * attn_out
    mid_ref[...] = middle
    hid_ref[...] = (normed(middle) * (1.0 + mod_ref[4:5, :]) + mod_ref[3:4, :]).astype(
        jnp.bfloat16
    )


def mlp_kernel(
    gate_ref,
    up_ref,
    down_ref,
    outw_ref,
    hid_ref,
    mid_ref,
    attn_ref,
    cot_ref,
    mod_ref,
    output_ref,
    mgrad_ref,
    agrad_ref,
    dgrad_ref,
    sums_ref,
    low_ref,
    mlp_ref,
    back_ref,
):
    step = pl.program_id(0)
    blocks = dgrad_ref.shape[0]
    heads = HEADS // blocks
    gate_mid = mod_ref[5:6, :]

    @pl.when(step == 0)
    def _():
        low_ref[...] = (gate_mid * cot_ref[...]).astype(jnp.bfloat16)
        mlp_ref[...] = jnp.zeros_like(mlp_ref)
        back_ref[...] = jnp.zeros_like(back_ref)

    hidden = hid_ref[...]
    gate = dot_nn(hidden, gate_ref[...])
    up = dot_nn(hidden, up_ref[...])
    sigma = sigmoid(gate)
    silu = gate * sigma
    act = (silu * up).astype(jnp.bfloat16)
    mlp_ref[...] += dot_nn(act, down_ref[...])
    act_grad = dot_nt(low_ref[...], down_ref[...])
    slope = sigma * (1.0 + gate * (1.0 - sigma))
    gate_grad = (act_grad * up * slope).astype(jnp.bfloat16)
    up_grad = (act_grad * silu).astype(jnp.bfloat16)
    back_ref[...] += dot_nt(gate_grad, gate_ref[...]) + dot_nt(up_grad, up_ref[...])

    @pl.when(step == pl.num_programs(0) - 1)
    def _():
        middle = mid_ref[...]
        upstream = cot_ref[...]
        mlp_out = mlp_ref[...]
        output_ref[...] = middle + gate_mid * mlp_out
        back = back_ref[...]
        inverse = lax.rsqrt(jnp.mean(middle * middle, axis=-1, keepdims=True) + EPS)
        unit = middle * inverse
        lifted = back * (1.0 + mod_ref[4:5, :])
        middle_grad = upstream + inverse * (
            lifted - unit * jnp.mean(lifted * unit, axis=-1, keepdims=True)
        )
        mgrad_ref[...] = middle_grad
        attn_grad = (mod_ref[2:3, :] * middle_grad).astype(jnp.bfloat16)
        agrad_ref[...] = attn_grad
        dgrad_ref[...] = jnp.zeros_like(dgrad_ref)
        for index in range(blocks):
            rows = outw_ref[HD * heads * index : HD * heads * (index + 1), :]
            part = dot_nt(attn_grad, rows).astype(jnp.bfloat16)
            for head in range(heads):
                dgrad_ref[index, :, LANES * head : LANES * head + HD] = part[
                    :, HD * head : HD * (head + 1)
                ]
        sums_ref[...] = jnp.zeros_like(sums_ref)
        sums_ref[2:3, :] = column_sum(middle_grad * attn_ref[...])
        sums_ref[3:4, :] = column_sum(back)
        sums_ref[4:5, :] = column_sum(back * unit)
        sums_ref[5:6, :] = column_sum(upstream * mlp_out)


def gather_blocks(pieces, ref, place, tokens):
    own, core, xn, yn, d1, d2, cx, cy, cd1, cd2 = pieces
    half = d1.shape[0]
    for index, piece in ((0, own), (1, xn), (2, core), (3, cx), (4, yn), (6, cy)):
        ref[pl.ds(place(index), tokens), :] = piece[...]
    for index, first, second in ((5, d1, d2), (7, cd1, cd2)):
        ref[pl.ds(place(index), half), :] = first[...]
        ref[pl.ds(place(index) + half, tokens - half), :] = second[...]


def mlp_weights_kernel(scalars, *refs):
    hid_pieces, cot_pieces, refs = refs[:10], refs[10:20], refs[20:]
    gate_ref, up_ref, down_ref, mod_ref, gateup_ref, dgrad_ref, all_ref, low_ref, act_ref = refs
    tokens, width = hid_pieces[0].shape
    blocks = gateup_ref.shape[0]
    rows = width // blocks
    gather_blocks(hid_pieces, all_ref, lambda index: index * tokens, tokens)
    gather_blocks(cot_pieces, low_ref, lambda index: index * tokens, tokens)
    gate_mid = mod_ref[5:6, :]
    units = act_ref.shape[2]

    def chunked(index, carry):
        span = pl.ds(pl.multiple_of(index * tokens, tokens), tokens)
        low = (low_ref[span, :].astype(jnp.float32) * gate_mid).astype(jnp.bfloat16)
        low_ref[span, :] = low
        hidden = all_ref[span, :]
        gate = dot_nn(hidden, gate_ref[...])
        up = dot_nn(hidden, up_ref[...])
        act_grad = dot_nt(low, down_ref[...])
        sigma = sigmoid(gate)
        silu = gate * sigma
        slope = sigma * (1.0 + gate * (1.0 - sigma))
        act_ref[0, span, :] = (silu * up).astype(jnp.bfloat16)
        act_ref[1, span, :] = (act_grad * up * slope).astype(jnp.bfloat16)
        act_ref[2, span, :] = (act_grad * silu).astype(jnp.bfloat16)
        return carry

    lax.fori_loop(0, blocks, chunked, 0)
    down = dot_tn(low_ref[...], act_ref[0]).astype(jnp.bfloat16)
    dgrad_ref[...] = down.reshape(dgrad_ref.shape)
    for side in range(2):
        grad = dot_tn(all_ref[...], act_ref[1 + side]).astype(jnp.bfloat16)
        gateup_ref[:, side, :, :] = grad.reshape(blocks, rows, units)


def attend_back_kernel(
    attg_ref, qkv_ref, raw_ref, turn_ref, qgain_ref, kgain_ref, back_ref, gsum_ref,
    kt_ref, qt_ref, grad_ref, gain_ref,
):
    heads = attg_ref.shape[1] // LANES
    everyone = attg_ref.shape[0]
    chunk = 256
    scale = HD ** (-0.5)
    query_gain = wide_gain(qgain_ref, gain_ref.at[0])
    key_gain = wide_gain(kgain_ref, gain_ref.at[1])
    grad_ref[...] = jnp.zeros_like(grad_ref)
    for head in range(heads):
        keys = qkv_ref[heads + head]
        values = qkv_ref[2 * heads + head]
        kt_ref[...] = keys.T

        def attend(index, carry):
            rows = pl.ds(pl.multiple_of(index * chunk, chunk), chunk)
            query = qkv_ref[head, rows, :]
            upstream = attg_ref[rows, LANES * head : LANES * (head + 1)]
            expo = jnp.exp2(dot_nt(keys, query) * (scale * math.log2(math.e)))
            probs = expo * (1.0 / column_sum(expo))
            weighted = probs * dot_nt(values, upstream)
            score_grad = (weighted - probs * column_sum(weighted)).astype(jnp.bfloat16)
            grad_ref[2 * heads + head] += dot_nn(probs.astype(jnp.bfloat16), upstream)
            grad_ref[heads + head] += dot_nn(score_grad, query)
            grad_ref[head, rows, :] = dot_nn(kt_ref[...], score_grad).T
            return carry

        lax.fori_loop(0, everyone // chunk, attend, 0)
    gsum_ref[...] = jnp.zeros_like(gsum_ref)

    def finish(index, carry):
        rows = pl.ds(pl.multiple_of(index * LANES, LANES), LANES)
        turn_cos = turn_ref[0, rows, :]
        turn_sin = turn_ref[1, rows, :]
        parts = []
        for part in range(2 * heads):
            gain = query_gain if part < heads else key_gain
            grad = grad_ref[part, rows, :] * scale
            turned = grad * turn_cos - partner(grad) * turn_sin
            raw = raw_ref[part, rows, :]
            rate = unit_rate(raw)
            unit = raw * rate
            line = 0 if part < heads else 1
            gsum_ref[line : line + 1, :] += column_sum(turned * unit)
            lifted = turned * gain
            mean = jnp.sum(lifted * unit, axis=-1, keepdims=True) * (1.0 / HD)
            parts.append((rate * (lifted - unit * mean)).astype(jnp.bfloat16))
        for part in range(2 * heads, 3 * heads):
            parts.append(grad_ref[part, rows, :].astype(jnp.bfloat16))
        back_ref[rows, :] = jnp.zeros((LANES, back_ref.shape[1]), jnp.bfloat16)
        back_ref[rows, 0 : 3 * heads * HD] = jnp.concatenate(
            [part[:, 0:HD] for part in parts], axis=1
        )
        return carry

    lax.fori_loop(0, everyone // LANES, finish, 0)


def qkv_weights_kernel(images, scalars, *refs):
    pieces, refs = refs[:10], refs[10:]
    hid_ref, back_ref, att_ref, qgrad_ref, ograd_ref, low_ref = refs
    tokens, width = pieces[0].shape
    mine = scalars[0]
    blocks = hid_ref.shape[0] // tokens
    heads = HEADS // blocks
    gather_blocks(
        pieces, low_ref, lambda index: pl.multiple_of((mine ^ index) * tokens, 16), tokens
    )
    grad = dot_tn(hid_ref[...], back_ref[...]).astype(jnp.bfloat16)
    qgrad_ref[...] = grad.reshape(qgrad_ref.shape)
    outw = dot_tn(att_ref[...], low_ref[...]).astype(jnp.bfloat16)
    share = width // images
    for image in range(images):
        for head in range(heads):
            ograd_ref[image, HD * head : HD * (head + 1), :] = outw[
                LANES * head : LANES * head + HD, share * image : share * (image + 1)
            ]


def join_kernel(images, grad_ref, ograd_ref, out_ref):
    blocks = grad_ref.shape[0]
    span = HD * HEADS // blocks
    whole = jnp.concatenate(
        [
            grad_ref[index][:, span * side : span * (side + 1)]
            for side in range(3)
            for index in range(blocks)
        ],
        axis=1,
    )
    share = whole.shape[1] // images
    for image in range(images):
        out_ref[image] = jnp.concatenate(
            [whole[:, share * image : share * (image + 1)], ograd_ref[image]], axis=1
        )


def input_kernel(
    back_ref, weight_ref, x_ref, mgrad_ref, mod_ref, sums_ref, gsum_ref, scalars,
    grad_ref, send_ref, acc_ref, flat_ref,
):
    step = pl.program_id(0)
    blocks = back_ref.shape[0]
    span = HD * HEADS // blocks
    width = x_ref.shape[1]
    columns = 6 * width // blocks

    for side in range(3):

        @pl.when(step == side)
        def _(side=side):
            natural = jnp.concatenate(
                [back_ref[index, :, span * side : span * (side + 1)] for index in range(blocks)],
                axis=1,
            )
            part = dot_nt(natural, weight_ref[...])
            acc_ref[...] = part if side == 0 else acc_ref[...] + part

    @pl.when(step == 2)
    def _():
        x = x_ref[...]
        back = acc_ref[...]
        inverse = lax.rsqrt(jnp.mean(x * x, axis=-1, keepdims=True) + EPS)
        unit = x * inverse
        lifted = back * (1.0 + mod_ref[1:2, :])
        grad_ref[...] = mgrad_ref[...] + inverse * (
            lifted - unit * jnp.mean(lifted * unit, axis=-1, keepdims=True)
        )
        flat_ref[0:1, 0:width] = column_sum(back)
        flat_ref[0:1, width : 2 * width] = column_sum(back * unit)
        for index in range(2, 6):
            flat_ref[0:1, width * index : width * (index + 1)] = sums_ref[index : index + 1, :]
        send_ref[...] = jnp.zeros_like(send_ref)
        for index in range(blocks):
            send_ref[index : index + 1, 0:columns] = flat_ref[
                0:1, columns * index : columns * (index + 1)
            ]
        send_ref[:, columns : columns + 1] = jnp.broadcast_to(
            scalars[0].astype(jnp.float32), (blocks, 1)
        )
        for line in range(2):
            start = columns + 16 + HD * line
            send_ref[:, start : start + HD] = jnp.broadcast_to(
                gsum_ref[line : line + 1, 0:HD], (blocks, HD)
            )


def whole_spec(shape):
    return pl.BlockSpec(shape, lambda *_: (0,) * len(shape))


def call(kernel, operands, outs, scratch=(), scalars=None, name=None, flops=0):
    moved = sum(math.prod(a.shape) * a.dtype.itemsize for a in (*operands, *outs))
    return pl.pallas_call(
        kernel,
        out_shape=outs,
        grid_spec=pltpu.PrefetchScalarGridSpec(
            num_scalar_prefetch=0 if scalars is None else 1,
            grid=(1,),
            in_specs=[
                pl.BlockSpec(a.shape, lambda *_, n=len(a.shape): (0,) * n) for a in operands
            ],
            out_specs=[
                pl.BlockSpec(o.shape, lambda *_, n=len(o.shape): (0,) * n) for o in outs
            ],
            scratch_shapes=list(scratch),
        ),
        cost_estimate=pl.CostEstimate(flops=flops, transcendentals=0, bytes_accessed=moved),
        name=name,
    )(*(() if scalars is None else (scalars,)), *operands)


def struct(shape, dtype=jnp.float32):
    return jax.ShapeDtypeStruct(shape, dtype)


PLANE = ("ty", "tx")


def swap(value, bit):
    return lax.ppermute(value, PLANE, [(index, index ^ bit) for index in range(8)])


def gather_plane(value, half):
    core, xn, yn = swap(value, 2), swap(value, 1), swap(value, 4)
    d1 = swap(xn[:half], 4)
    cx = swap(xn, 2)
    d2 = swap(yn[half:], 1)
    cy = swap(yn, 2)
    return (value, core, xn, yn, d1, d2, cx, cy, swap(d1, 2), swap(d2, 2))


def exchange(value, axes=PLANE):
    return lax.all_to_all(value, axes, split_axis=0, concat_axis=0, tiled=True)


def line_reduce(pick, images):
    place = lax.axis_index("img")
    rising = falling = None
    for step in range(1, images):
        value = pick(jnp.clip(place + images - step, 0, images - 1))
        if rising is not None:
            value = value + rising.astype(jnp.float32)
        rising = lax.ppermute(
            value.astype(jnp.bfloat16),
            "img",
            [(i, i + 1) for i in range(images - 1) if i + images - step < images],
        )
        value = pick(jnp.clip(place - images + step, 0, images - 1))
        if falling is not None:
            value = value + falling.astype(jnp.float32)
        falling = lax.ppermute(
            value.astype(jnp.bfloat16),
            "img",
            [(i, i - 1) for i in range(1, images) if i - images + step >= 0],
        )
    return pick(place) + rising.astype(jnp.float32) + falling.astype(jnp.float32)


def on_plane(
    images,
    block_in,
    bucket,
    tile_anchor,
    cond_table,
    mod_weight,
    mod_bias,
    qkv_weight,
    query_gain,
    key_gain,
    out_weight,
    gate_up_weight,
    down_weight,
    cotangent,
):
    blocks = 8
    _, tile_rows, tile_cols, width = block_in.shape
    tokens = tile_rows * tile_cols
    everyone = blocks * tokens
    hidden_units = down_weight.shape[0]
    units = hidden_units // blocks
    heads = HEADS // blocks
    span = heads * HD
    columns = mod_weight.shape[1]
    bf16 = jnp.bfloat16
    image = lax.axis_index("img")
    mine = lax.axis_index("ty") * 2 + lax.axis_index("tx")
    where = mine.reshape(1).astype(jnp.int32)
    x = block_in.reshape(tokens, width)
    cot = cotangent.reshape(tokens, width)
    half = tokens // 2
    pay, low_cot = call(
        open_kernel,
        (x, cond_table, mod_weight, mod_bias.reshape(1, columns), cot),
        (struct((tokens + EXTRA, width), bf16), struct((tokens, width), bf16)),
        [pltpu.VMEM((8, width), jnp.float32)],
        jnp.concatenate([bucket, tile_anchor.reshape(2)]),
        "open",
    )
    pieces = gather_plane(pay, half)
    cot_pieces = gather_plane(low_cot, half)
    own_weight = jnp.concatenate(
        [
            lax.dynamic_slice(qkv_weight, (0, width * side + span * mine), (width, span))
            for side in range(3)
        ],
        axis=1,
    )
    gains = (query_gain.reshape(1, HD), key_gain.reshape(1, HD))
    att, hid, qkv, raw, turn, mod = call(
        functools.partial(attend_kernel, blocks, tile_cols),
        (*pieces, own_weight, *gains),
        (
            struct((everyone, LANES * heads), bf16),
            struct((everyone, width), bf16),
            struct((3 * heads, everyone, LANES), bf16),
            struct((2 * heads, everyone, LANES)),
            struct((2, everyone, LANES)),
            struct((8, width)),
        ),
        [
            pltpu.VMEM((width, 3 * heads * LANES), bf16),
            pltpu.VMEM((8, width), jnp.float32),
            pltpu.VMEM((1, 6 * width), jnp.float32),
            pltpu.VMEM((2, 8, LANES), jnp.float32),
            pltpu.VMEM((2, 8, LANES), jnp.float32),
            pltpu.VMEM((LANES, everyone), bf16),
        ],
        where,
        "attend",
        4 * everyone * everyone * LANES * heads,
    )
    att_all = exchange(att.reshape(blocks, tokens, LANES * heads))
    attn_out, middle, hidden_mid = call(
        middle_kernel,
        (att_all, out_weight, x, mod),
        (struct((tokens, width)), struct((tokens, width)), struct((tokens, width), bf16)),
        name="middle",
    )
    hid_pieces = gather_plane(hidden_mid, half)
    steps = blocks
    whole = whole_spec
    output, middle_grad, attn_grad, attg, sums = pl.pallas_call(
        mlp_kernel,
        out_shape=(
            struct((tokens, width)),
            struct((tokens, width)),
            struct((tokens, width), bf16),
            struct((blocks, tokens, LANES * heads), bf16),
            struct((8, width)),
        ),
        grid=(steps,),
        in_specs=[
            pl.BlockSpec((width, units), lambda f: (0, f)),
            pl.BlockSpec((width, units), lambda f: (0, steps + f)),
            pl.BlockSpec((units, width), lambda f: (f, 0)),
            whole(out_weight.shape),
            whole((tokens, width)),
            whole((tokens, width)),
            whole((tokens, width)),
            whole((tokens, width)),
            whole((8, width)),
        ],
        out_specs=(
            whole((tokens, width)),
            whole((tokens, width)),
            whole((tokens, width)),
            whole((blocks, tokens, LANES * heads)),
            whole((8, width)),
        ),
        scratch_shapes=[
            pltpu.VMEM((tokens, width), bf16),
            pltpu.VMEM((tokens, width), jnp.float32),
            pltpu.VMEM((tokens, width), jnp.float32),
        ],
        name="mlp",
    )(gate_up_weight, gate_up_weight, down_weight, out_weight, hidden_mid, middle, attn_out, cot, mod)
    grad_pieces = gather_plane(attn_grad, half)
    gateup_part, down_part = pl.pallas_call(
        mlp_weights_kernel,
        out_shape=(
            struct((blocks, 2, width // blocks, units), bf16),
            struct((images, width // images, units), bf16),
        ),
        grid_spec=pltpu.PrefetchScalarGridSpec(
            num_scalar_prefetch=1,
            grid=(1,),
            in_specs=[
                *(whole(a.shape) for a in (*hid_pieces, *cot_pieces)),
                pl.BlockSpec((width, units), lambda i, s: (0, s[0])),
                pl.BlockSpec((width, units), lambda i, s: (0, blocks + s[0])),
                pl.BlockSpec((units, width), lambda i, s: (s[0], 0)),
                whole((8, width)),
            ],
            out_specs=(
                whole((blocks, 2, width // blocks, units)),
                whole((images, width // images, units)),
            ),
            scratch_shapes=[
                pltpu.VMEM((everyone, width), bf16),
                pltpu.VMEM((everyone, width), bf16),
                pltpu.VMEM((3, everyone, units), bf16),
            ],
        ),
        name="mlp_weights",
    )(where, *hid_pieces, *cot_pieces, gate_up_weight, gate_up_weight, down_weight, mod)
    gateup_rows = exchange(gateup_part)

    def pick_mlp(owner):
        gateup = lax.dynamic_slice(
            gateup_rows,
            (4 * (owner % 2), owner // 2, 0, 0),
            (4, 1, width // blocks, units),
        ).reshape(4 * width // blocks, units)
        down = lax.dynamic_index_in_dim(down_part, owner, 0, False)
        return jnp.concatenate([gateup, down], axis=0).astype(jnp.float32)

    mlp_total = line_reduce(pick_mlp, images)
    attg_all = exchange(attg)
    back, gain_sums = call(
        attend_back_kernel,
        (attg_all.reshape(everyone, LANES * heads), qkv, raw, turn, *gains),
        (struct((everyone, 512), bf16), struct((8, LANES))),
        [
            pltpu.VMEM((LANES, everyone), bf16),
            pltpu.VMEM((LANES, everyone), bf16),
            pltpu.VMEM((3 * heads, everyone, LANES), jnp.float32),
            pltpu.VMEM((2, 8, LANES), jnp.float32),
        ],
        None,
        "attend_back",
        10 * everyone * everyone * LANES * heads,
    )
    back_all = exchange(back.reshape(blocks, tokens, 512))
    qkv_part, outw_part = call(
        functools.partial(qkv_weights_kernel, images),
        (*grad_pieces, hid, back, att),
        (
            struct((blocks, width // blocks, 512), bf16),
            struct((images, span, width // images), bf16),
        ),
        [pltpu.VMEM((everyone, width), bf16)],
        where,
        "qkv_weights",
    )
    qkv_rows = exchange(qkv_part)
    (joined,) = call(
        functools.partial(join_kernel, images),
        (qkv_rows, outw_part),
        (struct((images, width // blocks, (3 * width + width) // images), bf16),),
        name="join",
    )
    attn_total = line_reduce(
        lambda owner: lax.dynamic_index_in_dim(joined, owner, 0, False).astype(jnp.float32),
        images,
    )
    in_grad, send = pl.pallas_call(
        input_kernel,
        out_shape=(struct((tokens, width)), struct((blocks, 1024))),
        grid=(3,),
        in_specs=[
            whole((blocks, tokens, 512)),
            pl.BlockSpec((width, width), lambda s: (0, s)),
            whole((tokens, width)),
            whole((tokens, width)),
            whole((8, width)),
            whole((8, width)),
            whole((8, LANES)),
            pl.BlockSpec(memory_space=pltpu.SMEM),
        ],
        out_specs=(whole((tokens, width)), whole((blocks, 1024))),
        scratch_shapes=[
            pltpu.VMEM((tokens, width), jnp.float32),
            pltpu.VMEM((1, 6 * width), jnp.float32),
        ],
        name="input",
    )(back_all, qkv_weight, x, middle_grad, mod, sums, gain_sums, bucket)
    everywhere = exchange(
        jnp.broadcast_to(send[None], (images, blocks, 1024)).reshape(images * blocks, 1, 1024),
        ("img", "ty", "tx"),
    ).reshape(images, blocks, 1024)
    mod_cols = jnp.sum(everywhere[:, :, :columns], axis=1)
    buckets = everywhere[:, 0, columns]
    gain_total = jnp.sum(everywhere[:, :, columns + 16 : columns + 16 + 2 * HD], axis=(0, 1))
    share = width // images
    table_part = lax.dynamic_slice(cond_table, (0, share * image), (cond_table.shape[0], share))
    onehot = (
        buckets[:, None] == jnp.arange(cond_table.shape[0], dtype=jnp.float32)[None, :]
    ).astype(jnp.float32)
    condition = jnp.dot(onehot, table_part, precision=PRECISE)
    cond_act = jax.nn.silu(condition).astype(bf16).astype(jnp.float32)
    modw_total = jnp.dot(cond_act.T, mod_cols, precision=PRECISE)
    modb_total = jnp.sum(mod_cols, axis=0)
    weight_part = lax.dynamic_slice(mod_weight, (share * image, 0), (share, columns))
    act_part = jnp.dot(mod_cols, weight_part.astype(jnp.float32).T, precision=PRECISE)
    act_grad = jnp.sum(
        exchange(jnp.broadcast_to(act_part[None], (blocks, images, share))), axis=0
    )
    cond_grad = act_grad * silu_slope(condition)
    lines = cond_table.shape[0] // blocks
    own_hot = lax.dynamic_slice(onehot, (0, lines * mine), (images, lines))
    table_total = jnp.dot(own_hot.T, cond_grad, precision=PRECISE)
    rows = width // blocks
    gateup_total = (
        mlp_total[: 4 * rows].reshape(4, rows, units).transpose(1, 0, 2).reshape(rows, 4 * units)
    )
    down_total = mlp_total[4 * rows :].T
    return (
        output.reshape(block_in.shape),
        in_grad.reshape(block_in.shape),
        table_total,
        modw_total,
        modb_total,
        attn_total[:, : 3 * share],
        gain_total[:HD],
        gain_total[HD:],
        attn_total[:, 3 * share :],
        gateup_total,
        down_total,
    )


def solution(mesh):
    sizes = mesh.shape
    fits = sizes["ty"] == 4 and sizes["tx"] == 2 and sizes["img"] == 4
    return jax.shard_map(
        functools.partial(on_plane, sizes["img"]) if fits else on_device,
        mesh=mesh,
        in_specs=(
            P("img", "ty", "tx", None),
            P("img"),
            P("img", "ty", "tx", None),
            P(),
            P(None, ("ty", "tx")),
            P(("ty", "tx")),
            P(),
            P(),
            P(),
            P(),
            P(),
            P(),
            P("img", "ty", "tx", None),
        ),
        out_specs=(
            P("img", "ty", "tx", None),
            P("img", "ty", "tx", None),
            P(("ty", "tx"), "img"),
            P("img", ("ty", "tx")),
            P(("ty", "tx")),
            P(("ty", "tx"), "img"),
            P(),
            P(),
            P(("ty", "tx"), "img"),
            P(("ty", "tx"), "img"),
            P(("ty", "tx"), "img"),
        ),
        check_vma=False,
    )
```

```python
import functools
import math

import jax
import jax.numpy as jnp
from jax import lax
from jax.experimental import pallas as pl
from jax.experimental.pallas import tpu as pltpu
from jax.sharding import PartitionSpec as P

HEADS = 16
HD = 72


EPS = 1e-06
PRECISE = lax.Precision.HIGHEST


def normed(value):
    return value * lax.rsqrt(jnp.mean(value * value, axis=-1, keepdims=True) + EPS)


def norm_back(value, upstream):
    inverse = lax.rsqrt(jnp.mean(value * value, axis=-1, keepdims=True) + EPS)
    unit_value = value * inverse
    return inverse * (
        upstream - unit_value * jnp.mean(upstream * unit_value, axis=-1, keepdims=True)
    )


def rotate(value, tables, turning):
    row_cos, row_sin, col_cos, col_sin = tables
    quarter = value.shape[-1] // 4
    first = value[..., :quarter]
    second = value[..., quarter : 2 * quarter]
    third = value[..., 2 * quarter : 3 * quarter]
    fourth = value[..., 3 * quarter :]
    row_turn = turning * row_sin
    col_turn = turning * col_sin
    return jnp.concatenate(
        [
            first * row_cos - second * row_turn,
            second * row_cos + first * row_turn,
            third * col_cos - fourth * col_turn,
            fourth * col_cos + third * col_turn,
        ],
        axis=-1,
    )


def silu_slope(value):
    sigma = jax.nn.sigmoid(value)
    return sigma * (1.0 + value * (1.0 - sigma))


def product(left, right):
    return jnp.einsum("ik,kj->ij", left, right, preferred_element_type=jnp.float32)


def product_rt(left, right):
    return jnp.einsum("ik,jk->ij", left, right, preferred_element_type=jnp.float32)


def product_lt(left, right):
    return jnp.einsum("ki,kj->ij", left, right, preferred_element_type=jnp.float32)


def on_device(
    block_in,
    bucket,
    tile_anchor,
    cond_table,
    mod_weight,
    mod_bias,
    qkv_weight,
    query_gain,
    key_gain,
    out_weight,
    gate_up_weight,
    down_weight,
    cotangent,
):
    images, tile_rows, tile_cols, model_width = block_in.shape
    tokens = tile_rows * tile_cols
    all_rows = images * tokens
    head_count = HEADS
    head_size = HD
    score_scale = head_size ** (-0.5)
    hidden_units = down_weight.shape[0]
    onehot = (bucket[:, None] == jnp.arange(cond_table.shape[0], dtype=jnp.int32)[None, :]).astype(
        jnp.float32
    )
    condition = jnp.dot(onehot, cond_table, precision=PRECISE)
    cond_act = jax.nn.silu(condition).astype(jnp.bfloat16)
    mod_part = product(cond_act, mod_weight) + mod_bias[None, :]
    modulation = lax.all_gather(mod_part, ("ty", "tx"), axis=1, tiled=True)
    pieces = [
        modulation[:, None, index * model_width : (index + 1) * model_width] for index in range(6)
    ]
    shift_in, scale_in, gate_in, shift_mid, scale_mid, gate_mid = pieces
    places = jnp.arange(tokens, dtype=jnp.int32)
    row_pos = (tile_anchor[:, 0, 0, 0][:, None] + places[None, :] // tile_cols).astype(jnp.float32)
    col_pos = (tile_anchor[:, 0, 0, 1][:, None] + places[None, :] % tile_cols).astype(jnp.float32)
    quarter = head_size // 4
    frequency = jnp.exp(-math.log(10000.0) * jnp.arange(quarter, dtype=jnp.float32) / quarter)
    row_angle = row_pos[:, :, None, None] * frequency
    col_angle = col_pos[:, :, None, None] * frequency
    tables = (jnp.cos(row_angle), jnp.sin(row_angle), jnp.cos(col_angle), jnp.sin(col_angle))
    inputs = block_in.reshape(images, tokens, model_width)
    normed_in = normed(inputs)
    hidden_in = (
        (normed_in * (1.0 + scale_in) + shift_in)
        .astype(jnp.bfloat16)
        .reshape(all_rows, model_width)
    )
    qkv = product(hidden_in, qkv_weight).reshape(images, tokens, 3 * model_width)
    query_raw = qkv[..., :model_width].reshape(images, tokens, head_count, head_size)
    key_raw = qkv[..., model_width : 2 * model_width].reshape(images, tokens, head_count, head_size)
    query_unit = normed(query_raw)
    key_unit = normed(key_raw)
    query_low = rotate(query_unit * query_gain, tables, 1.0).astype(jnp.bfloat16)
    key_low = rotate(key_unit * key_gain, tables, 1.0).astype(jnp.bfloat16)
    value_low = qkv[..., 2 * model_width :].astype(jnp.bfloat16)
    keys_all, values_all = (
        lax.all_gather(
            key_low.reshape(images, tokens, model_width), ("ty", "tx"), axis=1, tiled=True
        ),
        lax.all_gather(value_low, ("ty", "tx"), axis=1, tiled=True),
    )
    key_heads = keys_all.reshape(images, -1, head_count, head_size)
    value_heads = values_all.reshape(images, -1, head_count, head_size)

    def attend(items):
        query_img, key_img, value_img = items
        scores = (
            jnp.einsum("qhd,khd->hqk", query_img, key_img, preferred_element_type=jnp.float32)
            * score_scale
        )
        row_max = jnp.max(scores, axis=-1, keepdims=True)
        expo = jnp.exp(scores - row_max)
        row_sum = jnp.sum(expo, axis=-1, keepdims=True)
        mixed = jnp.einsum(
            "hqk,khd->qhd",
            (expo / row_sum).astype(jnp.bfloat16),
            value_img,
            preferred_element_type=jnp.float32,
        )
        return (mixed, (row_max + jnp.log(row_sum))[:, :, 0])

    mixed_full, log_total = lax.map(attend, (query_low, key_heads, value_heads))
    attended = mixed_full.reshape(all_rows, model_width).astype(jnp.bfloat16)
    attn_out = product(attended, out_weight).reshape(images, tokens, model_width)
    middle = inputs + gate_in * attn_out
    normed_mid = normed(middle)
    hidden_mid = (
        (normed_mid * (1.0 + scale_mid) + shift_mid)
        .astype(jnp.bfloat16)
        .reshape(all_rows, model_width)
    )

    def feed(hidden_value):
        gate_up = product(hidden_value, gate_up_weight)
        return (gate_up[:, :hidden_units], gate_up[:, hidden_units:])

    gate_pre, up_pre = feed(hidden_mid)
    activ = (jax.nn.silu(gate_pre) * up_pre).astype(jnp.bfloat16)
    mlp_out = product(activ, down_weight).reshape(images, tokens, model_width)
    output = middle + gate_mid * mlp_out
    upstream = cotangent.reshape(images, tokens, model_width)
    gmid_grad = jnp.sum(upstream * mlp_out, axis=1)
    mlp_grad = (gate_mid * upstream).astype(jnp.bfloat16).reshape(all_rows, model_width)
    down_grad = product_lt(activ, mlp_grad)
    activ_grad = product_rt(mlp_grad, down_weight)
    gate_pre, up_pre = feed(hidden_mid)
    gu_grad = jnp.concatenate(
        [activ_grad * up_pre * silu_slope(gate_pre), activ_grad * jax.nn.silu(gate_pre)], axis=1
    ).astype(jnp.bfloat16)
    gateup_grad = product_lt(hidden_mid, gu_grad)
    mid_grad = product_rt(gu_grad, gate_up_weight).reshape(images, tokens, model_width)
    smid_grad = jnp.sum(mid_grad, axis=1)
    cmid_grad = jnp.sum(mid_grad * normed_mid, axis=1)
    middle_grad = upstream + norm_back(middle, mid_grad * (1.0 + scale_mid))
    gin_grad = jnp.sum(middle_grad * attn_out, axis=1)
    attn_grad = (gate_in * middle_grad).astype(jnp.bfloat16).reshape(all_rows, model_width)
    outw_grad = product_lt(attended, attn_grad)
    attended_grad = (
        product_rt(attn_grad, out_weight)
        .astype(jnp.bfloat16)
        .reshape(images, tokens, head_count, head_size)
    )
    row_delta = jnp.swapaxes(jnp.sum(attended_grad.astype(jnp.float32) * mixed_full, axis=-1), 1, 2)

    def score_parts(query_img, key_img, value_img, grad_img, total_img, delta_img):
        scores = (
            jnp.einsum("qhd,khd->hqk", query_img, key_img, preferred_element_type=jnp.float32)
            * score_scale
        )
        probs = jnp.exp(scores - total_img[:, :, None])
        prob_grad = jnp.einsum(
            "qhd,khd->hqk", grad_img, value_img, preferred_element_type=jnp.float32
        )
        score_grad = (probs * (prob_grad - delta_img[:, :, None])).astype(jnp.bfloat16)
        return (probs.astype(jnp.bfloat16), score_grad)

    def grads_all(items):
        query_img, key_img, value_img, grad_img, total_img, delta_img = items
        probs_low, score_grad = score_parts(
            query_img, key_img, value_img, grad_img, total_img, delta_img
        )
        query_part = (
            jnp.einsum("hqk,khd->qhd", score_grad, key_img, preferred_element_type=jnp.float32)
            * score_scale
        )
        key_part = (
            jnp.einsum("hqk,qhd->khd", score_grad, query_img, preferred_element_type=jnp.float32)
            * score_scale
        )
        value_part = jnp.einsum(
            "hqk,qhd->khd", probs_low, grad_img, preferred_element_type=jnp.float32
        )
        return (query_part, key_part.reshape(-1, model_width), value_part.reshape(-1, model_width))

    query_grad, key_full, value_full = lax.map(
        grads_all, (query_low, key_heads, value_heads, attended_grad, log_total, row_delta)
    )
    key_grad, value_grad = (
        lax.psum_scatter(
            key_full.astype(jnp.bfloat16), ("ty", "tx"), scatter_dimension=1, tiled=True
        ).astype(jnp.float32),
        lax.psum_scatter(
            value_full.astype(jnp.bfloat16), ("ty", "tx"), scatter_dimension=1, tiled=True
        ).astype(jnp.float32),
    )
    query_turned = rotate(query_grad, tables, -1.0)
    key_turned = rotate(key_grad.reshape(images, tokens, head_count, head_size), tables, -1.0)
    qgain_part = jnp.sum(query_turned * query_unit, axis=(0, 1, 2))
    kgain_part = jnp.sum(key_turned * key_unit, axis=(0, 1, 2))
    query_back = norm_back(query_raw, query_turned * query_gain).reshape(
        images, tokens, model_width
    )
    key_back = norm_back(key_raw, key_turned * key_gain).reshape(images, tokens, model_width)
    qkv_back = jnp.concatenate([query_back, key_back, value_grad], axis=-1).astype(jnp.bfloat16)
    qkv_back = qkv_back.reshape(all_rows, 3 * model_width)
    qkv_part = product_lt(hidden_in, qkv_back)
    in_back = product_rt(qkv_back, qkv_weight).reshape(images, tokens, model_width)
    sin_grad = jnp.sum(in_back, axis=1)
    cin_grad = jnp.sum(in_back * normed_in, axis=1)
    in_grad = middle_grad + norm_back(inputs, in_back * (1.0 + scale_in))
    mod_grad = jnp.concatenate(
        [sin_grad, cin_grad, gin_grad, smid_grad, cmid_grad, gmid_grad], axis=1
    )
    mod_cols = lax.psum_scatter(mod_grad, ("ty", "tx"), scatter_dimension=1, tiled=True)
    modw_part = jnp.dot(cond_act.astype(jnp.float32).T, mod_cols, precision=PRECISE)
    modb_part = jnp.sum(mod_cols, axis=0)
    act_grad = jnp.dot(mod_cols, mod_weight.astype(jnp.float32).T, precision=PRECISE)
    cond_grad = act_grad * silu_slope(condition)
    table_part = jnp.dot(onehot.T, cond_grad, precision=PRECISE)
    qkv_share, outw_share, gateup_share, down_share, table_share = (
        lax.psum_scatter(
            qkv_part.astype(jnp.bfloat16), ("ty", "tx"), scatter_dimension=0, tiled=True
        ).astype(jnp.float32),
        lax.psum_scatter(
            outw_grad.astype(jnp.bfloat16), ("ty", "tx"), scatter_dimension=0, tiled=True
        ).astype(jnp.float32),
        lax.psum_scatter(
            gateup_grad.astype(jnp.bfloat16), ("ty", "tx"), scatter_dimension=0, tiled=True
        ).astype(jnp.float32),
        lax.psum_scatter(
            down_grad.astype(jnp.bfloat16), ("ty", "tx"), scatter_dimension=0, tiled=True
        ).astype(jnp.float32),
        lax.psum_scatter(
            table_part.astype(jnp.bfloat16), ("ty", "tx"), scatter_dimension=0, tiled=True
        ).astype(jnp.float32),
    )
    qkv_total, outw_total, gateup_total, down_total, table_total = (
        lax.psum_scatter(
            qkv_share.astype(jnp.bfloat16), "img", scatter_dimension=1, tiled=True
        ).astype(jnp.float32),
        lax.psum_scatter(
            outw_share.astype(jnp.bfloat16), "img", scatter_dimension=1, tiled=True
        ).astype(jnp.float32),
        lax.psum_scatter(
            gateup_share.astype(jnp.bfloat16), "img", scatter_dimension=1, tiled=True
        ).astype(jnp.float32),
        lax.psum_scatter(
            down_share.astype(jnp.bfloat16), "img", scatter_dimension=1, tiled=True
        ).astype(jnp.float32),
        lax.psum_scatter(
            table_share.astype(jnp.bfloat16), "img", scatter_dimension=1, tiled=True
        ).astype(jnp.float32),
    )
    modw_total = lax.psum_scatter(
        modw_part.astype(jnp.bfloat16), "img", scatter_dimension=0, tiled=True
    ).astype(jnp.float32)
    modb_total = lax.psum(modb_part, "img")
    qgain_total, kgain_total = lax.psum((qgain_part, kgain_part), ("img", "ty", "tx"))
    return (
        output.reshape(block_in.shape),
        in_grad.reshape(block_in.shape),
        table_total,
        modw_total,
        modb_total,
        qkv_total,
        qgain_total,
        kgain_total,
        outw_total,
        gateup_total,
        down_total,
    )


def sigmoid(value):
    return 1.0 / (1.0 + jnp.exp(-value))


def dot_nn(left, right):
    return lax.dot_general(
        left, right, (((1,), (0,)), ((), ())), preferred_element_type=jnp.float32
    )


def dot_nt(left, right):
    return lax.dot_general(
        left, right, (((1,), (1,)), ((), ())), preferred_element_type=jnp.float32
    )


def dot_tn(left, right):
    return lax.dot_general(
        left, right, (((0,), (0,)), ((), ())), preferred_element_type=jnp.float32
    )


def column_sum(value):
    return jnp.sum(value, axis=0, keepdims=True)


EXTRA = 16
LANES = 128
QUARTER = HD // 4
PLACES = ((0, 0), (QUARTER, LANES // 2), (2 * QUARTER, QUARTER), (3 * QUARTER, LANES // 2 + QUARTER))


def lane_entry(lane):
    low = lane % (LANES // 2)
    upper = lane // (LANES // 2)
    column = low // QUARTER
    entry = jnp.where(
        low < 2 * QUARTER, low % QUARTER + QUARTER * upper + 2 * QUARTER * column, -1
    )
    return entry, column == 1


def wide_row(row, ref, line):
    for source, target in PLACES:
        ref[line : line + 1, target : target + QUARTER] = row[:, source : source + QUARTER]


def open_kernel(
    bucket_ref, anchor_ref, x_ref, table_ref, weight_ref, bias_ref, cot_ref,
    pay_ref, low_ref, wide_ref,
):
    tokens, width = x_ref.shape
    columns = weight_ref.shape[0]
    x = x_ref[...]
    pay_ref[0:tokens, :] = normed(x).astype(jnp.bfloat16)
    low_ref[...] = cot_ref[...].astype(jnp.bfloat16)
    row = table_ref[pl.ds(bucket_ref[0], 1), :]
    act = (row * sigmoid(row)).astype(jnp.bfloat16)
    mod = dot_nt(jnp.broadcast_to(act, (8, width)), weight_ref[...])
    wide_ref[...] = jnp.zeros_like(wide_ref)
    wide_ref[:, 0:columns] = mod + bias_ref[...].reshape(1, columns)
    full = wide_ref[0:1, :]
    high = full.astype(jnp.bfloat16).astype(jnp.float32)
    rest = full - high
    middle = rest.astype(jnp.bfloat16).astype(jnp.float32)
    least = rest - middle
    lane = lax.broadcasted_iota(jnp.int32, (EXTRA, width), 1)
    line = lax.broadcasted_iota(jnp.int32, (EXTRA, width), 0)
    entry, column = lane_entry(lane % LANES)
    anchor = jnp.where(
        column, anchor_ref[1].astype(jnp.float32), anchor_ref[0].astype(jnp.float32)
    )
    anchor = jnp.where(entry >= 0, anchor, 0.0)
    extra = jnp.where(
        line == 0,
        high,
        jnp.where(
            line == 1, middle, jnp.where(line == 2, least, jnp.where(line == 3, anchor, 0.0))
        ),
    )
    pay_ref[tokens : tokens + EXTRA, :] = extra.astype(jnp.bfloat16)


def ready_kernel(
    blocks, tile_cols, scalars, *refs,
):
    qkv_parts, refs = refs[:6], refs[6:]
    (
        gate_a, gate_b, up_a, up_b, qgain_ref, kgain_ref, table_ref, modw_ref,
        spread_ref, order_ref, turn_ref, gain_ref, gate_ref, up_ref, tshare_ref, mshare_ref,
        window_ref, pick_ref,
    ) = refs
    mine = scalars[0]
    share = tshare_ref.shape[1]
    for image in range(table_ref.shape[1] // share):

        @pl.when(scalars[1] == image)
        def _(image=image):
            tshare_ref[...] = table_ref[:, share * image : share * (image + 1)]
            mshare_ref[...] = modw_ref[:, share * image : share * (image + 1)]

    heads = HEADS // blocks
    span = heads * HD
    wide = 3 * heads * LANES
    for index, part in enumerate(qkv_parts):
        window_ref[:, LANES * index : LANES * (index + 1)] = part[...]
    row = lax.broadcasted_iota(jnp.int32, (wide, wide), 0)
    lane = lax.broadcasted_iota(jnp.int32, (wide, wide), 1)
    place = lane % LANES
    part = lane // LANES
    side = part // heads
    entry, _ = lane_entry(place)
    entry = jnp.where(side == 2, jnp.where(place < HD, place, -1), entry)
    local = HD * (part % heads) + entry
    skew = mine * (span - LANES)
    pick = (entry >= 0) & (row == side * (2 * LANES) + skew + local)
    pick_ref[...] = pick.astype(jnp.float32).astype(jnp.bfloat16)
    spread_ref[...] = dot_nn(window_ref[...], pick_ref[...]).astype(jnp.bfloat16)
    columns = order_ref.shape[1]
    row = lax.broadcasted_iota(jnp.int32, (wide, columns), 0)
    lane = lax.broadcasted_iota(jnp.int32, (wide, columns), 1)
    place = row % LANES
    part = row // LANES
    side = part // heads
    entry, _ = lane_entry(place)
    entry = jnp.where(side == 2, jnp.where(place < HD, place, -1), entry)
    pick = (entry >= 0) & (lane == side * span + HD * (part % heads) + entry)
    order_ref[...] = pick.astype(jnp.float32).astype(jnp.bfloat16)
    tokens = turn_ref.shape[1]
    token = lax.broadcasted_iota(jnp.int32, (tokens, LANES), 0)
    entry, column = lane_entry(lax.broadcasted_iota(jnp.int32, (tokens, LANES), 1))
    rate = jnp.exp((entry % QUARTER).astype(jnp.float32) * (-math.log(10000.0) / QUARTER))
    rate = jnp.where(entry >= 0, rate, 0.0)
    offset = jnp.where(column, token % tile_cols, token // tile_cols).astype(jnp.float32) * rate
    turn_ref[0] = jnp.cos(offset)
    turn_ref[1] = jnp.sin(offset)
    turn_ref[2] = rate
    gain_ref[...] = jnp.zeros_like(gain_ref)
    wide_row(qgain_ref[...].reshape(1, HD), gain_ref, 0)
    wide_row(kgain_ref[...].reshape(1, HD), gain_ref, 1)
    units = gate_ref.shape[1]
    run = units // 2
    for parity in range(2):

        @pl.when(mine % 2 == parity)
        def _(parity=parity):
            for source_a, source_b, target in ((gate_a, gate_b, gate_ref), (up_a, up_b, up_ref)):
                target[:, 0:run] = source_a[:, run * parity : run * (parity + 1)]
                target[:, run:units] = source_b[:, run * parity : run * (parity + 1)]


def unit_rate(raw):
    return lax.rsqrt(jnp.sum(raw * raw, axis=-1, keepdims=True) * (1.0 / HD) + EPS)


def block_copies(pieces, ref, place, tokens, sems):
    if len(pieces) == 8:
        plan = [(piece, index, tokens, 0) for index, piece in enumerate(pieces)]
    else:
        own, xn, core, cx, yn, d1, d2, cy, cd1, cd2 = pieces
        half = d1.shape[0]
        plan = [
            (own, 0, tokens, 0), (xn, 1, tokens, 0), (core, 2, tokens, 0), (cx, 3, tokens, 0),
            (yn, 4, tokens, 0), (d1, 5, half, 0), (d2, 5, tokens - half, half), (cy, 6, tokens, 0),
            (cd1, 7, half, 0), (cd2, 7, tokens - half, half),
        ]
    return [
        pltpu.make_async_copy(
            piece.at[pl.ds(0, rows), :],
            ref.at[pl.ds(place(index) + offset, rows), :],
            sems.at[number],
        )
        for number, (piece, index, rows, offset) in enumerate(plan)
    ]


def attend_kernel(blocks, scalars, *refs):
    pieces, refs = refs[:10], refs[10:]
    (
        spread_ref, offset_ref, gain_ref,
        att_ref, hid_ref, qkv_ref, raw_ref, turn_ref, mod_ref, log_ref, mixed_ref,
        all_ref, extra_ref, rows_ref, flat_ref, anchor_ref, vt_ref, sems, extra_sems,
    ) = refs
    mine = scalars[0]
    own, xn, core, cx, yn, d1, d2, cy, cd1, cd2 = pieces
    width = own.shape[1]
    tokens = own.shape[0] - EXTRA
    columns = 6 * width // blocks
    half = d1.shape[0]
    everyone = blocks * tokens
    heads = HEADS // blocks
    extras = [
        pltpu.make_async_copy(
            piece.at[pl.ds(piece.shape[0] - EXTRA, EXTRA), :],
            extra_ref.at[index],
            extra_sems.at[index],
        )
        for index, piece in enumerate((own, xn, core, cx, yn, d2, cy, cd2))
    ]
    copies = block_copies(
        pieces,
        all_ref,
        lambda index: pl.multiple_of((mine ^ index) * tokens, tokens),
        tokens,
        sems,
    )
    for copy in (*extras, *copies):
        copy.start()
    for copy in extras:
        copy.wait()
    for index in range(blocks):
        extra = extra_ref[index].astype(jnp.float32)
        place = mine ^ index
        rows_ref[pl.ds(place, 1), :] = extra[0:1] + extra[1:2] + extra[2:3]
        anchor_ref[0, pl.ds(place, 1), :] = extra[3:4, 0:LANES]
    for index in range(blocks):
        flat_ref[0:1, columns * index : columns * (index + 1)] = rows_ref[
            index : index + 1, 0:columns
        ]
    mod_ref[...] = jnp.zeros_like(mod_ref)
    for index in range(6):
        mod_ref[index : index + 1, :] = flat_ref[0:1, width * index : width * (index + 1)]
    shift_in = mod_ref[0:1, :]
    scale_in = 1.0 + mod_ref[1:2, :]
    anchor = anchor_ref[0] * offset_ref[2, 0:blocks, :]
    anchor_ref[0] = jnp.cos(anchor)
    anchor_ref[1] = jnp.sin(anchor)
    lane = lax.broadcasted_iota(jnp.int32, (tokens, LANES), 1)
    sign = jnp.where(lane < LANES // 2, -1.0, 1.0)
    offset_cos, offset_sin = offset_ref[0], offset_ref[1]
    query_gain, key_gain = gain_ref[0:1, :], gain_ref[1:2, :]
    scale = HD ** (-0.5) * math.log2(math.e)
    for copy in copies:
        copy.wait()

    def project(index, carry):
        rows = pl.ds(pl.multiple_of(index * tokens, tokens), tokens)
        hidden = (all_ref[rows, :].astype(jnp.float32) * scale_in + shift_in).astype(jnp.bfloat16)
        hid_ref[rows, :] = hidden
        anchor_cos = anchor_ref[0, pl.ds(index, 1), :]
        anchor_sin = anchor_ref[1, pl.ds(index, 1), :]
        turn_cos = anchor_cos * offset_cos - anchor_sin * offset_sin
        turn_sin = (anchor_sin * offset_cos + anchor_cos * offset_sin) * sign
        turn_ref[0, rows, :] = turn_cos
        turn_ref[1, rows, :] = turn_sin
        product = dot_nn(hidden, spread_ref[...])
        for part in range(2 * heads):
            raw = product[:, LANES * part : LANES * (part + 1)]
            raw_ref[part, rows, :] = raw
            gain = query_gain * scale if part < heads else key_gain
            unit = raw * unit_rate(raw) * gain
            turned = unit * turn_cos + pltpu.roll(unit, LANES // 2, 1) * turn_sin
            qkv_ref[part, rows, :] = turned.astype(jnp.bfloat16)
        for part in range(2 * heads, 3 * heads):
            qkv_ref[part, rows, :] = product[:, LANES * part : LANES * (part + 1)].astype(
                jnp.bfloat16
            )
        return carry

    lax.fori_loop(0, blocks, project, 0, unroll=2)
    chunk = 2 * tokens
    for head in range(heads):
        vt_ref[head] = qkv_ref[2 * heads + head].T

    def attend(index, carry):
        rows = pl.ds(pl.multiple_of(index * chunk, chunk), chunk)
        for head in range(heads):
            scores = dot_nt(qkv_ref[heads + head], qkv_ref[head, rows, :])
            expo = jnp.exp2(scores)
            total = column_sum(expo)
            mixed = dot_nn(vt_ref[head], expo.astype(jnp.bfloat16)) * (1.0 / total)
            mixed = mixed.T
            log_ref[head, pl.ds(index, 1), :] = jnp.log2(total)
            mixed_ref[head, rows, :] = mixed
            att_ref[rows, LANES * head : LANES * (head + 1)] = mixed.astype(jnp.bfloat16)
        return carry

    lax.fori_loop(0, everyone // chunk, attend, 0)


def middle_kernel(att_ref, weight_ref, x_ref, mod_ref, out_ref, mid_ref, hid_ref):
    blocks = att_ref.shape[0]
    heads = HEADS // blocks
    attended = jnp.concatenate(
        [
            att_ref[index, :, LANES * head : LANES * head + HD]
            for index in range(blocks)
            for head in range(heads)
        ],
        axis=1,
    )
    attn_out = dot_nn(attended, weight_ref[...])
    out_ref[...] = attn_out
    middle = x_ref[...] + mod_ref[2:3, :] * attn_out
    mid_ref[...] = middle
    hid_ref[...] = (normed(middle) * (1.0 + mod_ref[4:5, :]) + mod_ref[3:4, :]).astype(
        jnp.bfloat16
    )


def act_grad_kernel(down_ref, cot_ref, mod_ref, out_ref, low_ref):
    @pl.when(pl.program_id(0) == 0)
    def _():
        low_ref[...] = (mod_ref[5:6, :] * cot_ref[...]).astype(jnp.bfloat16)

    out_ref[...] = dot_nt(low_ref[...], down_ref[...])


def mlp_kernel(
    gate_ref, up_ref, outw_ref, hid_ref, mid_ref, attn_ref, cot_ref, agrad_in, mod_ref,
    act_ref, mgrad_ref, agrad_ref, dgrad_ref, sums_ref, back_ref,
):
    step = pl.program_id(0)
    blocks = dgrad_ref.shape[0]
    heads = HEADS // blocks

    hidden = hid_ref[...]
    gate = dot_nn(hidden, gate_ref[...])
    up = dot_nn(hidden, up_ref[...])
    sigma = sigmoid(gate)
    silu = gate * sigma
    act_ref[...] = (silu * up).astype(jnp.bfloat16)
    act_grad = agrad_in[...]
    slope = sigma * (1.0 + gate * (1.0 - sigma))
    gate_grad = (act_grad * up * slope).astype(jnp.bfloat16)
    up_grad = (act_grad * silu).astype(jnp.bfloat16)
    part = dot_nt(gate_grad, gate_ref[...]) + dot_nt(up_grad, up_ref[...])

    @pl.when(step == 0)
    def _():
        back_ref[...] = part

    @pl.when(step > 0)
    def _():
        back_ref[...] += part

    @pl.when(step == pl.num_programs(0) - 1)
    def _():
        middle = mid_ref[...]
        upstream = cot_ref[...]
        back = back_ref[...]
        inverse = lax.rsqrt(jnp.mean(middle * middle, axis=-1, keepdims=True) + EPS)
        unit = middle * inverse
        lifted = back * (1.0 + mod_ref[4:5, :])
        middle_grad = upstream + inverse * (
            lifted - unit * jnp.mean(lifted * unit, axis=-1, keepdims=True)
        )
        mgrad_ref[...] = middle_grad
        attn_grad = (mod_ref[2:3, :] * middle_grad).astype(jnp.bfloat16)
        agrad_ref[...] = attn_grad
        dgrad_ref[...] = jnp.zeros_like(dgrad_ref)
        for index in range(blocks):
            rows = outw_ref[HD * heads * index : HD * heads * (index + 1), :]
            piece = dot_nt(attn_grad, rows).astype(jnp.bfloat16)
            for head in range(heads):
                dgrad_ref[index, :, LANES * head : LANES * head + HD] = piece[
                    :, HD * head : HD * (head + 1)
                ]
        sums_ref[...] = jnp.zeros_like(sums_ref)
        sums_ref[2:3, :] = column_sum(middle_grad * attn_ref[...])
        sums_ref[3:4, :] = column_sum(back)
        sums_ref[4:5, :] = column_sum(back * unit)


def mlp_out_kernel(act_ref, down_ref, mid_ref, cot_ref, mod_ref, output_ref, sum_ref, acc_ref):
    step = pl.program_id(0)
    part = dot_nn(act_ref[...], down_ref[...])

    @pl.when(step == 0)
    def _():
        acc_ref[...] = part

    @pl.when(step > 0)
    def _():
        acc_ref[...] += part

    @pl.when(step == pl.num_programs(0) - 1)
    def _():
        output_ref[...] = mid_ref[...] + mod_ref[5:6, :] * acc_ref[...]
        sum_ref[...] = jnp.broadcast_to(column_sum(cot_ref[...] * acc_ref[...]), sum_ref.shape)


def mlp_weights_kernel(scalars, *refs):
    hid_pieces, cot_pieces, refs = refs[:8], refs[8:16], refs[16:]
    (
        gate_ref, up_ref, down_a, down_b, mod_ref, own_ref, next_ref, two_ref, last_ref, far_ref,
        all_ref, low_ref, act_ref, down_ref, out_ref, sems, out_sems,
    ) = refs
    tokens, width = hid_pieces[0].shape
    everyone = all_ref.shape[0]
    run = down_a.shape[0]
    units = 2 * run
    copies = [
        *block_copies(hid_pieces, all_ref, lambda index: index * tokens, tokens, sems.at[0]),
        *block_copies(cot_pieces, low_ref, lambda index: index * tokens, tokens, sems.at[1]),
    ]
    for copy in copies:
        copy.start()
    down_ref[0:run, :] = down_a[...]
    down_ref[run:units, :] = down_b[...]
    gate_mid = mod_ref[5:6, :]
    for copy in copies:
        copy.wait()
    chunk = everyone // 4

    def chunked(index, carry):
        span = pl.ds(pl.multiple_of(index * chunk, chunk), chunk)
        low = (low_ref[span, :].astype(jnp.float32) * gate_mid).astype(jnp.bfloat16)
        low_ref[span, :] = low
        hidden = all_ref[span, :]
        gate = dot_nn(hidden, gate_ref[...])
        up = dot_nn(hidden, up_ref[...])
        act_grad = dot_nt(low, down_ref[...])
        sigma = sigmoid(gate)
        silu = gate * sigma
        slope = sigma * (1.0 + gate * (1.0 - sigma))
        act_ref[0, span, :] = (silu * up).astype(jnp.bfloat16)
        act_ref[1, span, :] = (act_grad * up * slope).astype(jnp.bfloat16)
        act_ref[2, span, :] = (act_grad * silu).astype(jnp.bfloat16)
        return carry

    lax.fori_loop(0, everyone // chunk, chunked, 0, unroll=2)
    lanes = width // units
    for side in range(2):
        grad = dot_tn(act_ref[1 + side], all_ref[...]).astype(jnp.bfloat16)
        for part in range(2):
            for index in range(lanes):
                out_ref[2 * side + part, run * index : run * (index + 1), :] = grad[
                    run * part : run * (part + 1), units * index : units * (index + 1)
                ]
    down = dot_tn(act_ref[0], low_ref[...]).astype(jnp.bfloat16).T
    share = width // out_ref.shape[0]
    for image in range(out_ref.shape[0]):
        out_ref[image, run * lanes : run * lanes + share, :] = down[
            share * image : share * (image + 1), :
        ]
    deal(out_ref, scalars[1], (own_ref, next_ref, two_ref, last_ref, far_ref), out_sems)


def deal(ref, place, targets, sems):
    owners = [place, (place + 1) % 4, (place + 2) % 4, (place + 3) % 4, 3 - place]
    copies = [
        pltpu.make_async_copy(ref.at[owner], target, sems.at[index])
        for index, (owner, target) in enumerate(zip(owners, targets, strict=False))
    ]
    for copy in copies:
        copy.start()
    for copy in copies:
        copy.wait()


def summed(refs, rows):
    total = refs[0][rows, :].astype(jnp.float32)
    for ref in refs[1:]:
        total = total + ref[rows, :].astype(jnp.float32)
    return total


def turn_kernel(scalars, *refs):
    parts, refs = refs[:3], refs[3:]
    send_ref, first_ref, second_ref = refs
    blocks, rows, run = send_ref.shape
    units = parts[0].shape[1]
    lanes = rows * blocks // units
    whole = jnp.concatenate(
        [summed(parts, pl.ds(run * index, run)).T for index in range(lanes)], axis=0
    )
    send_ref[...] = whole.astype(jnp.bfloat16).reshape(send_ref.shape)
    down = summed(parts, pl.ds(run * lanes, first_ref.shape[0])).astype(jnp.bfloat16)
    even = scalars[0] % 2 == 0
    for parity in range(2):

        @pl.when(scalars[0] % 2 == parity)
        def _(parity=parity):
            first_ref[...] = down[:, run * parity : run * (parity + 1)]
            second_ref[...] = down[:, run * (1 - parity) : run * (2 - parity)]


def lay_kernel(scalars, got_ref, first_ref, second_ref, out_ref, down_ref):
    out_ref[...] = jnp.concatenate(
        [got_ref[index].astype(jnp.float32) for index in range(got_ref.shape[0])], axis=1
    )
    run = first_ref.shape[1]
    first = first_ref[...].astype(jnp.float32)
    second = second_ref[...].astype(jnp.float32)
    half = got_ref.shape[0] // 2

    @pl.when(scalars[0] < half)
    def _():
        down_ref[...] = jnp.concatenate([first, second], axis=1)

    @pl.when(scalars[0] >= half)
    def _():
        down_ref[...] = jnp.concatenate([second, first], axis=1)


def finish_kernel(*refs):
    parts, (qkv_ref, out_ref) = refs[:3], refs[3:]
    total = summed(parts, pl.ds(0, qkv_ref.shape[0]))
    columns = qkv_ref.shape[1]
    qkv_ref[...] = total[:, 0:columns]
    out_ref[...] = total[:, columns:]


def dot_exact(left, right, dims):
    total = None
    for _ in range(3):
        part = left.astype(jnp.bfloat16)
        left = left - part.astype(jnp.float32)
        product = lax.dot_general(
            part, right, (dims, ((), ())), preferred_element_type=jnp.float32
        )
        total = product if total is None else total + product
    return total


def tail_kernel(
    got_ref, table_ref, weight_ref,
    modw_ref, modb_ref, qgain_ref, kgain_ref, send_ref, cond_ref, bucket_ref,
    cols_ref, act_ref,
):
    columns = modb_ref.shape[0]
    blocks = send_ref.shape[0]
    images = got_ref.shape[0] // blocks
    lines = table_ref.shape[0]
    cols_ref[...] = jnp.zeros_like(cols_ref)
    act_ref[...] = jnp.zeros_like(act_ref)
    bucket_ref[...] = jnp.full(bucket_ref.shape, -1.0, jnp.float32)
    cond_ref[...] = jnp.zeros_like(cond_ref)
    gains = None
    line = lax.broadcasted_iota(jnp.int32, (lines, 1), 0).astype(jnp.float32)
    for image in range(images):
        total = got_ref[blocks * image]
        for index in range(1, blocks):
            total = total + got_ref[blocks * image + index]
        row = jnp.concatenate([total[index : index + 1, :] for index in range(8)], axis=1)
        cols_ref[image : image + 1, :] = row[:, 0:columns]
        gains = row if gains is None else gains + row
        first = got_ref[blocks * image]
        place = columns // LANES
        bucket = first[place : place + 1, columns % LANES : columns % LANES + 1]
        bucket_ref[image : image + 1, :] = jnp.broadcast_to(bucket, (1, LANES))
        cond = jnp.sum(
            jnp.where(line == bucket, table_ref[...], 0.0), axis=0, keepdims=True
        )
        cond_ref[image : image + 1, :] = cond
        act_ref[image : image + 1, :] = (
            (cond * sigmoid(cond)).astype(jnp.bfloat16).astype(jnp.float32)
        )
    cols = cols_ref[...]
    modw_ref[...] = lax.dot_general(
        act_ref[...], cols, (((0,), (0,)), ((), ())),
        precision=PRECISE, preferred_element_type=jnp.float32,
    )
    modb_ref[...] = column_sum(cols).reshape(columns)
    start = columns + 16
    qgain_ref[...] = gains[:, start : start + HD].reshape(HD)
    kgain_ref[...] = gains[:, start + HD : start + 2 * HD].reshape(HD)
    part = dot_exact(cols, weight_ref[...], ((1,), (0,)))
    send_ref[...] = jnp.broadcast_to(part[None], send_ref.shape)


def table_kernel(scalars, got_ref, cond_ref, bucket_ref, out_ref):
    total = jnp.sum(got_ref[...], axis=0)
    cond = cond_ref[...]
    sigma = sigmoid(cond)
    grad = total * (sigma * (1.0 + cond * (1.0 - sigma)))
    lines = out_ref.shape[0]
    line = lax.broadcasted_iota(jnp.int32, (lines, 1), 0) + scalars[0] * lines
    out = jnp.zeros(out_ref.shape, jnp.float32)
    for image in range(4):
        hot = line.astype(jnp.float32) == bucket_ref[image : image + 1, 0:1]
        out = out + jnp.where(hot, grad[image : image + 1, :], 0.0)
    out_ref[...] = out


def attend_back_kernel(
    attg_ref, qkv_ref, raw_ref, turn_ref, log_ref, mixed_ref, gain_ref, order_ref,
    back_ref, gsum_ref, kt_ref, grad_ref,
):
    heads = attg_ref.shape[1] // LANES
    everyone = attg_ref.shape[0]
    lines, chunk = log_ref.shape[1:]
    scale = HD ** (-0.5)
    query_gain, key_gain = gain_ref[0:1, :], gain_ref[1:2, :]
    for head in range(heads):
        kt_ref[head] = qkv_ref[heads + head].T
    ones = jnp.ones((8, LANES), jnp.bfloat16)

    def attend(index, first):
        rows = pl.ds(pl.multiple_of(index * chunk, chunk), chunk)
        for head in range(heads):
            query = qkv_ref[head, rows, :]
            upstream = attg_ref[rows, LANES * head : LANES * (head + 1)]
            weighted = upstream.astype(jnp.float32) * mixed_ref[head, rows, :]
            high = weighted.astype(jnp.bfloat16)
            low = (weighted - high.astype(jnp.float32)).astype(jnp.bfloat16)
            delta = (dot_nt(ones, high) + dot_nt(ones, low))[0:1, :]
            probs = jnp.exp2(
                dot_nt(qkv_ref[heads + head], query) - log_ref[head, pl.ds(index, 1), :]
            )
            score_grad = (probs * (dot_nt(qkv_ref[2 * heads + head], upstream) - delta)).astype(
                jnp.bfloat16
            )
            value_part = dot_nn(probs.astype(jnp.bfloat16), upstream)
            key_part = dot_nn(score_grad, query)
            if first:
                grad_ref[2 * heads + head] = value_part
                grad_ref[heads + head] = key_part
            else:
                grad_ref[2 * heads + head] += value_part
                grad_ref[heads + head] += key_part
            grad_ref[head, rows, :] = dot_nn(kt_ref[head], score_grad).T

    attend(0, True)

    def later(index, carry):
        attend(index, False)
        return carry

    lax.fori_loop(1, lines, later, 0)
    gsum_ref[...] = jnp.zeros_like(gsum_ref)
    step = 2 * LANES

    def finish(index, carry):
        rows = pl.ds(pl.multiple_of(index * step, step), step)
        turn_cos = turn_ref[0, rows, :]
        turn_sin = turn_ref[1, rows, :]
        parts = []
        for part in range(2 * heads):
            gain = query_gain if part < heads else key_gain
            grad = grad_ref[part, rows, :] * (scale if part < heads else math.log(2.0))
            turned = grad * turn_cos - pltpu.roll(grad, LANES // 2, 1) * turn_sin
            raw = raw_ref[part, rows, :]
            rate = unit_rate(raw)
            unit = raw * rate
            line = 0 if part < heads else 1
            product = turned * unit
            gsum_ref[line : line + 1, :] += column_sum(product)
            lifted = turned * gain
            mean = jnp.sum(product * gain, axis=-1, keepdims=True) * (1.0 / HD)
            parts.append((rate * (lifted - unit * mean)).astype(jnp.bfloat16))
        for part in range(2 * heads, 3 * heads):
            parts.append(grad_ref[part, rows, :].astype(jnp.bfloat16))
        back_ref[rows, :] = dot_nn(jnp.concatenate(parts, axis=1), order_ref[...]).astype(
            jnp.bfloat16
        )
        return carry

    lax.fori_loop(0, everyone // step, finish, 0)


def qkv_weights_kernel(hid_ref, back_ref, grad_ref):
    grad = dot_tn(hid_ref[...], back_ref[...]).astype(jnp.bfloat16)
    grad_ref[...] = grad.reshape(grad_ref.shape)


def out_weights_kernel(images, scalars, *refs):
    pieces, refs = refs[:8], refs[8:]
    att_ref, ograd_ref, low_ref, sems = refs
    tokens, width = pieces[0].shape
    mine = scalars[0]
    heads = att_ref.shape[1] // LANES
    copies = block_copies(
        pieces,
        low_ref,
        lambda index: pl.multiple_of((mine ^ index) * tokens, tokens),
        tokens,
        sems,
    )
    for copy in copies:
        copy.start()
    for copy in copies:
        copy.wait()
    outw = dot_tn(att_ref[...], low_ref[...]).astype(jnp.bfloat16)
    share = width // images
    for image in range(images):
        for head in range(heads):
            ograd_ref[image, HD * head : HD * (head + 1), :] = outw[
                LANES * head : LANES * head + HD, share * image : share * (image + 1)
            ]


def join_kernel(scalars, grad_ref, ograd_ref, *refs):
    targets, (out_ref, sems) = refs[:5], refs[5:]
    images = out_ref.shape[0]
    blocks = grad_ref.shape[0]
    span = HD * HEADS // blocks
    whole = jnp.concatenate(
        [
            grad_ref[index][:, span * side : span * (side + 1)]
            for side in range(3)
            for index in range(blocks)
        ],
        axis=1,
    )
    share = whole.shape[1] // images
    for image in range(images):
        out_ref[image] = jnp.concatenate(
            [whole[:, share * image : share * (image + 1)], ograd_ref[image]], axis=1
        )
    deal(out_ref, scalars[1], targets, sems)


def input_kernel(
    back_ref, weight_ref, x_ref, mgrad_ref, mod_ref, sums_ref, gmid_ref, gsum_ref, bucket_ref,
    grad_ref, send_ref, acc_ref, flat_ref, row_ref,
):
    step = pl.program_id(0)
    blocks = back_ref.shape[0]
    span = HD * HEADS // blocks
    width = x_ref.shape[1]
    columns = 6 * width // blocks

    for side in range(3):

        @pl.when(step == side)
        def _(side=side):
            natural = jnp.concatenate(
                [back_ref[index, :, span * side : span * (side + 1)] for index in range(blocks)],
                axis=1,
            )
            part = dot_nt(natural, weight_ref[...])
            acc_ref[...] = part if side == 0 else acc_ref[...] + part

    @pl.when(step == 2)
    def _():
        x = x_ref[...]
        back = acc_ref[...]
        inverse = lax.rsqrt(jnp.mean(x * x, axis=-1, keepdims=True) + EPS)
        unit = x * inverse
        lifted = back * (1.0 + mod_ref[1:2, :])
        grad_ref[...] = mgrad_ref[...] + inverse * (
            lifted - unit * jnp.mean(lifted * unit, axis=-1, keepdims=True)
        )
        flat_ref[0:1, 0:width] = column_sum(back)
        flat_ref[0:1, width : 2 * width] = column_sum(back * unit)
        for index in range(2, 5):
            flat_ref[0:1, width * index : width * (index + 1)] = sums_ref[index : index + 1, :]
        flat_ref[0:1, width * 5 : width * 6] = gmid_ref[0:1, :]
        row_ref[...] = jnp.zeros_like(row_ref)
        for index in range(blocks):
            row_ref[index : index + 1, 0:columns] = flat_ref[
                0:1, columns * index : columns * (index + 1)
            ]
        row_ref[:, columns : columns + 1] = jnp.broadcast_to(
            bucket_ref[0].astype(jnp.float32), (blocks, 1)
        )
        for line in range(2):
            for source, target in PLACES:
                start = columns + 16 + HD * line + source
                row_ref[:, start : start + QUARTER] = jnp.broadcast_to(
                    gsum_ref[line : line + 1, target : target + QUARTER], (blocks, QUARTER)
                )
        for index in range(blocks):
            tile = jnp.concatenate(
                [
                    row_ref[index : index + 1, LANES * part : LANES * (part + 1)]
                    for part in range(8)
                ],
                axis=0,
            )
            for image in range(send_ref.shape[0] // blocks):
                send_ref[blocks * image + index] = tile


def whole_spec(shape):
    return pl.BlockSpec(tuple(shape), lambda *_, n=len(shape): (0,) * n)


ANY = pl.BlockSpec(memory_space=pl.ANY)
SMEM = pl.BlockSpec(memory_space=pltpu.SMEM)


def call(
    kernel, operands, outs, scratch=(), scalars=None, name=None, micros=5, specs=None, grid=(1,),
    out_specs=None,
):
    return pl.pallas_call(
        kernel,
        out_shape=outs,
        grid_spec=pltpu.PrefetchScalarGridSpec(
            num_scalar_prefetch=0 if scalars is None else 1,
            grid=grid,
            in_specs=[
                (specs or {}).get(index) or whole_spec(a.shape) for index, a in enumerate(operands)
            ],
            out_specs=[
                (out_specs or {}).get(index) or whole_spec(o.shape) for index, o in enumerate(outs)
            ],
            scratch_shapes=list(scratch),
        ),
        cost_estimate=pl.CostEstimate(
            flops=int(micros * 1e9), transcendentals=0, bytes_accessed=int(micros * 1e6)
        ),
        name=name,
    )(*(() if scalars is None else (scalars,)), *operands)


def struct(shape, dtype=jnp.float32):
    return jax.ShapeDtypeStruct(shape, dtype)


PLANE = ("ty", "tx")


def swap(value, bit):
    return lax.ppermute(value, PLANE, [(index, index ^ bit) for index in range(8)])


def first_round(value):
    return swap(value, 2), swap(value, 1), swap(value, 4)


def split_round(xn, yn, half):
    d1 = swap(xn[:half], 4)
    cx = swap(xn, 2)
    d2 = swap(yn[half:], 1)
    return d1, d2, cx, swap(yn, 2)


def second_round(xn, yn):
    return swap(xn, 4), swap(xn, 2), swap(yn, 2)


def tie(*values):
    return lax.optimization_barrier(values)


def exchange(value, axes=PLANE):
    return lax.all_to_all(value, axes, split_axis=0, concat_axis=0, tiled=True)


def shift(value, pairs):
    return lax.ppermute(value, "img", pairs)


def onward(value, step):
    return shift(value, [(i, (i + step) % 4) for i in range(4)])


def add(left, right):
    return (left.astype(jnp.float32) + right.astype(jnp.float32)).astype(jnp.bfloat16)


def line_first(shares):
    return shift(shares[4], [(0, 1), (3, 2)])


def line_second(shares, first):
    value = add(shares[2], first)
    return shift(value, [(0, 1), (1, 2)]), shift(value, [(3, 2), (2, 1)])


def line_third(shares, up, down):
    return (
        shift(add(shares[1], up), [(0, 1), (1, 2), (2, 3)]),
        shift(add(shares[3], down), [(3, 2), (2, 1), (1, 0)]),
    )


def on_plane(
    images,
    block_in,
    bucket,
    tile_anchor,
    cond_table,
    mod_weight,
    mod_bias,
    qkv_weight,
    query_gain,
    key_gain,
    out_weight,
    gate_up_weight,
    down_weight,
    cotangent,
):
    blocks = 8
    _, tile_rows, tile_cols, width = block_in.shape
    tokens = tile_rows * tile_cols
    everyone = blocks * tokens
    hidden_units = down_weight.shape[0]
    units = hidden_units // blocks
    run = units // 2
    lanes = width // units
    heads = HEADS // blocks
    span = heads * HD
    columns = mod_weight.shape[1]
    wide = 3 * heads * LANES
    packed = -(-3 * span // LANES) * LANES
    bf16 = jnp.bfloat16
    image = lax.axis_index("img")
    mine = lax.axis_index("ty") * 2 + lax.axis_index("tx")
    where = jnp.stack([mine, image]).astype(jnp.int32)
    share = width // images
    x = block_in.reshape(tokens, width)
    cot = cotangent.reshape(tokens, width)
    half = tokens // 2
    pay, low_cot = call(
        open_kernel,
        (bucket, tile_anchor.reshape(2), x, cond_table, mod_weight.T, mod_bias, cot),
        (struct((tokens + EXTRA, width), bf16), struct((tokens, width), bf16)),
        [pltpu.VMEM((8, width), jnp.float32)],
        name="open",
        specs={0: SMEM, 1: SMEM},
    )
    core, xn, yn = first_round(pay)
    spread, order, offsets, gains, own_gate, own_up, table_share, modw_share = call(
        functools.partial(ready_kernel, blocks, tile_cols),
        (*[qkv_weight] * 6, *[gate_up_weight] * 4, query_gain, key_gain, cond_table, mod_weight.T),
        (
            struct((width, wide), bf16),
            struct((wide, packed), bf16),
            struct((3, tokens, LANES)),
            struct((8, LANES)),
            struct((width, units), bf16),
            struct((width, units), bf16),
            struct((cond_table.shape[0], share)),
            struct((columns, share), bf16),
        ),
        [pltpu.VMEM((width, wide), bf16), pltpu.VMEM((wide, wide), bf16)],
        where,
        "ready",
        specs={
            **{
                2 * side + n: pl.BlockSpec(
                    (width, LANES), lambda i, s, c=side * width // LANES + n: (0, c + s[0])
                )
                for side in range(3)
                for n in range(2)
            },
            **{
                6 + n: pl.BlockSpec((width, units), lambda i, s, n=n: (0, n * 4 + s[0] // 2))
                for n in range(4)
            },
        },
    )
    xn, yn, spread, order, offsets, gains, own_gate, own_up = tie(
        xn, yn, spread, order, offsets, gains, own_gate, own_up
    )
    d1, d2, cx, cy = split_round(xn, yn, half)
    pieces = (pay, xn, core, cx, yn, d1, d2, cy, swap(d1, 2), swap(d2, 2))
    c_core, c_xn, c_yn = first_round(low_cot)
    att, hid, qkv, raw, turn, mod, logs, mixed = call(
        functools.partial(attend_kernel, blocks),
        (*pieces, spread, offsets, gains),
        (
            struct((everyone, LANES * heads), bf16),
            struct((everyone, width), bf16),
            struct((3 * heads, everyone, LANES), bf16),
            struct((2 * heads, everyone, LANES)),
            struct((2, everyone, LANES)),
            struct((8, width)),
            struct((heads, everyone // (2 * tokens), 2 * tokens)),
            struct((heads, everyone, LANES)),
        ),
        [
            pltpu.VMEM((everyone, width), bf16),
            pltpu.VMEM((blocks, EXTRA, width), bf16),
            pltpu.VMEM((8, width), jnp.float32),
            pltpu.VMEM((1, 6 * width), jnp.float32),
            pltpu.VMEM((2, 8, LANES), jnp.float32),
            pltpu.VMEM((heads, LANES, everyone), bf16),
            pltpu.SemaphoreType.DMA((10,)),
            pltpu.SemaphoreType.DMA((blocks,)),
        ],
        where,
        "attend",
        15,
        {index: ANY for index in range(10)},
    )
    att, c_core, c_xn, c_yn = tie(att, c_core, c_xn, c_yn)
    att_all = exchange(att.reshape(blocks, tokens, LANES * heads))
    c_dn, c_cx, c_cy = second_round(c_xn, c_yn)
    mlp_steps = 4
    step_units = hidden_units // mlp_steps
    (act_grad,) = call(
        act_grad_kernel,
        (down_weight, cot, mod),
        (struct((tokens, hidden_units)),),
        [pltpu.VMEM((tokens, width), bf16)],
        name="act_grad",
        specs={0: pl.BlockSpec((step_units, width), lambda f: (f, 0))},
        out_specs={0: pl.BlockSpec((tokens, step_units), lambda f: (0, f))},
        grid=(mlp_steps,),
    )
    att_all, c_dn, c_cx, c_cy, act_grad = tie(att_all, c_dn, c_cx, c_cy, act_grad)
    cot_pieces = (low_cot, c_xn, c_core, c_cx, c_yn, c_dn, c_cy, swap(c_dn, 2))
    attn_out, middle, hidden_mid = call(
        middle_kernel,
        (att_all, out_weight, x, mod),
        (struct((tokens, width)), struct((tokens, width)), struct((tokens, width), bf16)),
        name="middle",
    )
    h_core, h_xn, h_yn = first_round(hidden_mid)
    act, middle_grad, attn_grad, attg, sums = call(
        mlp_kernel,
        (gate_up_weight, gate_up_weight, out_weight, hidden_mid, middle, attn_out, cot, act_grad, mod),
        (
            struct((tokens, hidden_units), bf16),
            struct((tokens, width)),
            struct((tokens, width), bf16),
            struct((blocks, tokens, LANES * heads), bf16),
            struct((8, width)),
        ),
        [pltpu.VMEM((tokens, width), jnp.float32)],
        name="mlp",
        micros=12,
        specs={
            0: pl.BlockSpec((width, step_units), lambda f: (0, f)),
            1: pl.BlockSpec((width, step_units), lambda f: (0, mlp_steps + f)),
            7: pl.BlockSpec((tokens, step_units), lambda f: (0, f)),
        },
        out_specs={0: pl.BlockSpec((tokens, step_units), lambda f: (0, f))},
        grid=(mlp_steps,),
    )
    attg, h_core, h_xn, h_yn = tie(attg, h_core, h_xn, h_yn)
    attg_all = exchange(attg)
    h_dn, h_cx, h_cy = second_round(h_xn, h_yn)
    output, gmid = call(
        mlp_out_kernel,
        (act, down_weight, middle, cot, mod),
        (struct((tokens, width)), struct((8, width))),
        [pltpu.VMEM((tokens, width), jnp.float32)],
        name="mlp_out",
        specs={
            0: pl.BlockSpec((tokens, step_units), lambda f: (0, f)),
            1: pl.BlockSpec((step_units, width), lambda f: (f, 0)),
        },
        grid=(mlp_steps,),
    )
    h_dn, h_cx, h_cy, gmid = tie(h_dn, h_cx, h_cy, gmid)
    hid_pieces = (hidden_mid, h_xn, h_core, h_cx, h_yn, h_dn, h_cy, swap(h_dn, 2))
    zrows = run * lanes + width // images
    a_core, a_xn, a_yn = first_round(attn_grad)
    shares = call(
        mlp_weights_kernel,
        (*hid_pieces, *cot_pieces, own_gate, own_up, down_weight, down_weight, mod),
        (struct((zrows, units), bf16),) * 5,
        [
            pltpu.VMEM((everyone, width), bf16),
            pltpu.VMEM((everyone, width), bf16),
            pltpu.VMEM((3, everyone, units), bf16),
            pltpu.VMEM((units, width), bf16),
            pltpu.VMEM((images, zrows, units), bf16),
            pltpu.SemaphoreType.DMA((2, blocks)),
            pltpu.SemaphoreType.DMA((5,)),
        ],
        where,
        "mlp_weights",
        12,
        {
            **{index: ANY for index in range(16)},
            18: pl.BlockSpec((run, width), lambda i, s: (s[0], 0)),
            19: pl.BlockSpec((run, width), lambda i, s: (8 + s[0], 0)),
        },
        out_specs={index: ANY for index in range(5)},
    )
    attg_all, a_core, a_xn, a_yn, *shares = tie(attg_all, a_core, a_xn, a_yn, *shares)
    way = line_first(shares)
    a_dn, a_cx, a_cy = second_round(a_xn, a_yn)
    back, gain_sums = call(
        attend_back_kernel,
        (attg_all.reshape(everyone, LANES * heads), qkv, raw, turn, logs, mixed, gains, order),
        (struct((everyone, packed), bf16), struct((8, LANES))),
        [
            pltpu.VMEM((heads, LANES, everyone), bf16),
            pltpu.VMEM((3 * heads, everyone, LANES), jnp.float32),
        ],
        name="attend_back",
        micros=15,
    )
    back, way, a_dn, a_cx, a_cy = tie(back, way, a_dn, a_cx, a_cy)
    back_all = exchange(back.reshape(blocks, tokens, packed))
    a_cd = swap(a_dn, 2)
    own_back, a_cd, way = tie(back, a_cd, way)
    up, down = line_second(shares, way)
    grad_pieces = (attn_grad, a_xn, a_core, a_cx, a_yn, a_dn, a_cy, a_cd)
    (qkv_part,) = call(
        qkv_weights_kernel,
        (hid, own_back),
        (struct((blocks, width // blocks, packed), bf16),),
        name="qkv_weights",
    )
    qkv_part, att = tie(qkv_part, att)
    qkv_rows = exchange(qkv_part)
    (outw_part,) = call(
        functools.partial(out_weights_kernel, images),
        (*grad_pieces, att),
        (struct((images, span, width // images), bf16),),
        [pltpu.VMEM((everyone, width), bf16), pltpu.SemaphoreType.DMA((blocks,))],
        where,
        "out_weights",
        specs={index: ANY for index in range(blocks)},
    )
    back_all, outw_part, up, down = tie(back_all, outw_part, up, down)
    up, down = line_third(shares, up, down)
    in_grad, send = call(
        input_kernel,
        (back_all, qkv_weight, x, middle_grad, mod, sums, gmid, gain_sums, bucket),
        (struct((tokens, width)), struct((images * blocks, 8, LANES))),
        [
            pltpu.VMEM((tokens, width), jnp.float32),
            pltpu.VMEM((1, 6 * width), jnp.float32),
            pltpu.VMEM((blocks, 1024), jnp.float32),
        ],
        name="input",
        micros=7,
        specs={1: pl.BlockSpec((width, width), lambda s: (0, s)), 8: SMEM},
        grid=(3,),
    )
    send_gateup, first, second = call(
        turn_kernel,
        (shares[0], up, down),
        (
            struct((blocks, width // blocks, run), bf16),
            struct((share, run), bf16),
            struct((share, run), bf16),
        ),
        scalars=where,
        name="turn",
    )
    joined = call(
        join_kernel,
        (qkv_rows, outw_part),
        (struct((width // blocks, 4 * share), bf16),) * 5,
        [
            pltpu.VMEM((images, width // blocks, 4 * share), bf16),
            pltpu.SemaphoreType.DMA((5,)),
        ],
        where,
        "join",
        out_specs={index: ANY for index in range(5)},
    )
    way = line_first(joined)
    send, joined = tie(send, joined)
    everywhere = exchange(send, ("img", "ty", "tx"))
    everywhere, way, send_gateup = tie(everywhere, way, send_gateup)
    up, down = line_second(joined, way)
    modw_total, modb_total, qgain_total, kgain_total, act_send, condition, buckets = call(
        tail_kernel,
        (everywhere, table_share, modw_share),
        (
            struct((share, columns)),
            struct((columns,)),
            struct((HD,)),
            struct((HD,)),
            struct((blocks, 8, share)),
            struct((8, share)),
            struct((8, LANES)),
        ),
        [pltpu.VMEM((8, columns), jnp.float32), pltpu.VMEM((8, share), jnp.float32)],
        name="tail",
    )
    act_parts = exchange(act_send)
    act_parts, up, down = tie(act_parts, up, down)
    up, down = line_third(joined, up, down)
    gateup_rows = exchange(send_gateup)
    first = lax.ppermute(first, PLANE, [(t, t // 2 + 4 * (t % 2)) for t in range(8)])
    second = lax.ppermute(second, PLANE, [(t, t // 2 + 4 * (1 - t % 2)) for t in range(8)])
    (table_total,) = call(
        table_kernel,
        (act_parts, condition, buckets),
        (struct((cond_table.shape[0] // blocks, share)),),
        scalars=where,
        name="table",
    )
    gateup_total, down_total = call(
        lay_kernel,
        (gateup_rows, first, second),
        (struct((width // blocks, blocks * run)), struct((share, units))),
        scalars=where,
        name="lay",
    )
    qkv_total, outw_total = call(
        finish_kernel,
        (joined[0], up, down),
        (struct((width // blocks, 3 * share)), struct((width // blocks, share))),
        name="finish",
    )
    return (
        output.reshape(block_in.shape),
        in_grad.reshape(block_in.shape),
        table_total,
        modw_total,
        modb_total,
        qkv_total,
        qgain_total,
        kgain_total,
        outw_total,
        gateup_total,
        down_total.T,
    )


def solution(mesh):
    sizes = mesh.shape
    fits = sizes["ty"] == 4 and sizes["tx"] == 2 and sizes["img"] == 4
    return jax.shard_map(
        functools.partial(on_plane, sizes["img"]) if fits else on_device,
        mesh=mesh,
        in_specs=(
            P("img", "ty", "tx", None),
            P("img"),
            P("img", "ty", "tx", None),
            P(),
            P(None, ("ty", "tx")),
            P(("ty", "tx")),
            P(),
            P(),
            P(),
            P(),
            P(),
            P(),
            P("img", "ty", "tx", None),
        ),
        out_specs=(
            P("img", "ty", "tx", None),
            P("img", "ty", "tx", None),
            P(("ty", "tx"), "img"),
            P("img", ("ty", "tx")),
            P(("ty", "tx")),
            P(("ty", "tx"), "img"),
            P(),
            P(),
            P(("ty", "tx"), "img"),
            P(("ty", "tx"), "img"),
            P(("ty", "tx"), "img"),
        ),
        check_vma=False,
    )
```

```python
import functools
import math

import jax
import jax.numpy as jnp
from jax import lax
from jax.experimental import pallas as pl
from jax.experimental.pallas import tpu as pltpu
from jax.sharding import PartitionSpec as P

HEADS = 16
HD = 72


EPS = 1e-06
PRECISE = lax.Precision.HIGHEST


def normed(value):
    return value * lax.rsqrt(jnp.mean(value * value, axis=-1, keepdims=True) + EPS)


def norm_back(value, upstream):
    inverse = lax.rsqrt(jnp.mean(value * value, axis=-1, keepdims=True) + EPS)
    unit_value = value * inverse
    return inverse * (
        upstream - unit_value * jnp.mean(upstream * unit_value, axis=-1, keepdims=True)
    )


def rotate(value, tables, turning):
    row_cos, row_sin, col_cos, col_sin = tables
    quarter = value.shape[-1] // 4
    first = value[..., :quarter]
    second = value[..., quarter : 2 * quarter]
    third = value[..., 2 * quarter : 3 * quarter]
    fourth = value[..., 3 * quarter :]
    row_turn = turning * row_sin
    col_turn = turning * col_sin
    return jnp.concatenate(
        [
            first * row_cos - second * row_turn,
            second * row_cos + first * row_turn,
            third * col_cos - fourth * col_turn,
            fourth * col_cos + third * col_turn,
        ],
        axis=-1,
    )


def silu_slope(value):
    sigma = jax.nn.sigmoid(value)
    return sigma * (1.0 + value * (1.0 - sigma))


def product(left, right):
    return jnp.einsum("ik,kj->ij", left, right, preferred_element_type=jnp.float32)


def product_rt(left, right):
    return jnp.einsum("ik,jk->ij", left, right, preferred_element_type=jnp.float32)


def product_lt(left, right):
    return jnp.einsum("ki,kj->ij", left, right, preferred_element_type=jnp.float32)


def on_device(
    block_in,
    bucket,
    tile_anchor,
    cond_table,
    mod_weight,
    mod_bias,
    qkv_weight,
    query_gain,
    key_gain,
    out_weight,
    gate_up_weight,
    down_weight,
    cotangent,
):
    images, tile_rows, tile_cols, model_width = block_in.shape
    tokens = tile_rows * tile_cols
    all_rows = images * tokens
    head_count = HEADS
    head_size = HD
    score_scale = head_size ** (-0.5)
    hidden_units = down_weight.shape[0]
    onehot = (bucket[:, None] == jnp.arange(cond_table.shape[0], dtype=jnp.int32)[None, :]).astype(
        jnp.float32
    )
    condition = jnp.dot(onehot, cond_table, precision=PRECISE)
    cond_act = jax.nn.silu(condition).astype(jnp.bfloat16)
    mod_part = product(cond_act, mod_weight) + mod_bias[None, :]
    modulation = lax.all_gather(mod_part, ("ty", "tx"), axis=1, tiled=True)
    pieces = [
        modulation[:, None, index * model_width : (index + 1) * model_width] for index in range(6)
    ]
    shift_in, scale_in, gate_in, shift_mid, scale_mid, gate_mid = pieces
    places = jnp.arange(tokens, dtype=jnp.int32)
    row_pos = (tile_anchor[:, 0, 0, 0][:, None] + places[None, :] // tile_cols).astype(jnp.float32)
    col_pos = (tile_anchor[:, 0, 0, 1][:, None] + places[None, :] % tile_cols).astype(jnp.float32)
    quarter = head_size // 4
    frequency = jnp.exp(-math.log(10000.0) * jnp.arange(quarter, dtype=jnp.float32) / quarter)
    row_angle = row_pos[:, :, None, None] * frequency
    col_angle = col_pos[:, :, None, None] * frequency
    tables = (jnp.cos(row_angle), jnp.sin(row_angle), jnp.cos(col_angle), jnp.sin(col_angle))
    inputs = block_in.reshape(images, tokens, model_width)
    normed_in = normed(inputs)
    hidden_in = (
        (normed_in * (1.0 + scale_in) + shift_in)
        .astype(jnp.bfloat16)
        .reshape(all_rows, model_width)
    )
    qkv = product(hidden_in, qkv_weight).reshape(images, tokens, 3 * model_width)
    query_raw = qkv[..., :model_width].reshape(images, tokens, head_count, head_size)
    key_raw = qkv[..., model_width : 2 * model_width].reshape(images, tokens, head_count, head_size)
    query_unit = normed(query_raw)
    key_unit = normed(key_raw)
    query_low = rotate(query_unit * query_gain, tables, 1.0).astype(jnp.bfloat16)
    key_low = rotate(key_unit * key_gain, tables, 1.0).astype(jnp.bfloat16)
    value_low = qkv[..., 2 * model_width :].astype(jnp.bfloat16)
    keys_all, values_all = (
        lax.all_gather(
            key_low.reshape(images, tokens, model_width), ("ty", "tx"), axis=1, tiled=True
        ),
        lax.all_gather(value_low, ("ty", "tx"), axis=1, tiled=True),
    )
    key_heads = keys_all.reshape(images, -1, head_count, head_size)
    value_heads = values_all.reshape(images, -1, head_count, head_size)

    def attend(items):
        query_img, key_img, value_img = items
        scores = (
            jnp.einsum("qhd,khd->hqk", query_img, key_img, preferred_element_type=jnp.float32)
            * score_scale
        )
        row_max = jnp.max(scores, axis=-1, keepdims=True)
        expo = jnp.exp(scores - row_max)
        row_sum = jnp.sum(expo, axis=-1, keepdims=True)
        mixed = jnp.einsum(
            "hqk,khd->qhd",
            (expo / row_sum).astype(jnp.bfloat16),
            value_img,
            preferred_element_type=jnp.float32,
        )
        return (mixed, (row_max + jnp.log(row_sum))[:, :, 0])

    mixed_full, log_total = lax.map(attend, (query_low, key_heads, value_heads))
    attended = mixed_full.reshape(all_rows, model_width).astype(jnp.bfloat16)
    attn_out = product(attended, out_weight).reshape(images, tokens, model_width)
    middle = inputs + gate_in * attn_out
    normed_mid = normed(middle)
    hidden_mid = (
        (normed_mid * (1.0 + scale_mid) + shift_mid)
        .astype(jnp.bfloat16)
        .reshape(all_rows, model_width)
    )

    def feed(hidden_value):
        gate_up = product(hidden_value, gate_up_weight)
        return (gate_up[:, :hidden_units], gate_up[:, hidden_units:])

    gate_pre, up_pre = feed(hidden_mid)
    activ = (jax.nn.silu(gate_pre) * up_pre).astype(jnp.bfloat16)
    mlp_out = product(activ, down_weight).reshape(images, tokens, model_width)
    output = middle + gate_mid * mlp_out
    upstream = cotangent.reshape(images, tokens, model_width)
    gmid_grad = jnp.sum(upstream * mlp_out, axis=1)
    mlp_grad = (gate_mid * upstream).astype(jnp.bfloat16).reshape(all_rows, model_width)
    down_grad = product_lt(activ, mlp_grad)
    activ_grad = product_rt(mlp_grad, down_weight)
    gate_pre, up_pre = feed(hidden_mid)
    gu_grad = jnp.concatenate(
        [activ_grad * up_pre * silu_slope(gate_pre), activ_grad * jax.nn.silu(gate_pre)], axis=1
    ).astype(jnp.bfloat16)
    gateup_grad = product_lt(hidden_mid, gu_grad)
    mid_grad = product_rt(gu_grad, gate_up_weight).reshape(images, tokens, model_width)
    smid_grad = jnp.sum(mid_grad, axis=1)
    cmid_grad = jnp.sum(mid_grad * normed_mid, axis=1)
    middle_grad = upstream + norm_back(middle, mid_grad * (1.0 + scale_mid))
    gin_grad = jnp.sum(middle_grad * attn_out, axis=1)
    attn_grad = (gate_in * middle_grad).astype(jnp.bfloat16).reshape(all_rows, model_width)
    outw_grad = product_lt(attended, attn_grad)
    attended_grad = (
        product_rt(attn_grad, out_weight)
        .astype(jnp.bfloat16)
        .reshape(images, tokens, head_count, head_size)
    )
    row_delta = jnp.swapaxes(jnp.sum(attended_grad.astype(jnp.float32) * mixed_full, axis=-1), 1, 2)

    def score_parts(query_img, key_img, value_img, grad_img, total_img, delta_img):
        scores = (
            jnp.einsum("qhd,khd->hqk", query_img, key_img, preferred_element_type=jnp.float32)
            * score_scale
        )
        probs = jnp.exp(scores - total_img[:, :, None])
        prob_grad = jnp.einsum(
            "qhd,khd->hqk", grad_img, value_img, preferred_element_type=jnp.float32
        )
        score_grad = (probs * (prob_grad - delta_img[:, :, None])).astype(jnp.bfloat16)
        return (probs.astype(jnp.bfloat16), score_grad)

    def grads_all(items):
        query_img, key_img, value_img, grad_img, total_img, delta_img = items
        probs_low, score_grad = score_parts(
            query_img, key_img, value_img, grad_img, total_img, delta_img
        )
        query_part = (
            jnp.einsum("hqk,khd->qhd", score_grad, key_img, preferred_element_type=jnp.float32)
            * score_scale
        )
        key_part = (
            jnp.einsum("hqk,qhd->khd", score_grad, query_img, preferred_element_type=jnp.float32)
            * score_scale
        )
        value_part = jnp.einsum(
            "hqk,qhd->khd", probs_low, grad_img, preferred_element_type=jnp.float32
        )
        return (query_part, key_part.reshape(-1, model_width), value_part.reshape(-1, model_width))

    query_grad, key_full, value_full = lax.map(
        grads_all, (query_low, key_heads, value_heads, attended_grad, log_total, row_delta)
    )
    key_grad, value_grad = (
        lax.psum_scatter(
            key_full.astype(jnp.bfloat16), ("ty", "tx"), scatter_dimension=1, tiled=True
        ).astype(jnp.float32),
        lax.psum_scatter(
            value_full.astype(jnp.bfloat16), ("ty", "tx"), scatter_dimension=1, tiled=True
        ).astype(jnp.float32),
    )
    query_turned = rotate(query_grad, tables, -1.0)
    key_turned = rotate(key_grad.reshape(images, tokens, head_count, head_size), tables, -1.0)
    qgain_part = jnp.sum(query_turned * query_unit, axis=(0, 1, 2))
    kgain_part = jnp.sum(key_turned * key_unit, axis=(0, 1, 2))
    query_back = norm_back(query_raw, query_turned * query_gain).reshape(
        images, tokens, model_width
    )
    key_back = norm_back(key_raw, key_turned * key_gain).reshape(images, tokens, model_width)
    qkv_back = jnp.concatenate([query_back, key_back, value_grad], axis=-1).astype(jnp.bfloat16)
    qkv_back = qkv_back.reshape(all_rows, 3 * model_width)
    qkv_part = product_lt(hidden_in, qkv_back)
    in_back = product_rt(qkv_back, qkv_weight).reshape(images, tokens, model_width)
    sin_grad = jnp.sum(in_back, axis=1)
    cin_grad = jnp.sum(in_back * normed_in, axis=1)
    in_grad = middle_grad + norm_back(inputs, in_back * (1.0 + scale_in))
    mod_grad = jnp.concatenate(
        [sin_grad, cin_grad, gin_grad, smid_grad, cmid_grad, gmid_grad], axis=1
    )
    mod_cols = lax.psum_scatter(mod_grad, ("ty", "tx"), scatter_dimension=1, tiled=True)
    modw_part = jnp.dot(cond_act.astype(jnp.float32).T, mod_cols, precision=PRECISE)
    modb_part = jnp.sum(mod_cols, axis=0)
    act_grad = jnp.dot(mod_cols, mod_weight.astype(jnp.float32).T, precision=PRECISE)
    cond_grad = act_grad * silu_slope(condition)
    table_part = jnp.dot(onehot.T, cond_grad, precision=PRECISE)
    qkv_share, outw_share, gateup_share, down_share, table_share = (
        lax.psum_scatter(
            qkv_part.astype(jnp.bfloat16), ("ty", "tx"), scatter_dimension=0, tiled=True
        ).astype(jnp.float32),
        lax.psum_scatter(
            outw_grad.astype(jnp.bfloat16), ("ty", "tx"), scatter_dimension=0, tiled=True
        ).astype(jnp.float32),
        lax.psum_scatter(
            gateup_grad.astype(jnp.bfloat16), ("ty", "tx"), scatter_dimension=0, tiled=True
        ).astype(jnp.float32),
        lax.psum_scatter(
            down_grad.astype(jnp.bfloat16), ("ty", "tx"), scatter_dimension=0, tiled=True
        ).astype(jnp.float32),
        lax.psum_scatter(
            table_part.astype(jnp.bfloat16), ("ty", "tx"), scatter_dimension=0, tiled=True
        ).astype(jnp.float32),
    )
    qkv_total, outw_total, gateup_total, down_total, table_total = (
        lax.psum_scatter(
            qkv_share.astype(jnp.bfloat16), "img", scatter_dimension=1, tiled=True
        ).astype(jnp.float32),
        lax.psum_scatter(
            outw_share.astype(jnp.bfloat16), "img", scatter_dimension=1, tiled=True
        ).astype(jnp.float32),
        lax.psum_scatter(
            gateup_share.astype(jnp.bfloat16), "img", scatter_dimension=1, tiled=True
        ).astype(jnp.float32),
        lax.psum_scatter(
            down_share.astype(jnp.bfloat16), "img", scatter_dimension=1, tiled=True
        ).astype(jnp.float32),
        lax.psum_scatter(
            table_share.astype(jnp.bfloat16), "img", scatter_dimension=1, tiled=True
        ).astype(jnp.float32),
    )
    modw_total = lax.psum_scatter(
        modw_part.astype(jnp.bfloat16), "img", scatter_dimension=0, tiled=True
    ).astype(jnp.float32)
    modb_total = lax.psum(modb_part, "img")
    qgain_total, kgain_total = lax.psum((qgain_part, kgain_part), ("img", "ty", "tx"))
    return (
        output.reshape(block_in.shape),
        in_grad.reshape(block_in.shape),
        table_total,
        modw_total,
        modb_total,
        qkv_total,
        qgain_total,
        kgain_total,
        outw_total,
        gateup_total,
        down_total,
    )


def sigmoid(value):
    return 1.0 / (1.0 + jnp.exp(-value))


def dot_nn(left, right):
    return lax.dot_general(
        left, right, (((1,), (0,)), ((), ())), preferred_element_type=jnp.float32
    )


def dot_nt(left, right):
    return lax.dot_general(
        left, right, (((1,), (1,)), ((), ())), preferred_element_type=jnp.float32
    )


def dot_tn(left, right):
    return lax.dot_general(
        left, right, (((0,), (0,)), ((), ())), preferred_element_type=jnp.float32
    )


def column_sum(value):
    return jnp.sum(value, axis=0, keepdims=True)


EXTRA = 16
LANES = 128
QUARTER = HD // 4
PLACES = ((0, 0), (QUARTER, LANES // 2), (2 * QUARTER, QUARTER), (3 * QUARTER, LANES // 2 + QUARTER))


def lane_entry(lane):
    low = lane % (LANES // 2)
    upper = lane // (LANES // 2)
    column = low // QUARTER
    entry = jnp.where(
        low < 2 * QUARTER, low % QUARTER + QUARTER * upper + 2 * QUARTER * column, -1
    )
    return entry, column == 1


def wide_row(row, ref, line):
    for source, target in PLACES:
        ref[line : line + 1, target : target + QUARTER] = row[:, source : source + QUARTER]


def open_kernel(
    bucket_ref, anchor_ref, x_ref, table_ref, weight_ref, bias_ref, cot_ref,
    pay_ref, low_ref, wide_ref,
):
    tokens, width = x_ref.shape
    columns = weight_ref.shape[0]
    x = x_ref[...]
    pay_ref[0:tokens, :] = normed(x).astype(jnp.bfloat16)
    low_ref[...] = cot_ref[...].astype(jnp.bfloat16)
    row = table_ref[pl.ds(bucket_ref[0], 1), :]
    act = (row * sigmoid(row)).astype(jnp.bfloat16)
    mod = dot_nt(jnp.broadcast_to(act, (8, width)), weight_ref[...])
    wide_ref[...] = jnp.zeros_like(wide_ref)
    wide_ref[:, 0:columns] = mod + bias_ref[...].reshape(1, columns)
    full = wide_ref[0:1, :]
    high = full.astype(jnp.bfloat16).astype(jnp.float32)
    rest = full - high
    middle = rest.astype(jnp.bfloat16).astype(jnp.float32)
    least = rest - middle
    lane = lax.broadcasted_iota(jnp.int32, (EXTRA, width), 1)
    line = lax.broadcasted_iota(jnp.int32, (EXTRA, width), 0)
    entry, column = lane_entry(lane % LANES)
    anchor = jnp.where(
        column, anchor_ref[1].astype(jnp.float32), anchor_ref[0].astype(jnp.float32)
    )
    anchor = jnp.where(entry >= 0, anchor, 0.0)
    extra = jnp.where(
        line == 0,
        high,
        jnp.where(
            line == 1, middle, jnp.where(line == 2, least, jnp.where(line == 3, anchor, 0.0))
        ),
    )
    pay_ref[tokens : tokens + EXTRA, :] = extra.astype(jnp.bfloat16)


def ready_kernel(
    blocks, tile_cols, scalars, *refs,
):
    qkv_parts, refs = refs[:6], refs[6:]
    (
        gate_a, gate_b, up_a, up_b, qgain_ref, kgain_ref, table_ref, modw_ref,
        spread_ref, order_ref, turn_ref, gain_ref, gate_ref, up_ref, tshare_ref, mshare_ref,
        window_ref, pick_ref,
    ) = refs
    mine = scalars[0]
    share = tshare_ref.shape[1]
    for image in range(table_ref.shape[1] // share):

        @pl.when(scalars[1] == image)
        def _(image=image):
            tshare_ref[...] = table_ref[:, share * image : share * (image + 1)]
            mshare_ref[...] = modw_ref[:, share * image : share * (image + 1)]

    heads = HEADS // blocks
    span = heads * HD
    wide = 3 * heads * LANES
    for index, part in enumerate(qkv_parts):
        window_ref[:, LANES * index : LANES * (index + 1)] = part[...]
    lane = lax.broadcasted_iota(jnp.int32, (1, wide), 1)
    place = lane % LANES
    part = lane // LANES
    side = part // heads
    entry, _ = lane_entry(place)
    entry = jnp.where(side == 2, jnp.where(place < HD, place, -1), entry)
    local = HD * (part % heads) + entry
    source = jnp.where(entry >= 0, side * (2 * LANES) + mine * (span - LANES) + local, -1)
    row = lax.broadcasted_iota(jnp.int32, (wide, wide), 0)
    pick_ref[...] = (row == source).astype(jnp.float32).astype(jnp.bfloat16)
    spread_ref[...] = dot_nn(window_ref[...], pick_ref[...]).astype(jnp.bfloat16)
    source = jnp.where(entry >= 0, side * span + local, -1)
    row = lax.broadcasted_iota(jnp.int32, order_ref.shape, 0)
    order_ref[...] = (row == source).astype(jnp.float32).astype(jnp.bfloat16)
    tokens = turn_ref.shape[1]
    token = lax.broadcasted_iota(jnp.int32, (tokens, LANES), 0)
    entry, column = lane_entry(lax.broadcasted_iota(jnp.int32, (tokens, LANES), 1))
    rate = jnp.exp((entry % QUARTER).astype(jnp.float32) * (-math.log(10000.0) / QUARTER))
    rate = jnp.where(entry >= 0, rate, 0.0)
    offset = jnp.where(column, token % tile_cols, token // tile_cols).astype(jnp.float32) * rate
    turn_ref[0] = jnp.cos(offset)
    turn_ref[1] = jnp.sin(offset)
    turn_ref[2] = rate
    gain_ref[...] = jnp.zeros_like(gain_ref)
    wide_row(qgain_ref[...].reshape(1, HD), gain_ref, 0)
    wide_row(kgain_ref[...].reshape(1, HD), gain_ref, 1)
    units = gate_ref.shape[1]
    run = units // 2
    for parity in range(2):

        @pl.when(mine % 2 == parity)
        def _(parity=parity):
            for source_a, source_b, target in ((gate_a, gate_b, gate_ref), (up_a, up_b, up_ref)):
                target[:, 0:run] = source_a[:, run * parity : run * (parity + 1)]
                target[:, run:units] = source_b[:, run * parity : run * (parity + 1)]


def unit_rate(raw):
    return lax.rsqrt(jnp.sum(raw * raw, axis=-1, keepdims=True) * (1.0 / HD) + EPS)


def block_copies(pieces, ref, place, tokens, sems):
    if len(pieces) == 8:
        plan = [(piece, index, tokens, 0) for index, piece in enumerate(pieces)]
    else:
        own, xn, core, cx, yn, d1, d2, cy, cd1, cd2 = pieces
        half = d1.shape[0]
        plan = [
            (own, 0, tokens, 0), (xn, 1, tokens, 0), (core, 2, tokens, 0), (cx, 3, tokens, 0),
            (yn, 4, tokens, 0), (d1, 5, half, 0), (d2, 5, tokens - half, half), (cy, 6, tokens, 0),
            (cd1, 7, half, 0), (cd2, 7, tokens - half, half),
        ]
    return [
        pltpu.make_async_copy(
            piece.at[pl.ds(0, rows), :],
            ref.at[pl.ds(place(index) + offset, rows), :],
            sems.at[number],
        )
        for number, (piece, index, rows, offset) in enumerate(plan)
    ]


def attend_kernel(blocks, scalars, *refs):
    pieces, refs = refs[:10], refs[10:]
    (
        spread_ref, offset_ref, gain_ref,
        att_ref, hid_any, qkv_any, unit_any, turn_any, mod_ref, log_ref, mixed_ref,
        all_ref, extra_ref, rows_ref, flat_ref, anchor_ref, vt_ref,
        hid_ref, qkv_ref, unit_ref, turn_ref, sems, extra_sems, out_sems,
    ) = refs
    mine = scalars[0]
    own, xn, core, cx, yn, d1, d2, cy, cd1, cd2 = pieces
    width = own.shape[1]
    tokens = own.shape[0] - EXTRA
    columns = 6 * width // blocks
    half = d1.shape[0]
    everyone = blocks * tokens
    heads = HEADS // blocks
    extras = [
        pltpu.make_async_copy(
            piece.at[pl.ds(piece.shape[0] - EXTRA, EXTRA), :],
            extra_ref.at[index],
            extra_sems.at[index],
        )
        for index, piece in enumerate((own, xn, core, cx, yn, d2, cy, cd2))
    ]
    copies = block_copies(
        pieces,
        all_ref,
        lambda index: pl.multiple_of((mine ^ index) * tokens, tokens),
        tokens,
        sems,
    )
    for copy in (*extras, *copies):
        copy.start()
    for copy in extras:
        copy.wait()
    for index in range(blocks):
        extra = extra_ref[index].astype(jnp.float32)
        place = mine ^ index
        rows_ref[pl.ds(place, 1), :] = extra[0:1] + extra[1:2] + extra[2:3]
        anchor_ref[0, pl.ds(place, 1), :] = extra[3:4, 0:LANES]
    for index in range(blocks):
        flat_ref[0:1, columns * index : columns * (index + 1)] = rows_ref[
            index : index + 1, 0:columns
        ]
    mod_ref[...] = jnp.zeros_like(mod_ref)
    for index in range(6):
        mod_ref[index : index + 1, :] = flat_ref[0:1, width * index : width * (index + 1)]
    shift_in = mod_ref[0:1, :]
    scale_in = 1.0 + mod_ref[1:2, :]
    anchor = anchor_ref[0] * offset_ref[2, 0:blocks, :]
    anchor_ref[0] = jnp.cos(anchor)
    anchor_ref[1] = jnp.sin(anchor)
    lane = lax.broadcasted_iota(jnp.int32, (tokens, LANES), 1)
    sign = jnp.where(lane < LANES // 2, -1.0, 1.0)
    offset_cos, offset_sin = offset_ref[0], offset_ref[1]
    query_gain, key_gain = gain_ref[0:1, :], gain_ref[1:2, :]
    scale = HD ** (-0.5) * math.log2(math.e)
    for copy in copies:
        copy.wait()

    def project(index, carry):
        rows = pl.ds(pl.multiple_of(index * tokens, tokens), tokens)
        hidden = (all_ref[rows, :].astype(jnp.float32) * scale_in + shift_in).astype(jnp.bfloat16)
        hid_ref[rows, :] = hidden
        anchor_cos = anchor_ref[0, pl.ds(index, 1), :]
        anchor_sin = anchor_ref[1, pl.ds(index, 1), :]
        turn_cos = anchor_cos * offset_cos - anchor_sin * offset_sin
        turn_sin = (anchor_sin * offset_cos + anchor_cos * offset_sin) * sign
        turn_ref[0, rows, :] = turn_cos
        turn_ref[1, rows, :] = turn_sin
        product = dot_nn(hidden, spread_ref[...])
        for part in range(2 * heads):
            raw = product[:, LANES * part : LANES * (part + 1)]
            gain = query_gain * scale if part < heads else key_gain
            rate = unit_rate(raw)
            unit = raw * rate
            unit_ref[part, rows, :] = jnp.where(lane < LANES - 1, unit, rate)
            unit = unit * gain
            turned = unit * turn_cos + pltpu.roll(unit, LANES // 2, 1) * turn_sin
            qkv_ref[part, rows, :] = turned.astype(jnp.bfloat16)
        for part in range(2 * heads, 3 * heads):
            qkv_ref[part, rows, :] = product[:, LANES * part : LANES * (part + 1)].astype(
                jnp.bfloat16
            )
        return carry

    lax.fori_loop(0, blocks, project, 0, unroll=2)
    leaving = [
        pltpu.make_async_copy(source, target, out_sems.at[index])
        for index, (source, target) in enumerate(
            ((qkv_ref, qkv_any), (unit_ref, unit_any), (hid_ref, hid_any), (turn_ref, turn_any))
        )
    ]
    for copy in leaving:
        copy.start()
    chunk = 2 * tokens
    for head in range(heads):
        vt_ref[head] = qkv_ref[2 * heads + head].T

    def attend(index, carry):
        rows = pl.ds(pl.multiple_of(index * chunk, chunk), chunk)
        for head in range(heads):
            scores = dot_nt(qkv_ref[heads + head], qkv_ref[head, rows, :])
            expo = jnp.exp2(scores)
            total = column_sum(expo)
            mixed = dot_nn(vt_ref[head], expo.astype(jnp.bfloat16)) * (1.0 / total)
            log_ref[head, pl.ds(index, 1), :] = jnp.log2(total)
            mixed_ref[head, :, rows] = mixed
            for block in range(chunk // tokens):
                att_ref[index * (chunk // tokens) + block, HD * head : HD * (head + 1), :] = mixed[
                    0:HD, tokens * block : tokens * (block + 1)
                ].astype(jnp.bfloat16)
        return carry

    lax.fori_loop(0, everyone // chunk, attend, 0, unroll=2)
    for copy in leaving:
        copy.wait()


def middle_kernel(att_ref, weight_ref, x_ref, mod_ref, out_ref, mid_ref, hid_ref):
    attended = att_ref[...].reshape(weight_ref.shape[0], att_ref.shape[2])
    attn_out = dot_tn(attended, weight_ref[...])
    out_ref[...] = attn_out
    middle = x_ref[...] + mod_ref[2:3, :] * attn_out
    mid_ref[...] = middle
    hid_ref[...] = (normed(middle) * (1.0 + mod_ref[4:5, :]) + mod_ref[3:4, :]).astype(
        jnp.bfloat16
    )


def act_grad_kernel(down_ref, cot_ref, mod_ref, out_ref, low_ref):
    @pl.when(pl.program_id(0) == 0)
    def _():
        low_ref[...] = (mod_ref[5:6, :] * cot_ref[...]).astype(jnp.bfloat16)

    out_ref[...] = dot_nt(low_ref[...], down_ref[...])


def mlp_kernel(
    gate_ref, up_ref, outw_ref, hid_ref, mid_ref, attn_ref, cot_ref, agrad_in, mod_ref,
    act_ref, mgrad_ref, agrad_ref, dgrad_ref, sums_ref, back_ref,
):
    step = pl.program_id(0)

    hidden = hid_ref[...]
    gate = dot_nn(hidden, gate_ref[...])
    up = dot_nn(hidden, up_ref[...])
    sigma = sigmoid(gate)
    silu = gate * sigma
    act_ref[...] = (silu * up).astype(jnp.bfloat16)
    act_grad = agrad_in[...]
    slope = sigma * (1.0 + gate * (1.0 - sigma))
    gate_grad = (act_grad * up * slope).astype(jnp.bfloat16)
    up_grad = (act_grad * silu).astype(jnp.bfloat16)
    part = dot_nt(gate_grad, gate_ref[...]) + dot_nt(up_grad, up_ref[...])

    @pl.when(step == 0)
    def _():
        back_ref[...] = part

    @pl.when(step > 0)
    def _():
        back_ref[...] += part

    @pl.when(step == pl.num_programs(0) - 1)
    def _():
        middle = mid_ref[...]
        upstream = cot_ref[...]
        back = back_ref[...]
        inverse = lax.rsqrt(jnp.mean(middle * middle, axis=-1, keepdims=True) + EPS)
        unit = middle * inverse
        lifted = back * (1.0 + mod_ref[4:5, :])
        middle_grad = upstream + inverse * (
            lifted - unit * jnp.mean(lifted * unit, axis=-1, keepdims=True)
        )
        mgrad_ref[...] = middle_grad
        attn_grad = (mod_ref[2:3, :] * middle_grad).astype(jnp.bfloat16)
        agrad_ref[...] = attn_grad
        attended = dot_nt(outw_ref[...], attn_grad).astype(jnp.bfloat16)
        dgrad_ref[...] = attended.reshape(dgrad_ref.shape)
        sums_ref[...] = jnp.zeros_like(sums_ref)
        sums_ref[2:3, :] = column_sum(middle_grad * attn_ref[...])
        sums_ref[3:4, :] = column_sum(back)
        sums_ref[4:5, :] = column_sum(back * unit)


def mlp_out_kernel(act_ref, down_ref, mid_ref, cot_ref, mod_ref, output_ref, sum_ref, acc_ref):
    step = pl.program_id(0)
    part = dot_nn(act_ref[...], down_ref[...])

    @pl.when(step == 0)
    def _():
        acc_ref[...] = part

    @pl.when(step > 0)
    def _():
        acc_ref[...] += part

    @pl.when(step == pl.num_programs(0) - 1)
    def _():
        output_ref[...] = mid_ref[...] + mod_ref[5:6, :] * acc_ref[...]
        sum_ref[...] = jnp.broadcast_to(column_sum(cot_ref[...] * acc_ref[...]), sum_ref.shape)


def mlp_weights_kernel(scalars, *refs):
    hid_pieces, cot_pieces, refs = refs[:8], refs[8:16], refs[16:]
    (
        gate_ref, up_ref, down_a, down_b, mod_ref, own_ref, near_ref, two_ref, far_ref,
        all_ref, low_ref, act_ref, down_ref, out_ref, sems, out_sems,
    ) = refs
    tokens, width = hid_pieces[0].shape
    everyone = all_ref.shape[0]
    run = down_a.shape[0]
    units = 2 * run
    copies = [
        *block_copies(hid_pieces, all_ref, lambda index: index * tokens, tokens, sems.at[0]),
        *block_copies(cot_pieces, low_ref, lambda index: index * tokens, tokens, sems.at[1]),
    ]
    for copy in copies:
        copy.start()
    down_ref[0:run, :] = down_a[...]
    down_ref[run:units, :] = down_b[...]
    gate_mid = mod_ref[5:6, :]
    chunk = everyone // 2
    early = [copies[index] for index in (0, 1, 2, 3, 8, 9, 10, 11)]
    late = [copies[index] for index in (4, 5, 6, 7, 12, 13, 14, 15)]
    for copy in early:
        copy.wait()

    def chunked(index, carry):
        @pl.when(index == 1)
        def _():
            for copy in late:
                copy.wait()

        span = pl.ds(pl.multiple_of(index * chunk, chunk), chunk)
        low = (low_ref[span, :].astype(jnp.float32) * gate_mid).astype(jnp.bfloat16)
        low_ref[span, :] = low
        hidden = all_ref[span, :]
        gate = dot_nn(hidden, gate_ref[...])
        up = dot_nn(hidden, up_ref[...])
        act_grad = dot_nt(low, down_ref[...])
        sigma = sigmoid(gate)
        silu = gate * sigma
        slope = sigma * (1.0 + gate * (1.0 - sigma))
        act_ref[0, span, :] = (silu * up).astype(jnp.bfloat16)
        act_ref[1, span, :] = (act_grad * up * slope).astype(jnp.bfloat16)
        act_ref[2, span, :] = (act_grad * silu).astype(jnp.bfloat16)
        return carry

    lax.fori_loop(0, everyone // chunk, chunked, 0)
    lanes = width // units
    for side in range(2):
        grad = dot_tn(act_ref[1 + side], all_ref[...]).astype(jnp.bfloat16)
        for part in range(2):
            for index in range(lanes):
                out_ref[2 * side + part, run * index : run * (index + 1), :] = grad[
                    run * part : run * (part + 1), units * index : units * (index + 1)
                ]
    down = dot_tn(act_ref[0], low_ref[...]).astype(jnp.bfloat16).T
    share = width // out_ref.shape[0]
    for image in range(out_ref.shape[0]):
        out_ref[image, run * lanes : run * lanes + share, :] = down[
            share * image : share * (image + 1), :
        ]
    deal(out_ref, scalars[1], (own_ref, near_ref, two_ref, far_ref), out_sems)


def deal(ref, place, targets, sems):
    owners = [place ^ bits for bits in range(4)]
    copies = [
        pltpu.make_async_copy(ref.at[owner], target, sems.at[index])
        for index, (owner, target) in enumerate(zip(owners, targets, strict=True))
    ]
    for copy in copies:
        copy.start()
    for copy in copies:
        copy.wait()


def summed(refs, rows):
    total = refs[0][rows, :].astype(jnp.float32)
    for ref in refs[1:]:
        total = total + ref[rows, :].astype(jnp.float32)
    return total


def turn_kernel(scalars, *refs):
    parts, refs = refs[:5], refs[5:]
    send_ref, first_ref, second_ref = refs
    blocks, rows, run = send_ref.shape
    units = parts[0].shape[1]
    lanes = rows * blocks // units
    whole = jnp.concatenate(
        [summed(parts, pl.ds(run * index, run)).T for index in range(lanes)], axis=0
    )
    send_ref[...] = whole.astype(jnp.bfloat16).reshape(send_ref.shape)
    down = summed(parts, pl.ds(run * lanes, first_ref.shape[0])).astype(jnp.bfloat16)
    even = scalars[0] % 2 == 0
    for parity in range(2):

        @pl.when(scalars[0] % 2 == parity)
        def _(parity=parity):
            first_ref[...] = down[:, run * parity : run * (parity + 1)]
            second_ref[...] = down[:, run * (1 - parity) : run * (2 - parity)]


def lay_kernel(scalars, got_ref, first_ref, second_ref, *refs):
    parts, (gateup_ref, down_ref, qkv_ref, out_ref) = refs[:5], refs[5:]
    gateup_ref[...] = jnp.concatenate(
        [got_ref[index].astype(jnp.float32) for index in range(got_ref.shape[0])], axis=1
    )
    first = first_ref[...].astype(jnp.float32)
    second = second_ref[...].astype(jnp.float32)
    half = got_ref.shape[0] // 2

    @pl.when(scalars[0] < half)
    def _():
        down_ref[...] = jnp.concatenate([first, second], axis=1)

    @pl.when(scalars[0] >= half)
    def _():
        down_ref[...] = jnp.concatenate([second, first], axis=1)

    total = summed(parts, pl.ds(0, qkv_ref.shape[0]))
    columns = qkv_ref.shape[1]
    qkv_ref[...] = total[:, 0:columns]
    out_ref[...] = total[:, columns:]


def dot_exact(left, right, dims):
    total = None
    for _ in range(3):
        part = left.astype(jnp.bfloat16)
        left = left - part.astype(jnp.float32)
        product = lax.dot_general(
            part, right, (dims, ((), ())), preferred_element_type=jnp.float32
        )
        total = product if total is None else total + product
    return total


def tail_kernel(
    got_ref, table_ref, weight_ref,
    modw_ref, modb_ref, qgain_ref, kgain_ref, send_ref, cond_ref, bucket_ref,
    cols_ref, act_ref,
):
    columns = modb_ref.shape[0]
    blocks = send_ref.shape[0]
    images = got_ref.shape[0] // blocks
    lines = table_ref.shape[0]
    cols_ref[...] = jnp.zeros_like(cols_ref)
    act_ref[...] = jnp.zeros_like(act_ref)
    bucket_ref[...] = jnp.full(bucket_ref.shape, -1.0, jnp.float32)
    cond_ref[...] = jnp.zeros_like(cond_ref)
    gains = None
    line = lax.broadcasted_iota(jnp.int32, (lines, 1), 0).astype(jnp.float32)
    for image in range(images):
        total = got_ref[blocks * image]
        for index in range(1, blocks):
            total = total + got_ref[blocks * image + index]
        row = jnp.concatenate([total[index : index + 1, :] for index in range(8)], axis=1)
        cols_ref[image : image + 1, :] = row[:, 0:columns]
        gains = row if gains is None else gains + row
        first = got_ref[blocks * image]
        place = columns // LANES
        bucket = first[place : place + 1, columns % LANES : columns % LANES + 1]
        bucket_ref[image : image + 1, :] = jnp.broadcast_to(bucket, (1, LANES))
        cond = jnp.sum(
            jnp.where(line == bucket, table_ref[...], 0.0), axis=0, keepdims=True
        )
        cond_ref[image : image + 1, :] = cond
        act_ref[image : image + 1, :] = (
            (cond * sigmoid(cond)).astype(jnp.bfloat16).astype(jnp.float32)
        )
    cols = cols_ref[...]
    modw_ref[...] = lax.dot_general(
        act_ref[...], cols, (((0,), (0,)), ((), ())),
        precision=PRECISE, preferred_element_type=jnp.float32,
    )
    modb_ref[...] = column_sum(cols).reshape(columns)
    start = columns + 16
    qgain_ref[...] = gains[:, start : start + HD].reshape(HD)
    kgain_ref[...] = gains[:, start + HD : start + 2 * HD].reshape(HD)
    part = dot_exact(cols, weight_ref[...], ((1,), (0,)))
    send_ref[...] = jnp.broadcast_to(part[None], send_ref.shape)


def table_kernel(scalars, got_ref, cond_ref, bucket_ref, out_ref):
    total = jnp.sum(got_ref[...], axis=0)
    cond = cond_ref[...]
    sigma = sigmoid(cond)
    grad = total * (sigma * (1.0 + cond * (1.0 - sigma)))
    lines = out_ref.shape[0]
    line = lax.broadcasted_iota(jnp.int32, (lines, 1), 0) + scalars[0] * lines
    out = jnp.zeros(out_ref.shape, jnp.float32)
    for image in range(4):
        hot = line.astype(jnp.float32) == bucket_ref[image : image + 1, 0:1]
        out = out + jnp.where(hot, grad[image : image + 1, :], 0.0)
    out_ref[...] = out


def attend_back_kernel(
    attg_ref, qkv_ref, log_ref, mixed_ref, gain_ref, unit_any, turn_any, order_any,
    back_ref, gsum_ref, kt_ref, up_ref, upt_ref, grad_ref, unit_ref, turn_ref, order_ref, sems,
):
    blocks, _, tokens = attg_ref.shape
    heads = HEADS // blocks
    everyone = blocks * tokens
    lines, chunk = log_ref.shape[1:]
    scale = HD ** (-0.5)
    late = [
        pltpu.make_async_copy(source, target, sems.at[index])
        for index, (source, target) in enumerate(
            ((unit_any, unit_ref), (turn_any, turn_ref), (order_any, order_ref))
        )
    ]
    for copy in late:
        copy.start()
    query_gain, key_gain = gain_ref[0:1, :], gain_ref[1:2, :]
    for head in range(heads):
        kt_ref[head] = qkv_ref[heads + head].T
        grad_ref[heads + head] = jnp.zeros((everyone, LANES), jnp.float32)
        grad_ref[2 * heads + head] = jnp.zeros((everyone, LANES), jnp.float32)
        for block in range(blocks):
            piece = jnp.concatenate(
                [
                    attg_ref[block, HD * head : HD * (head + 1), :],
                    jnp.zeros((LANES - HD, tokens), jnp.bfloat16),
                ],
                axis=0,
            )
            upt_ref[head, :, tokens * block : tokens * (block + 1)] = piece
        up_ref[head] = upt_ref[head].T

    def attend(index, carry):
        rows = pl.ds(pl.multiple_of(index * chunk, chunk), chunk)
        for head in range(heads):
            query = qkv_ref[head, rows, :]
            upstream = up_ref[head, rows, :]
            turned = upt_ref[head, :, rows]
            delta = column_sum(turned.astype(jnp.float32) * mixed_ref[head, :, rows])
            probs = jnp.exp2(
                dot_nt(qkv_ref[heads + head], query) - log_ref[head, pl.ds(index, 1), :]
            )
            score_grad = (probs * (dot_nn(qkv_ref[2 * heads + head], turned) - delta)).astype(
                jnp.bfloat16
            )
            grad_ref[2 * heads + head] += dot_nn(probs.astype(jnp.bfloat16), upstream)
            grad_ref[heads + head] += dot_nn(score_grad, query)
            grad_ref[head, rows, :] = dot_nn(kt_ref[head], score_grad).T
        return carry

    lax.fori_loop(0, lines, attend, 0, unroll=2)
    gsum_ref[...] = jnp.zeros_like(gsum_ref)
    step = tokens
    for copy in late:
        copy.wait()

    def finish(index, carry):
        rows = pl.ds(pl.multiple_of(index * step, step), step)
        turn_cos = turn_ref[0, rows, :]
        turn_sin = turn_ref[1, rows, :]
        parts = []
        for part in range(2 * heads):
            gain = query_gain if part < heads else key_gain
            grad = grad_ref[part, rows, :] * (scale if part < heads else math.log(2.0))
            turned = grad * turn_cos - pltpu.roll(grad, LANES // 2, 1) * turn_sin
            unit = unit_ref[part, rows, :]
            rate = unit[:, LANES - 1 : LANES]
            line = 0 if part < heads else 1
            product = turned * unit
            gsum_ref[line : line + 1, :] += column_sum(product)
            mean = jnp.sum(product * gain, axis=-1, keepdims=True) * (1.0 / HD)
            parts.append((rate * (turned * gain - unit * mean)).astype(jnp.bfloat16))
        for part in range(2 * heads, 3 * heads):
            parts.append(grad_ref[part, rows, :].astype(jnp.bfloat16))
        back_ref[index] = dot_nt(order_ref[...], jnp.concatenate(parts, axis=1)).astype(
            jnp.bfloat16
        )
        return carry

    lax.fori_loop(0, everyone // step, finish, 0, unroll=2)


def qkv_weights_kernel(hid_ref, back_ref, grad_ref):
    blocks = back_ref.shape[0]
    back = jnp.concatenate([back_ref[index] for index in range(blocks)], axis=1)
    grad = dot_nn(back, hid_ref[...]).astype(jnp.bfloat16).T
    columns = grad.shape[1]
    grad_ref[:, :, LANES * (columns // LANES) :] = jnp.zeros(
        (*grad_ref.shape[:2], grad_ref.shape[2] - LANES * (columns // LANES)), jnp.bfloat16
    )
    grad_ref[:, :, 0:columns] = grad.reshape(*grad_ref.shape[:2], columns)


def out_weights_kernel(images, scalars, *refs):
    pieces, refs = refs[:8], refs[8:]
    att_ref, ograd_ref, low_ref, sems = refs
    tokens, width = pieces[0].shape
    mine = scalars[0]
    copies = block_copies(
        pieces,
        low_ref,
        lambda index: pl.multiple_of((mine ^ index) * tokens, tokens),
        tokens,
        sems,
    )
    for copy in copies:
        copy.start()
    for copy in copies:
        copy.wait()
    attended = jnp.concatenate([att_ref[index] for index in range(att_ref.shape[0])], axis=1)
    outw = dot_nn(attended, low_ref[...]).astype(jnp.bfloat16)
    share = width // images
    for image in range(images):
        ograd_ref[image] = outw[:, share * image : share * (image + 1)]


def join_kernel(scalars, grad_ref, ograd_ref, *refs):
    targets, (out_ref, sems) = refs[:4], refs[4:]
    images = out_ref.shape[0]
    blocks = grad_ref.shape[0]
    span = HD * HEADS // blocks
    whole = jnp.concatenate(
        [
            grad_ref[index][:, span * side : span * (side + 1)]
            for side in range(3)
            for index in range(blocks)
        ],
        axis=1,
    )
    share = whole.shape[1] // images
    for image in range(images):
        out_ref[image] = jnp.concatenate(
            [whole[:, share * image : share * (image + 1)], ograd_ref[image]], axis=1
        )
    deal(out_ref, scalars[1], targets, sems)


def input_kernel(
    back_ref, weight_ref, x_ref, mgrad_ref, mod_ref, sums_ref, gmid_ref, gsum_ref, bucket_ref,
    grad_ref, send_ref, acc_ref, flat_ref, row_ref,
):
    step = pl.program_id(0)
    blocks = back_ref.shape[0]
    span = HD * HEADS // blocks
    width = x_ref.shape[1]
    columns = 6 * width // blocks

    for side in range(3):

        @pl.when(step == side)
        def _(side=side):
            natural = jnp.concatenate(
                [back_ref[index, span * side : span * (side + 1), :] for index in range(blocks)],
                axis=0,
            )
            part = lax.dot_general(
                natural, weight_ref[...], (((0,), (1,)), ((), ())),
                preferred_element_type=jnp.float32,
            )
            acc_ref[...] = part if side == 0 else acc_ref[...] + part

    @pl.when(step == 2)
    def _():
        x = x_ref[...]
        back = acc_ref[...]
        inverse = lax.rsqrt(jnp.mean(x * x, axis=-1, keepdims=True) + EPS)
        unit = x * inverse
        lifted = back * (1.0 + mod_ref[1:2, :])
        grad_ref[...] = mgrad_ref[...] + inverse * (
            lifted - unit * jnp.mean(lifted * unit, axis=-1, keepdims=True)
        )
        flat_ref[0:1, 0:width] = column_sum(back)
        flat_ref[0:1, width : 2 * width] = column_sum(back * unit)
        for index in range(2, 5):
            flat_ref[0:1, width * index : width * (index + 1)] = sums_ref[index : index + 1, :]
        flat_ref[0:1, width * 5 : width * 6] = gmid_ref[0:1, :]
        row_ref[...] = jnp.zeros_like(row_ref)
        for index in range(blocks):
            row_ref[index : index + 1, 0:columns] = flat_ref[
                0:1, columns * index : columns * (index + 1)
            ]
        row_ref[:, columns : columns + 1] = jnp.broadcast_to(
            bucket_ref[0].astype(jnp.float32), (blocks, 1)
        )
        for line in range(2):
            for source, target in PLACES:
                start = columns + 16 + HD * line + source
                row_ref[:, start : start + QUARTER] = jnp.broadcast_to(
                    gsum_ref[line : line + 1, target : target + QUARTER], (blocks, QUARTER)
                )
        for index in range(blocks):
            tile = jnp.concatenate(
                [
                    row_ref[index : index + 1, LANES * part : LANES * (part + 1)]
                    for part in range(8)
                ],
                axis=0,
            )
            for image in range(send_ref.shape[0] // blocks):
                send_ref[blocks * image + index] = tile


def whole_spec(shape):
    return pl.BlockSpec(tuple(shape), lambda *_, n=len(shape): (0,) * n)


ANY = pl.BlockSpec(memory_space=pl.ANY)
SMEM = pl.BlockSpec(memory_space=pltpu.SMEM)


def call(
    kernel, operands, outs, scratch=(), scalars=None, name=None, micros=5, specs=None, grid=(1,),
    out_specs=None,
):
    return pl.pallas_call(
        kernel,
        out_shape=outs,
        grid_spec=pltpu.PrefetchScalarGridSpec(
            num_scalar_prefetch=0 if scalars is None else 1,
            grid=grid,
            in_specs=[
                (specs or {}).get(index) or whole_spec(a.shape) for index, a in enumerate(operands)
            ],
            out_specs=[
                (out_specs or {}).get(index) or whole_spec(o.shape) for index, o in enumerate(outs)
            ],
            scratch_shapes=list(scratch),
        ),
        cost_estimate=pl.CostEstimate(
            flops=int(micros * 1e9), transcendentals=0, bytes_accessed=int(micros * 1e6)
        ),
        name=name,
    )(*(() if scalars is None else (scalars,)), *operands)


def struct(shape, dtype=jnp.float32):
    return jax.ShapeDtypeStruct(shape, dtype)


PLANE = ("ty", "tx")


def swap(value, bit):
    return lax.ppermute(value, PLANE, [(index, index ^ bit) for index in range(8)])


def first_round(value):
    return swap(value, 2), swap(value, 1), swap(value, 4)


def split_round(xn, yn, half):
    d1 = swap(xn[:half], 4)
    cx = swap(xn, 2)
    d2 = swap(yn[half:], 1)
    return d1, d2, cx, swap(yn, 2)


def second_round(xn, yn):
    return swap(xn, 4), swap(xn, 2), swap(yn, 2)


def tie(*values):
    return lax.optimization_barrier(values)


def exchange(value, axes=PLANE):
    return lax.all_to_all(value, axes, split_axis=0, concat_axis=0, tiled=True)


def shift(value, pairs):
    return lax.ppermute(value, "img", pairs)


def onward(value, step):
    return shift(value, [(i, (i + step) % 4) for i in range(4)])


def add(left, right):
    return (left.astype(jnp.float32) + right.astype(jnp.float32)).astype(jnp.bfloat16)


def line_first(shares):
    return shift(shares[3], [(0, 1), (3, 2)]), shift(shares[3], [(1, 2), (2, 1)])


def line_second(shares, way):
    return (
        shift(add(shares[2], way), [(1, 3), (2, 0)]),
        shift(shares[2], [(0, 2), (3, 1)]),
        shift(shares[1], [(0, 1), (1, 0), (2, 3), (3, 2)]),
    )


def on_plane(
    images,
    block_in,
    bucket,
    tile_anchor,
    cond_table,
    mod_weight,
    mod_bias,
    qkv_weight,
    query_gain,
    key_gain,
    out_weight,
    gate_up_weight,
    down_weight,
    cotangent,
):
    blocks = 8
    _, tile_rows, tile_cols, width = block_in.shape
    tokens = tile_rows * tile_cols
    everyone = blocks * tokens
    hidden_units = down_weight.shape[0]
    units = hidden_units // blocks
    run = units // 2
    lanes = width // units
    heads = HEADS // blocks
    span = heads * HD
    columns = mod_weight.shape[1]
    wide = 3 * heads * LANES
    packed = -(-3 * span // LANES) * LANES
    bf16 = jnp.bfloat16
    image = lax.axis_index("img")
    mine = lax.axis_index("ty") * 2 + lax.axis_index("tx")
    where = jnp.stack([mine, image]).astype(jnp.int32)
    share = width // images
    x = block_in.reshape(tokens, width)
    cot = cotangent.reshape(tokens, width)
    half = tokens // 2
    pay, low_cot = call(
        open_kernel,
        (bucket, tile_anchor.reshape(2), x, cond_table, mod_weight.T, mod_bias, cot),
        (struct((tokens + EXTRA, width), bf16), struct((tokens, width), bf16)),
        [pltpu.VMEM((8, width), jnp.float32)],
        name="open",
        specs={0: SMEM, 1: SMEM},
    )
    core, xn, yn = first_round(pay)
    spread, order, offsets, gains, own_gate, own_up, table_share, modw_share = call(
        functools.partial(ready_kernel, blocks, tile_cols),
        (*[qkv_weight] * 6, *[gate_up_weight] * 4, query_gain, key_gain, cond_table, mod_weight.T),
        (
            struct((width, wide), bf16),
            struct((3 * span, wide), bf16),
            struct((3, tokens, LANES)),
            struct((8, LANES)),
            struct((width, units), bf16),
            struct((width, units), bf16),
            struct((cond_table.shape[0], share)),
            struct((columns, share), bf16),
        ),
        [pltpu.VMEM((width, wide), bf16), pltpu.VMEM((wide, wide), bf16)],
        where,
        "ready",
        specs={
            **{
                2 * side + n: pl.BlockSpec(
                    (width, LANES), lambda i, s, c=side * width // LANES + n: (0, c + s[0])
                )
                for side in range(3)
                for n in range(2)
            },
            **{
                6 + n: pl.BlockSpec((width, units), lambda i, s, n=n: (0, n * 4 + s[0] // 2))
                for n in range(4)
            },
        },
    )
    xn, yn, spread, order, offsets, gains, own_gate, own_up = tie(
        xn, yn, spread, order, offsets, gains, own_gate, own_up
    )
    d1, d2, cx, cy = split_round(xn, yn, half)
    pieces = (pay, xn, core, cx, yn, d1, d2, cy, swap(d1, 2), swap(d2, 2))
    c_core, c_xn, c_yn = first_round(low_cot)
    att, hid, qkv, unit, turn, mod, logs, mixed = call(
        functools.partial(attend_kernel, blocks),
        (*pieces, spread, offsets, gains),
        (
            struct((blocks, span, tokens), bf16),
            struct((everyone, width), bf16),
            struct((3 * heads, everyone, LANES), bf16),
            struct((2 * heads, everyone, LANES)),
            struct((2, everyone, LANES)),
            struct((8, width)),
            struct((heads, everyone // (2 * tokens), 2 * tokens)),
            struct((heads, LANES, everyone)),
        ),
        [
            pltpu.VMEM((everyone, width), bf16),
            pltpu.VMEM((blocks, EXTRA, width), bf16),
            pltpu.VMEM((8, width), jnp.float32),
            pltpu.VMEM((1, 6 * width), jnp.float32),
            pltpu.VMEM((2, 8, LANES), jnp.float32),
            pltpu.VMEM((heads, LANES, everyone), bf16),
            pltpu.VMEM((everyone, width), bf16),
            pltpu.VMEM((3 * heads, everyone, LANES), bf16),
            pltpu.VMEM((2 * heads, everyone, LANES), jnp.float32),
            pltpu.VMEM((2, everyone, LANES), jnp.float32),
            pltpu.SemaphoreType.DMA((10,)),
            pltpu.SemaphoreType.DMA((blocks,)),
            pltpu.SemaphoreType.DMA((4,)),
        ],
        where,
        "attend",
        15,
        {index: ANY for index in range(10)},
        out_specs={index: ANY for index in range(1, 5)},
    )
    att, c_core, c_xn, c_yn = tie(att, c_core, c_xn, c_yn)
    att_all = exchange(att)
    c_dn, c_cx, c_cy = second_round(c_xn, c_yn)
    mlp_steps = 4
    step_units = hidden_units // mlp_steps
    (act_grad,) = call(
        act_grad_kernel,
        (down_weight, cot, mod),
        (struct((tokens, hidden_units)),),
        [pltpu.VMEM((tokens, width), bf16)],
        name="act_grad",
        specs={0: pl.BlockSpec((step_units, width), lambda f: (f, 0))},
        out_specs={0: pl.BlockSpec((tokens, step_units), lambda f: (0, f))},
        grid=(mlp_steps,),
    )
    att_all, c_dn, c_cx, c_cy, act_grad = tie(att_all, c_dn, c_cx, c_cy, act_grad)
    cot_pieces = (low_cot, c_xn, c_core, c_cx, c_yn, c_dn, c_cy, swap(c_dn, 2))
    attn_out, middle, hidden_mid = call(
        middle_kernel,
        (att_all, out_weight, x, mod),
        (struct((tokens, width)), struct((tokens, width)), struct((tokens, width), bf16)),
        name="middle",
    )
    h_core, h_xn, h_yn = first_round(hidden_mid)
    act, middle_grad, attn_grad, attg, sums = call(
        mlp_kernel,
        (gate_up_weight, gate_up_weight, out_weight, hidden_mid, middle, attn_out, cot, act_grad, mod),
        (
            struct((tokens, hidden_units), bf16),
            struct((tokens, width)),
            struct((tokens, width), bf16),
            struct((blocks, span, tokens), bf16),
            struct((8, width)),
        ),
        [pltpu.VMEM((tokens, width), jnp.float32)],
        name="mlp",
        micros=12,
        specs={
            0: pl.BlockSpec((width, step_units), lambda f: (0, f)),
            1: pl.BlockSpec((width, step_units), lambda f: (0, mlp_steps + f)),
            7: pl.BlockSpec((tokens, step_units), lambda f: (0, f)),
        },
        out_specs={0: pl.BlockSpec((tokens, step_units), lambda f: (0, f))},
        grid=(mlp_steps,),
    )
    attg, h_core, h_xn, h_yn = tie(attg, h_core, h_xn, h_yn)
    attg_all = exchange(attg)
    h_dn, h_cx, h_cy = second_round(h_xn, h_yn)
    output, gmid = call(
        mlp_out_kernel,
        (act, down_weight, middle, cot, mod),
        (struct((tokens, width)), struct((8, width))),
        [pltpu.VMEM((tokens, width), jnp.float32)],
        name="mlp_out",
        specs={
            0: pl.BlockSpec((tokens, step_units), lambda f: (0, f)),
            1: pl.BlockSpec((step_units, width), lambda f: (f, 0)),
        },
        grid=(mlp_steps,),
    )
    h_dn, h_cx, h_cy, gmid = tie(h_dn, h_cx, h_cy, gmid)
    hid_pieces = (hidden_mid, h_xn, h_core, h_cx, h_yn, h_dn, h_cy, swap(h_dn, 2))
    zrows = run * lanes + width // images
    a_core, a_xn, a_yn = first_round(attn_grad)
    shares = call(
        mlp_weights_kernel,
        (*hid_pieces, *cot_pieces, own_gate, own_up, down_weight, down_weight, mod),
        (struct((zrows, units), bf16),) * 4,
        [
            pltpu.VMEM((everyone, width), bf16),
            pltpu.VMEM((everyone, width), bf16),
            pltpu.VMEM((3, everyone, units), bf16),
            pltpu.VMEM((units, width), bf16),
            pltpu.VMEM((images, zrows, units), bf16),
            pltpu.SemaphoreType.DMA((2, blocks)),
            pltpu.SemaphoreType.DMA((4,)),
        ],
        where,
        "mlp_weights",
        12,
        {
            **{index: ANY for index in range(16)},
            18: pl.BlockSpec((run, width), lambda i, s: (s[0], 0)),
            19: pl.BlockSpec((run, width), lambda i, s: (8 + s[0], 0)),
        },
        out_specs={index: ANY for index in range(4)},
    )
    attg_all, a_core, a_xn, a_yn, *shares = tie(attg_all, a_core, a_xn, a_yn, *shares)
    way, mid = line_first(shares)
    a_dn, a_cx, a_cy = second_round(a_xn, a_yn)
    back, gain_sums = call(
        attend_back_kernel,
        (attg_all, qkv, logs, mixed, gains, unit, turn, order),
        (struct((blocks, 3 * span, tokens), bf16), struct((8, LANES))),
        [
            pltpu.VMEM((heads, LANES, everyone), bf16),
            pltpu.VMEM((heads, everyone, LANES), bf16),
            pltpu.VMEM((heads, LANES, everyone), bf16),
            pltpu.VMEM((3 * heads, everyone, LANES), jnp.float32),
            pltpu.VMEM(unit.shape, jnp.float32),
            pltpu.VMEM(turn.shape, jnp.float32),
            pltpu.VMEM(order.shape, bf16),
            pltpu.SemaphoreType.DMA((3,)),
        ],
        specs={5: ANY, 6: ANY, 7: ANY},
        name="attend_back",
        micros=15,
    )
    back, way, mid, a_dn, a_cx, a_cy = tie(back, way, mid, a_dn, a_cx, a_cy)
    back_all = exchange(back)
    a_cd = swap(a_dn, 2)
    own_back, a_cd, way = tie(back, a_cd, way)
    other, two, near = line_second(shares, way)
    grad_pieces = (attn_grad, a_xn, a_core, a_cx, a_yn, a_dn, a_cy, a_cd)
    (qkv_part,) = call(
        qkv_weights_kernel,
        (hid, own_back),
        (struct((blocks, width // blocks, packed), bf16),),
        name="qkv_weights",
    )
    qkv_part, att = tie(qkv_part, att)
    qkv_rows = exchange(qkv_part)
    (outw_part,) = call(
        functools.partial(out_weights_kernel, images),
        (*grad_pieces, att),
        (struct((images, span, width // images), bf16),),
        [pltpu.VMEM((everyone, width), bf16), pltpu.SemaphoreType.DMA((blocks,))],
        where,
        "out_weights",
        specs={index: ANY for index in range(blocks)},
    )
    back_all, outw_part = tie(back_all, outw_part)
    in_grad, send = call(
        input_kernel,
        (back_all, qkv_weight, x, middle_grad, mod, sums, gmid, gain_sums, bucket),
        (struct((tokens, width)), struct((images * blocks, 8, LANES))),
        [
            pltpu.VMEM((tokens, width), jnp.float32),
            pltpu.VMEM((1, 6 * width), jnp.float32),
            pltpu.VMEM((blocks, 1024), jnp.float32),
        ],
        name="input",
        micros=7,
        specs={1: pl.BlockSpec((width, width), lambda s: (0, s)), 8: SMEM},
        grid=(3,),
    )
    send, qkv_rows = tie(send, qkv_rows)
    everywhere = exchange(send, ("img", "ty", "tx"))
    joined = call(
        join_kernel,
        (qkv_rows, outw_part),
        (struct((width // blocks, 4 * share), bf16),) * 4,
        [
            pltpu.VMEM((images, width // blocks, 4 * share), bf16),
            pltpu.SemaphoreType.DMA((4,)),
        ],
        where,
        "join",
        out_specs={index: ANY for index in range(4)},
    )
    way, j_mid = line_first(joined)
    other, way, j_mid = tie(other, way, j_mid)
    j_other, j_two, j_near = line_second(joined, way)
    send_gateup, first, second = call(
        turn_kernel,
        (shares[0], mid, near, two, other),
        (
            struct((blocks, width // blocks, run), bf16),
            struct((share, run), bf16),
            struct((share, run), bf16),
        ),
        scalars=where,
        name="turn",
    )
    modw_total, modb_total, qgain_total, kgain_total, act_send, condition, buckets = call(
        tail_kernel,
        (everywhere, table_share, modw_share),
        (
            struct((share, columns)),
            struct((columns,)),
            struct((HD,)),
            struct((HD,)),
            struct((blocks, 8, share)),
            struct((8, share)),
            struct((8, LANES)),
        ),
        [pltpu.VMEM((8, columns), jnp.float32), pltpu.VMEM((8, share), jnp.float32)],
        name="tail",
    )
    act_parts = exchange(act_send)
    act_parts, send_gateup = tie(act_parts, send_gateup)
    gateup_rows = exchange(send_gateup)
    first = lax.ppermute(first, PLANE, [(t, t // 2 + 4 * (t % 2)) for t in range(8)])
    second = lax.ppermute(second, PLANE, [(t, t // 2 + 4 * (1 - t % 2)) for t in range(8)])
    (table_total,) = call(
        table_kernel,
        (act_parts, condition, buckets),
        (struct((cond_table.shape[0] // blocks, share)),),
        scalars=where,
        name="table",
    )
    gateup_rows, table_total, j_other = tie(gateup_rows, table_total, j_other)
    gateup_total, down_total, qkv_total, outw_total = call(
        lay_kernel,
        (gateup_rows, first, second, joined[0], j_mid, j_near, j_two, j_other),
        (
            struct((width // blocks, blocks * run)),
            struct((share, units)),
            struct((width // blocks, 3 * share)),
            struct((width // blocks, share)),
        ),
        scalars=where,
        name="lay",
    )
    return (
        output.reshape(block_in.shape),
        in_grad.reshape(block_in.shape),
        table_total,
        modw_total,
        modb_total,
        qkv_total,
        qgain_total,
        kgain_total,
        outw_total,
        gateup_total,
        down_total.T,
    )


def solution(mesh):
    sizes = mesh.shape
    fits = sizes["ty"] == 4 and sizes["tx"] == 2 and sizes["img"] == 4
    return jax.shard_map(
        functools.partial(on_plane, sizes["img"]) if fits else on_device,
        mesh=mesh,
        in_specs=(
            P("img", "ty", "tx", None),
            P("img"),
            P("img", "ty", "tx", None),
            P(),
            P(None, ("ty", "tx")),
            P(("ty", "tx")),
            P(),
            P(),
            P(),
            P(),
            P(),
            P(),
            P("img", "ty", "tx", None),
        ),
        out_specs=(
            P("img", "ty", "tx", None),
            P("img", "ty", "tx", None),
            P(("ty", "tx"), "img"),
            P("img", ("ty", "tx")),
            P(("ty", "tx")),
            P(("ty", "tx"), "img"),
            P(),
            P(),
            P(("ty", "tx"), "img"),
            P(("ty", "tx"), "img"),
            P(("ty", "tx"), "img"),
        ),
        check_vma=False,
    )
```

```python
import functools
import math

import jax
import jax.numpy as jnp
from jax import lax
from jax.experimental import pallas as pl
from jax.experimental.pallas import tpu as pltpu
from jax.sharding import PartitionSpec as P

HEADS = 16
HD = 72


EPS = 1e-06
PRECISE = lax.Precision.HIGHEST


def normed(value):
    return value * lax.rsqrt(jnp.mean(value * value, axis=-1, keepdims=True) + EPS)


def norm_back(value, upstream):
    inverse = lax.rsqrt(jnp.mean(value * value, axis=-1, keepdims=True) + EPS)
    unit_value = value * inverse
    return inverse * (
        upstream - unit_value * jnp.mean(upstream * unit_value, axis=-1, keepdims=True)
    )


def rotate(value, tables, turning):
    row_cos, row_sin, col_cos, col_sin = tables
    quarter = value.shape[-1] // 4
    first = value[..., :quarter]
    second = value[..., quarter : 2 * quarter]
    third = value[..., 2 * quarter : 3 * quarter]
    fourth = value[..., 3 * quarter :]
    row_turn = turning * row_sin
    col_turn = turning * col_sin
    return jnp.concatenate(
        [
            first * row_cos - second * row_turn,
            second * row_cos + first * row_turn,
            third * col_cos - fourth * col_turn,
            fourth * col_cos + third * col_turn,
        ],
        axis=-1,
    )


def silu_slope(value):
    sigma = jax.nn.sigmoid(value)
    return sigma * (1.0 + value * (1.0 - sigma))


def product(left, right):
    return jnp.einsum("ik,kj->ij", left, right, preferred_element_type=jnp.float32)


def product_rt(left, right):
    return jnp.einsum("ik,jk->ij", left, right, preferred_element_type=jnp.float32)


def product_lt(left, right):
    return jnp.einsum("ki,kj->ij", left, right, preferred_element_type=jnp.float32)


def on_device(
    block_in,
    bucket,
    tile_anchor,
    cond_table,
    mod_weight,
    mod_bias,
    qkv_weight,
    query_gain,
    key_gain,
    out_weight,
    gate_up_weight,
    down_weight,
    cotangent,
):
    images, tile_rows, tile_cols, model_width = block_in.shape
    tokens = tile_rows * tile_cols
    all_rows = images * tokens
    head_count = HEADS
    head_size = HD
    score_scale = head_size ** (-0.5)
    hidden_units = down_weight.shape[0]
    onehot = (bucket[:, None] == jnp.arange(cond_table.shape[0], dtype=jnp.int32)[None, :]).astype(
        jnp.float32
    )
    condition = jnp.dot(onehot, cond_table, precision=PRECISE)
    cond_act = jax.nn.silu(condition).astype(jnp.bfloat16)
    mod_part = product(cond_act, mod_weight) + mod_bias[None, :]
    modulation = lax.all_gather(mod_part, ("ty", "tx"), axis=1, tiled=True)
    pieces = [
        modulation[:, None, index * model_width : (index + 1) * model_width] for index in range(6)
    ]
    shift_in, scale_in, gate_in, shift_mid, scale_mid, gate_mid = pieces
    places = jnp.arange(tokens, dtype=jnp.int32)
    row_pos = (tile_anchor[:, 0, 0, 0][:, None] + places[None, :] // tile_cols).astype(jnp.float32)
    col_pos = (tile_anchor[:, 0, 0, 1][:, None] + places[None, :] % tile_cols).astype(jnp.float32)
    quarter = head_size // 4
    frequency = jnp.exp(-math.log(10000.0) * jnp.arange(quarter, dtype=jnp.float32) / quarter)
    row_angle = row_pos[:, :, None, None] * frequency
    col_angle = col_pos[:, :, None, None] * frequency
    tables = (jnp.cos(row_angle), jnp.sin(row_angle), jnp.cos(col_angle), jnp.sin(col_angle))
    inputs = block_in.reshape(images, tokens, model_width)
    normed_in = normed(inputs)
    hidden_in = (
        (normed_in * (1.0 + scale_in) + shift_in)
        .astype(jnp.bfloat16)
        .reshape(all_rows, model_width)
    )
    qkv = product(hidden_in, qkv_weight).reshape(images, tokens, 3 * model_width)
    query_raw = qkv[..., :model_width].reshape(images, tokens, head_count, head_size)
    key_raw = qkv[..., model_width : 2 * model_width].reshape(images, tokens, head_count, head_size)
    query_unit = normed(query_raw)
    key_unit = normed(key_raw)
    query_low = rotate(query_unit * query_gain, tables, 1.0).astype(jnp.bfloat16)
    key_low = rotate(key_unit * key_gain, tables, 1.0).astype(jnp.bfloat16)
    value_low = qkv[..., 2 * model_width :].astype(jnp.bfloat16)
    keys_all, values_all = (
        lax.all_gather(
            key_low.reshape(images, tokens, model_width), ("ty", "tx"), axis=1, tiled=True
        ),
        lax.all_gather(value_low, ("ty", "tx"), axis=1, tiled=True),
    )
    key_heads = keys_all.reshape(images, -1, head_count, head_size)
    value_heads = values_all.reshape(images, -1, head_count, head_size)

    def attend(items):
        query_img, key_img, value_img = items
        scores = (
            jnp.einsum("qhd,khd->hqk", query_img, key_img, preferred_element_type=jnp.float32)
            * score_scale
        )
        row_max = jnp.max(scores, axis=-1, keepdims=True)
        expo = jnp.exp(scores - row_max)
        row_sum = jnp.sum(expo, axis=-1, keepdims=True)
        mixed = jnp.einsum(
            "hqk,khd->qhd",
            (expo / row_sum).astype(jnp.bfloat16),
            value_img,
            preferred_element_type=jnp.float32,
        )
        return (mixed, (row_max + jnp.log(row_sum))[:, :, 0])

    mixed_full, log_total = lax.map(attend, (query_low, key_heads, value_heads))
    attended = mixed_full.reshape(all_rows, model_width).astype(jnp.bfloat16)
    attn_out = product(attended, out_weight).reshape(images, tokens, model_width)
    middle = inputs + gate_in * attn_out
    normed_mid = normed(middle)
    hidden_mid = (
        (normed_mid * (1.0 + scale_mid) + shift_mid)
        .astype(jnp.bfloat16)
        .reshape(all_rows, model_width)
    )

    def feed(hidden_value):
        gate_up = product(hidden_value, gate_up_weight)
        return (gate_up[:, :hidden_units], gate_up[:, hidden_units:])

    gate_pre, up_pre = feed(hidden_mid)
    activ = (jax.nn.silu(gate_pre) * up_pre).astype(jnp.bfloat16)
    mlp_out = product(activ, down_weight).reshape(images, tokens, model_width)
    output = middle + gate_mid * mlp_out
    upstream = cotangent.reshape(images, tokens, model_width)
    gmid_grad = jnp.sum(upstream * mlp_out, axis=1)
    mlp_grad = (gate_mid * upstream).astype(jnp.bfloat16).reshape(all_rows, model_width)
    down_grad = product_lt(activ, mlp_grad)
    activ_grad = product_rt(mlp_grad, down_weight)
    gate_pre, up_pre = feed(hidden_mid)
    gu_grad = jnp.concatenate(
        [activ_grad * up_pre * silu_slope(gate_pre), activ_grad * jax.nn.silu(gate_pre)], axis=1
    ).astype(jnp.bfloat16)
    gateup_grad = product_lt(hidden_mid, gu_grad)
    mid_grad = product_rt(gu_grad, gate_up_weight).reshape(images, tokens, model_width)
    smid_grad = jnp.sum(mid_grad, axis=1)
    cmid_grad = jnp.sum(mid_grad * normed_mid, axis=1)
    middle_grad = upstream + norm_back(middle, mid_grad * (1.0 + scale_mid))
    gin_grad = jnp.sum(middle_grad * attn_out, axis=1)
    attn_grad = (gate_in * middle_grad).astype(jnp.bfloat16).reshape(all_rows, model_width)
    outw_grad = product_lt(attended, attn_grad)
    attended_grad = (
        product_rt(attn_grad, out_weight)
        .astype(jnp.bfloat16)
        .reshape(images, tokens, head_count, head_size)
    )
    row_delta = jnp.swapaxes(jnp.sum(attended_grad.astype(jnp.float32) * mixed_full, axis=-1), 1, 2)

    def score_parts(query_img, key_img, value_img, grad_img, total_img, delta_img):
        scores = (
            jnp.einsum("qhd,khd->hqk", query_img, key_img, preferred_element_type=jnp.float32)
            * score_scale
        )
        probs = jnp.exp(scores - total_img[:, :, None])
        prob_grad = jnp.einsum(
            "qhd,khd->hqk", grad_img, value_img, preferred_element_type=jnp.float32
        )
        score_grad = (probs * (prob_grad - delta_img[:, :, None])).astype(jnp.bfloat16)
        return (probs.astype(jnp.bfloat16), score_grad)

    def grads_all(items):
        query_img, key_img, value_img, grad_img, total_img, delta_img = items
        probs_low, score_grad = score_parts(
            query_img, key_img, value_img, grad_img, total_img, delta_img
        )
        query_part = (
            jnp.einsum("hqk,khd->qhd", score_grad, key_img, preferred_element_type=jnp.float32)
            * score_scale
        )
        key_part = (
            jnp.einsum("hqk,qhd->khd", score_grad, query_img, preferred_element_type=jnp.float32)
            * score_scale
        )
        value_part = jnp.einsum(
            "hqk,qhd->khd", probs_low, grad_img, preferred_element_type=jnp.float32
        )
        return (query_part, key_part.reshape(-1, model_width), value_part.reshape(-1, model_width))

    query_grad, key_full, value_full = lax.map(
        grads_all, (query_low, key_heads, value_heads, attended_grad, log_total, row_delta)
    )
    key_grad, value_grad = (
        lax.psum_scatter(
            key_full.astype(jnp.bfloat16), ("ty", "tx"), scatter_dimension=1, tiled=True
        ).astype(jnp.float32),
        lax.psum_scatter(
            value_full.astype(jnp.bfloat16), ("ty", "tx"), scatter_dimension=1, tiled=True
        ).astype(jnp.float32),
    )
    query_turned = rotate(query_grad, tables, -1.0)
    key_turned = rotate(key_grad.reshape(images, tokens, head_count, head_size), tables, -1.0)
    qgain_part = jnp.sum(query_turned * query_unit, axis=(0, 1, 2))
    kgain_part = jnp.sum(key_turned * key_unit, axis=(0, 1, 2))
    query_back = norm_back(query_raw, query_turned * query_gain).reshape(
        images, tokens, model_width
    )
    key_back = norm_back(key_raw, key_turned * key_gain).reshape(images, tokens, model_width)
    qkv_back = jnp.concatenate([query_back, key_back, value_grad], axis=-1).astype(jnp.bfloat16)
    qkv_back = qkv_back.reshape(all_rows, 3 * model_width)
    qkv_part = product_lt(hidden_in, qkv_back)
    in_back = product_rt(qkv_back, qkv_weight).reshape(images, tokens, model_width)
    sin_grad = jnp.sum(in_back, axis=1)
    cin_grad = jnp.sum(in_back * normed_in, axis=1)
    in_grad = middle_grad + norm_back(inputs, in_back * (1.0 + scale_in))
    mod_grad = jnp.concatenate(
        [sin_grad, cin_grad, gin_grad, smid_grad, cmid_grad, gmid_grad], axis=1
    )
    mod_cols = lax.psum_scatter(mod_grad, ("ty", "tx"), scatter_dimension=1, tiled=True)
    modw_part = jnp.dot(cond_act.astype(jnp.float32).T, mod_cols, precision=PRECISE)
    modb_part = jnp.sum(mod_cols, axis=0)
    act_grad = jnp.dot(mod_cols, mod_weight.astype(jnp.float32).T, precision=PRECISE)
    cond_grad = act_grad * silu_slope(condition)
    table_part = jnp.dot(onehot.T, cond_grad, precision=PRECISE)
    qkv_share, outw_share, gateup_share, down_share, table_share = (
        lax.psum_scatter(
            qkv_part.astype(jnp.bfloat16), ("ty", "tx"), scatter_dimension=0, tiled=True
        ).astype(jnp.float32),
        lax.psum_scatter(
            outw_grad.astype(jnp.bfloat16), ("ty", "tx"), scatter_dimension=0, tiled=True
        ).astype(jnp.float32),
        lax.psum_scatter(
            gateup_grad.astype(jnp.bfloat16), ("ty", "tx"), scatter_dimension=0, tiled=True
        ).astype(jnp.float32),
        lax.psum_scatter(
            down_grad.astype(jnp.bfloat16), ("ty", "tx"), scatter_dimension=0, tiled=True
        ).astype(jnp.float32),
        lax.psum_scatter(
            table_part.astype(jnp.bfloat16), ("ty", "tx"), scatter_dimension=0, tiled=True
        ).astype(jnp.float32),
    )
    qkv_total, outw_total, gateup_total, down_total, table_total = (
        lax.psum_scatter(
            qkv_share.astype(jnp.bfloat16), "img", scatter_dimension=1, tiled=True
        ).astype(jnp.float32),
        lax.psum_scatter(
            outw_share.astype(jnp.bfloat16), "img", scatter_dimension=1, tiled=True
        ).astype(jnp.float32),
        lax.psum_scatter(
            gateup_share.astype(jnp.bfloat16), "img", scatter_dimension=1, tiled=True
        ).astype(jnp.float32),
        lax.psum_scatter(
            down_share.astype(jnp.bfloat16), "img", scatter_dimension=1, tiled=True
        ).astype(jnp.float32),
        lax.psum_scatter(
            table_share.astype(jnp.bfloat16), "img", scatter_dimension=1, tiled=True
        ).astype(jnp.float32),
    )
    modw_total = lax.psum_scatter(
        modw_part.astype(jnp.bfloat16), "img", scatter_dimension=0, tiled=True
    ).astype(jnp.float32)
    modb_total = lax.psum(modb_part, "img")
    qgain_total, kgain_total = lax.psum((qgain_part, kgain_part), ("img", "ty", "tx"))
    return (
        output.reshape(block_in.shape),
        in_grad.reshape(block_in.shape),
        table_total,
        modw_total,
        modb_total,
        qkv_total,
        qgain_total,
        kgain_total,
        outw_total,
        gateup_total,
        down_total,
    )


def sigmoid(value):
    return 1.0 / (1.0 + jnp.exp(-value))


def dot_nn(left, right):
    return lax.dot_general(
        left, right, (((1,), (0,)), ((), ())), preferred_element_type=jnp.float32
    )


def dot_nt(left, right):
    return lax.dot_general(
        left, right, (((1,), (1,)), ((), ())), preferred_element_type=jnp.float32
    )


def dot_tn(left, right):
    return lax.dot_general(
        left, right, (((0,), (0,)), ((), ())), preferred_element_type=jnp.float32
    )


def column_sum(value):
    return jnp.sum(value, axis=0, keepdims=True)


EXTRA = 16
LANES = 128
QUARTER = HD // 4
PLACES = ((0, 0), (QUARTER, LANES // 2), (2 * QUARTER, QUARTER), (3 * QUARTER, LANES // 2 + QUARTER))


def lane_entry(lane):
    low = lane % (LANES // 2)
    upper = lane // (LANES // 2)
    column = low // QUARTER
    entry = jnp.where(
        low < 2 * QUARTER, low % QUARTER + QUARTER * upper + 2 * QUARTER * column, -1
    )
    return entry, column == 1


def wide_row(row, ref, line):
    for source, target in PLACES:
        ref[line : line + 1, target : target + QUARTER] = row[:, source : source + QUARTER]


def open_kernel(
    bucket_ref, anchor_ref, x_ref, table_ref, weight_ref, bias_ref, cot_ref,
    pay_ref, low_ref, wide_ref,
):
    tokens, width = x_ref.shape
    columns = weight_ref.shape[0]
    x = x_ref[...]
    pay_ref[0:tokens, :] = normed(x).astype(jnp.bfloat16)
    low_ref[...] = cot_ref[...].astype(jnp.bfloat16)
    row = table_ref[pl.ds(bucket_ref[0], 1), :]
    act = (row * sigmoid(row)).astype(jnp.bfloat16)
    mod = dot_nt(jnp.broadcast_to(act, (8, width)), weight_ref[...])
    wide_ref[...] = jnp.zeros_like(wide_ref)
    wide_ref[:, 0:columns] = mod + bias_ref[...].reshape(1, columns)
    full = wide_ref[0:1, :]
    high = full.astype(jnp.bfloat16).astype(jnp.float32)
    rest = full - high
    middle = rest.astype(jnp.bfloat16).astype(jnp.float32)
    least = rest - middle
    lane = lax.broadcasted_iota(jnp.int32, (EXTRA, width), 1)
    line = lax.broadcasted_iota(jnp.int32, (EXTRA, width), 0)
    entry, column = lane_entry(lane % LANES)
    anchor = jnp.where(
        column, anchor_ref[1].astype(jnp.float32), anchor_ref[0].astype(jnp.float32)
    )
    anchor = jnp.where(entry >= 0, anchor, 0.0)
    extra = jnp.where(
        line == 0,
        high,
        jnp.where(
            line == 1, middle, jnp.where(line == 2, least, jnp.where(line == 3, anchor, 0.0))
        ),
    )
    pay_ref[tokens : tokens + EXTRA, :] = extra.astype(jnp.bfloat16)


def ready_kernel(blocks, tile_cols, scalars, *refs):
    qkv_parts, refs = refs[:6], refs[6:]
    (
        qgain_ref, kgain_ref, spread_ref, order_ref, turn_ref, gain_ref, window_ref, pick_ref,
    ) = refs
    mine = scalars[0]
    heads = HEADS // blocks
    span = heads * HD
    wide = 3 * heads * LANES
    for index, part in enumerate(qkv_parts):
        window_ref[:, LANES * index : LANES * (index + 1)] = part[...]
    lane = lax.broadcasted_iota(jnp.int32, (1, wide), 1)
    place = lane % LANES
    part = lane // LANES
    side = part // heads
    entry, _ = lane_entry(place)
    entry = jnp.where(side == 2, jnp.where(place < HD, place, -1), entry)
    local = HD * (part % heads) + entry
    source = jnp.where(entry >= 0, side * (2 * LANES) + mine * (span - LANES) + local, -1)
    row = lax.broadcasted_iota(jnp.int32, (wide, wide), 0)
    pick_ref[...] = (row == source).astype(jnp.float32).astype(jnp.bfloat16)
    spread_ref[...] = dot_nn(window_ref[...], pick_ref[...]).astype(jnp.bfloat16)
    source = jnp.where(entry >= 0, side * span + local, -1)
    row = lax.broadcasted_iota(jnp.int32, order_ref.shape, 0)
    order_ref[...] = (row == source).astype(jnp.float32).astype(jnp.bfloat16)
    tokens = turn_ref.shape[1]
    token = lax.broadcasted_iota(jnp.int32, (tokens, LANES), 0)
    entry, column = lane_entry(lax.broadcasted_iota(jnp.int32, (tokens, LANES), 1))
    rate = jnp.exp((entry % QUARTER).astype(jnp.float32) * (-math.log(10000.0) / QUARTER))
    rate = jnp.where(entry >= 0, rate, 0.0)
    offset = jnp.where(column, token % tile_cols, token // tile_cols).astype(jnp.float32) * rate
    turn_ref[0] = jnp.cos(offset)
    turn_ref[1] = jnp.sin(offset)
    turn_ref[2] = rate
    gain_ref[...] = jnp.zeros_like(gain_ref)
    wide_row(qgain_ref[...].reshape(1, HD), gain_ref, 0)
    wide_row(kgain_ref[...].reshape(1, HD), gain_ref, 1)


def layout_kernel(
    scalars, gate_a, gate_b, up_a, up_b, table_ref, modw_ref,
    gate_ref, up_ref, tshare_ref, mshare_ref,
):
    mine = scalars[0]
    share = tshare_ref.shape[1]
    for image in range(table_ref.shape[1] // share):

        @pl.when(scalars[1] == image)
        def _(image=image):
            tshare_ref[...] = table_ref[:, share * image : share * (image + 1)]
            mshare_ref[...] = modw_ref[:, share * image : share * (image + 1)]

    units = gate_ref.shape[1]
    run = units // 2
    for parity in range(2):

        @pl.when(mine % 2 == parity)
        def _(parity=parity):
            for source_a, source_b, target in ((gate_a, gate_b, gate_ref), (up_a, up_b, up_ref)):
                target[:, 0:run] = source_a[:, run * parity : run * (parity + 1)]
                target[:, run:units] = source_b[:, run * parity : run * (parity + 1)]


def unit_rate(raw):
    return lax.rsqrt(jnp.sum(raw * raw, axis=-1, keepdims=True) * (1.0 / HD) + EPS)


def block_copies(pieces, ref, place, tokens, sems):
    if len(pieces) == 8:
        plan = [(piece, index, tokens, 0) for index, piece in enumerate(pieces)]
    else:
        own, xn, core, cx, yn, d1, d2, cy, cd1, cd2 = pieces
        half = d1.shape[0]
        plan = [
            (own, 0, tokens, 0), (xn, 1, tokens, 0), (core, 2, tokens, 0), (cx, 3, tokens, 0),
            (yn, 4, tokens, 0), (d1, 5, half, 0), (d2, 5, tokens - half, half), (cy, 6, tokens, 0),
            (cd1, 7, half, 0), (cd2, 7, tokens - half, half),
        ]
    return [
        pltpu.make_async_copy(
            piece.at[pl.ds(0, rows), :],
            ref.at[pl.ds(place(index) + offset, rows), :],
            sems.at[number],
        )
        for number, (piece, index, rows, offset) in enumerate(plan)
    ]


def attend_kernel(blocks, scalars, *refs):
    pieces, refs = refs[:10], refs[10:]
    (
        spread_ref, offset_ref, gain_ref,
        att_ref, hid_any, qkv_any, unit_any, turn_any, mod_ref, log_ref, mixed_ref,
        all_ref, extra_ref, rows_ref, flat_ref, anchor_ref, vt_ref,
        hid_ref, qkv_ref, unit_ref, turn_ref, sems, extra_sems, out_sems,
    ) = refs
    mine = scalars[0]
    own, xn, core, cx, yn, d1, d2, cy, cd1, cd2 = pieces
    width = own.shape[1]
    tokens = own.shape[0] - EXTRA
    columns = 6 * width // blocks
    half = d1.shape[0]
    everyone = blocks * tokens
    heads = HEADS // blocks
    extras = [
        pltpu.make_async_copy(
            piece.at[pl.ds(piece.shape[0] - EXTRA, EXTRA), :],
            extra_ref.at[index],
            extra_sems.at[index],
        )
        for index, piece in enumerate((own, xn, core, cx, yn, d2, cy, cd2))
    ]
    copies = block_copies(
        pieces,
        all_ref,
        lambda index: pl.multiple_of((mine ^ index) * tokens, tokens),
        tokens,
        sems,
    )
    for copy in (*extras, *copies):
        copy.start()
    for copy in extras:
        copy.wait()
    for index in range(blocks):
        extra = extra_ref[index].astype(jnp.float32)
        place = mine ^ index
        rows_ref[pl.ds(place, 1), :] = extra[0:1] + extra[1:2] + extra[2:3]
        anchor_ref[0, pl.ds(place, 1), :] = extra[3:4, 0:LANES]
    for index in range(blocks):
        flat_ref[0:1, columns * index : columns * (index + 1)] = rows_ref[
            index : index + 1, 0:columns
        ]
    mod_ref[...] = jnp.zeros_like(mod_ref)
    for index in range(6):
        mod_ref[index : index + 1, :] = flat_ref[0:1, width * index : width * (index + 1)]
    shift_in = mod_ref[0:1, :]
    scale_in = 1.0 + mod_ref[1:2, :]
    anchor = anchor_ref[0] * offset_ref[2, 0:blocks, :]
    anchor_ref[0] = jnp.cos(anchor)
    anchor_ref[1] = jnp.sin(anchor)
    lane = lax.broadcasted_iota(jnp.int32, (tokens, LANES), 1)
    sign = jnp.where(lane < LANES // 2, -1.0, 1.0)
    offset_cos, offset_sin = offset_ref[0], offset_ref[1]
    query_gain, key_gain = gain_ref[0:1, :], gain_ref[1:2, :]
    scale = HD ** (-0.5) * math.log2(math.e)
    for copy in copies:
        copy.wait()

    def project(index, carry):
        rows = pl.ds(pl.multiple_of(index * tokens, tokens), tokens)
        hidden = (all_ref[rows, :].astype(jnp.float32) * scale_in + shift_in).astype(jnp.bfloat16)
        hid_ref[rows, :] = hidden
        anchor_cos = anchor_ref[0, pl.ds(index, 1), :]
        anchor_sin = anchor_ref[1, pl.ds(index, 1), :]
        turn_cos = anchor_cos * offset_cos - anchor_sin * offset_sin
        turn_sin = (anchor_sin * offset_cos + anchor_cos * offset_sin) * sign
        turn_ref[0, rows, :] = turn_cos
        turn_ref[1, rows, :] = turn_sin
        product = dot_nn(hidden, spread_ref[...])
        for part in range(2 * heads):
            raw = product[:, LANES * part : LANES * (part + 1)]
            gain = query_gain * scale if part < heads else key_gain
            rate = unit_rate(raw)
            unit = raw * rate
            unit_ref[part, rows, :] = jnp.where(lane < LANES - 1, unit, rate)
            unit = unit * gain
            turned = unit * turn_cos + pltpu.roll(unit, LANES // 2, 1) * turn_sin
            qkv_ref[part, rows, :] = turned.astype(jnp.bfloat16)
        for part in range(2 * heads, 3 * heads):
            qkv_ref[part, rows, :] = product[:, LANES * part : LANES * (part + 1)].astype(
                jnp.bfloat16
            )
        return carry

    lax.fori_loop(0, blocks, project, 0, unroll=2)
    leaving = [
        pltpu.make_async_copy(source, target, out_sems.at[index])
        for index, (source, target) in enumerate(
            ((qkv_ref, qkv_any), (unit_ref, unit_any), (hid_ref, hid_any), (turn_ref, turn_any))
        )
    ]
    for copy in leaving:
        copy.start()
    chunk = 2 * tokens
    for head in range(heads):
        vt_ref[head] = qkv_ref[2 * heads + head].T

    def attend(index, carry):
        rows = pl.ds(pl.multiple_of(index * chunk, chunk), chunk)
        for head in range(heads):
            scores = dot_nt(qkv_ref[heads + head], qkv_ref[head, rows, :])
            expo = jnp.exp2(scores)
            total = column_sum(expo)
            mixed = dot_nn(vt_ref[head], expo.astype(jnp.bfloat16)) * (1.0 / total)
            log_ref[head, pl.ds(index, 1), :] = jnp.log2(total)
            mixed_ref[head, :, rows] = mixed
            for block in range(chunk // tokens):
                att_ref[index * (chunk // tokens) + block, HD * head : HD * (head + 1), :] = mixed[
                    0:HD, tokens * block : tokens * (block + 1)
                ].astype(jnp.bfloat16)
        return carry

    lax.fori_loop(0, everyone // chunk, attend, 0, unroll=2)
    for copy in leaving:
        copy.wait()


def middle_kernel(att_ref, weight_ref, x_ref, mod_ref, out_ref, mid_ref, hid_ref):
    attended = att_ref[...].reshape(weight_ref.shape[0], att_ref.shape[2])
    attn_out = dot_tn(attended, weight_ref[...])
    out_ref[...] = attn_out
    middle = x_ref[...] + mod_ref[2:3, :] * attn_out
    mid_ref[...] = middle
    hid_ref[...] = (normed(middle) * (1.0 + mod_ref[4:5, :]) + mod_ref[3:4, :]).astype(
        jnp.bfloat16
    )


def act_grad_kernel(down_ref, cot_ref, mod_ref, out_ref, low_ref):
    @pl.when(pl.program_id(0) == 0)
    def _():
        low_ref[...] = (mod_ref[5:6, :] * cot_ref[...]).astype(jnp.bfloat16)

    out_ref[...] = dot_nt(low_ref[...], down_ref[...])


def mlp_step(gate_ref, up_ref, hid_ref, agrad_ref, act_ref):
    hidden = hid_ref[...]
    gate = dot_nn(hidden, gate_ref[...])
    up = dot_nn(hidden, up_ref[...])
    sigma = sigmoid(gate)
    silu = gate * sigma
    act_ref[...] = (silu * up).astype(jnp.bfloat16)
    act_grad = agrad_ref[...]
    slope = sigma * (1.0 + gate * (1.0 - sigma))
    gate_grad = (act_grad * up * slope).astype(jnp.bfloat16)
    up_grad = (act_grad * silu).astype(jnp.bfloat16)
    return dot_nt(gate_grad, gate_ref[...]) + dot_nt(up_grad, up_ref[...])


def mlp_first_kernel(gate_ref, up_ref, hid_ref, agrad_ref, act_ref, back_ref):
    part = mlp_step(gate_ref, up_ref, hid_ref, agrad_ref, act_ref)

    @pl.when(pl.program_id(0) == 0)
    def _():
        back_ref[...] = part

    @pl.when(pl.program_id(0) > 0)
    def _():
        back_ref[...] += part


def mlp_kernel(
    gate_ref, up_ref, outw_ref, hid_ref, mid_ref, attn_ref, cot_ref, agrad_in, mod_ref, start_ref,
    act_ref, mgrad_ref, agrad_ref, dgrad_ref, sums_ref, back_ref,
):
    step = pl.program_id(0)
    part = mlp_step(gate_ref, up_ref, hid_ref, agrad_in, act_ref)

    @pl.when(step == 0)
    def _():
        back_ref[...] = start_ref[...] + part

    @pl.when(step > 0)
    def _():
        back_ref[...] += part

    @pl.when(step == pl.num_programs(0) - 1)
    def _():
        middle = mid_ref[...]
        upstream = cot_ref[...]
        back = back_ref[...]
        inverse = lax.rsqrt(jnp.mean(middle * middle, axis=-1, keepdims=True) + EPS)
        unit = middle * inverse
        lifted = back * (1.0 + mod_ref[4:5, :])
        middle_grad = upstream + inverse * (
            lifted - unit * jnp.mean(lifted * unit, axis=-1, keepdims=True)
        )
        mgrad_ref[...] = middle_grad
        attn_grad = (mod_ref[2:3, :] * middle_grad).astype(jnp.bfloat16)
        agrad_ref[...] = attn_grad
        attended = dot_nt(outw_ref[...], attn_grad).astype(jnp.bfloat16)
        dgrad_ref[...] = attended.reshape(dgrad_ref.shape)
        sums_ref[...] = jnp.zeros_like(sums_ref)
        sums_ref[2:3, :] = column_sum(middle_grad * attn_ref[...])
        sums_ref[3:4, :] = column_sum(back)
        sums_ref[4:5, :] = column_sum(back * unit)


def mlp_out_kernel(
    first_ref, second_ref, low_ref, high_ref, mid_ref, cot_ref, mod_ref, sums_ref, insum_ref,
    gsum_ref, bucket_ref, output_ref, send_ref, acc_ref, flat_ref, row_ref,
):
    step = pl.program_id(0)
    blocks = row_ref.shape[0]
    width = mid_ref.shape[1]
    columns = 6 * width // blocks
    part = dot_nn(first_ref[...], low_ref[...]) + dot_nn(second_ref[...], high_ref[...])

    @pl.when(step == 0)
    def _():
        acc_ref[...] = part

    @pl.when(step > 0)
    def _():
        acc_ref[...] += part

    @pl.when(step == pl.num_programs(0) - 1)
    def _():
        output_ref[...] = mid_ref[...] + mod_ref[5:6, :] * acc_ref[...]
        for index in range(2):
            flat_ref[0:1, width * index : width * (index + 1)] = insum_ref[index : index + 1, :]
        for index in range(2, 5):
            flat_ref[0:1, width * index : width * (index + 1)] = sums_ref[index : index + 1, :]
        flat_ref[0:1, width * 5 : width * 6] = column_sum(cot_ref[...] * acc_ref[...])
        row_ref[...] = jnp.zeros_like(row_ref)
        for index in range(blocks):
            row_ref[index : index + 1, 0:columns] = flat_ref[
                0:1, columns * index : columns * (index + 1)
            ]
        row_ref[:, columns : columns + 1] = jnp.broadcast_to(
            bucket_ref[0].astype(jnp.float32), (blocks, 1)
        )
        for line in range(2):
            for source, target in PLACES:
                start = columns + 16 + HD * line + source
                row_ref[:, start : start + QUARTER] = jnp.broadcast_to(
                    gsum_ref[line : line + 1, target : target + QUARTER], (blocks, QUARTER)
                )
        for index in range(blocks):
            tile = jnp.concatenate(
                [
                    row_ref[index : index + 1, LANES * part : LANES * (part + 1)]
                    for part in range(8)
                ],
                axis=0,
            )
            for image in range(send_ref.shape[0] // blocks):
                send_ref[blocks * image + index] = tile


def mlp_weights_kernel(scalars, *refs):
    hid_pieces, cot_pieces, refs = refs[:8], refs[8:16], refs[16:]
    (
        gate_ref, up_ref, down_a, down_b, mod_ref, own_ref, near_ref, two_ref, far_ref,
        all_ref, low_ref, act_ref, down_ref, out_ref, sems, out_sems,
    ) = refs
    tokens, width = hid_pieces[0].shape
    everyone = all_ref.shape[0]
    run = down_a.shape[0]
    units = 2 * run
    copies = [
        *block_copies(hid_pieces, all_ref, lambda index: index * tokens, tokens, sems.at[0]),
        *block_copies(cot_pieces, low_ref, lambda index: index * tokens, tokens, sems.at[1]),
    ]
    for copy in copies:
        copy.start()
    down_ref[0:run, :] = down_a[...]
    down_ref[run:units, :] = down_b[...]
    gate_mid = mod_ref[5:6, :]
    chunk = everyone // 2
    early = [copies[index] for index in (0, 1, 2, 3, 8, 9, 10, 11)]
    late = [copies[index] for index in (4, 5, 6, 7, 12, 13, 14, 15)]
    for copy in early:
        copy.wait()

    def chunked(index, carry):
        @pl.when(index == 1)
        def _():
            for copy in late:
                copy.wait()

        span = pl.ds(pl.multiple_of(index * chunk, chunk), chunk)
        low = (low_ref[span, :].astype(jnp.float32) * gate_mid).astype(jnp.bfloat16)
        low_ref[span, :] = low
        hidden = all_ref[span, :]
        gate = dot_nn(hidden, gate_ref[...])
        up = dot_nn(hidden, up_ref[...])
        act_grad = dot_nt(low, down_ref[...])
        sigma = sigmoid(gate)
        silu = gate * sigma
        slope = sigma * (1.0 + gate * (1.0 - sigma))
        act_ref[0, span, :] = (silu * up).astype(jnp.bfloat16)
        act_ref[1, span, :] = (act_grad * up * slope).astype(jnp.bfloat16)
        act_ref[2, span, :] = (act_grad * silu).astype(jnp.bfloat16)
        return carry

    lax.fori_loop(0, everyone // chunk, chunked, 0)
    lanes = width // units
    for side in range(2):
        grad = dot_tn(act_ref[1 + side], all_ref[...]).astype(jnp.bfloat16)
        for part in range(2):
            for index in range(lanes):
                out_ref[2 * side + part, run * index : run * (index + 1), :] = grad[
                    run * part : run * (part + 1), units * index : units * (index + 1)
                ]
    down = dot_tn(act_ref[0], low_ref[...]).astype(jnp.bfloat16).T
    share = width // out_ref.shape[0]
    for image in range(out_ref.shape[0]):
        out_ref[image, run * lanes : run * lanes + share, :] = down[
            share * image : share * (image + 1), :
        ]
    deal(out_ref, scalars[1], (own_ref, near_ref, two_ref, far_ref), out_sems)


def deal(ref, place, targets, sems):
    owners = [place ^ bits for bits in range(4)]
    copies = [
        pltpu.make_async_copy(ref.at[owner], target, sems.at[index])
        for index, (owner, target) in enumerate(zip(owners, targets, strict=True))
    ]
    for copy in copies:
        copy.start()
    for copy in copies:
        copy.wait()


def summed(refs, rows):
    total = refs[0][rows, :].astype(jnp.float32)
    for ref in refs[1:]:
        total = total + ref[rows, :].astype(jnp.float32)
    return total


def turn_kernel(scalars, *refs):
    parts, refs = refs[:5], refs[5:]
    send_ref, first_ref, second_ref = refs
    blocks, rows, run = send_ref.shape
    units = parts[0].shape[1]
    lanes = rows * blocks // units
    whole = jnp.concatenate(
        [summed(parts, pl.ds(run * index, run)).T for index in range(lanes)], axis=0
    )
    send_ref[...] = whole.astype(jnp.bfloat16).reshape(send_ref.shape)
    down = summed(parts, pl.ds(run * lanes, first_ref.shape[0])).astype(jnp.bfloat16)
    even = scalars[0] % 2 == 0
    for parity in range(2):

        @pl.when(scalars[0] % 2 == parity)
        def _(parity=parity):
            first_ref[...] = down[:, run * parity : run * (parity + 1)]
            second_ref[...] = down[:, run * (1 - parity) : run * (2 - parity)]


def lay_kernel(scalars, got_ref, first_ref, second_ref, *refs):
    parts, (gateup_ref, down_ref, qkv_ref, out_ref) = refs[:5], refs[5:]
    gateup_ref[...] = jnp.concatenate(
        [got_ref[index].astype(jnp.float32) for index in range(got_ref.shape[0])], axis=1
    )
    first = first_ref[...].astype(jnp.float32)
    second = second_ref[...].astype(jnp.float32)
    half = got_ref.shape[0] // 2

    @pl.when(scalars[0] < half)
    def _():
        down_ref[...] = jnp.concatenate([first, second], axis=1)

    @pl.when(scalars[0] >= half)
    def _():
        down_ref[...] = jnp.concatenate([second, first], axis=1)

    total = summed(parts, pl.ds(0, qkv_ref.shape[0]))
    columns = qkv_ref.shape[1]
    qkv_ref[...] = total[:, 0:columns]
    out_ref[...] = total[:, columns:]


def dot_exact(left, right, dims):
    total = None
    for _ in range(3):
        part = left.astype(jnp.bfloat16)
        left = left - part.astype(jnp.float32)
        product = lax.dot_general(
            part, right, (dims, ((), ())), preferred_element_type=jnp.float32
        )
        total = product if total is None else total + product
    return total


def tail_kernel(
    got_ref, table_ref, weight_ref,
    modw_ref, modb_ref, qgain_ref, kgain_ref, send_ref, cond_ref, bucket_ref,
    cols_ref, act_ref,
):
    columns = modb_ref.shape[0]
    blocks = send_ref.shape[0]
    images = got_ref.shape[0] // blocks
    lines = table_ref.shape[0]
    cols_ref[...] = jnp.zeros_like(cols_ref)
    act_ref[...] = jnp.zeros_like(act_ref)
    bucket_ref[...] = jnp.full(bucket_ref.shape, -1.0, jnp.float32)
    cond_ref[...] = jnp.zeros_like(cond_ref)
    gains = None
    line = lax.broadcasted_iota(jnp.int32, (lines, 1), 0).astype(jnp.float32)
    for image in range(images):
        total = got_ref[blocks * image]
        for index in range(1, blocks):
            total = total + got_ref[blocks * image + index]
        row = jnp.concatenate([total[index : index + 1, :] for index in range(8)], axis=1)
        cols_ref[image : image + 1, :] = row[:, 0:columns]
        gains = row if gains is None else gains + row
        first = got_ref[blocks * image]
        place = columns // LANES
        bucket = first[place : place + 1, columns % LANES : columns % LANES + 1]
        bucket_ref[image : image + 1, :] = jnp.broadcast_to(bucket, (1, LANES))
        cond = jnp.sum(
            jnp.where(line == bucket, table_ref[...], 0.0), axis=0, keepdims=True
        )
        cond_ref[image : image + 1, :] = cond
        act_ref[image : image + 1, :] = (
            (cond * sigmoid(cond)).astype(jnp.bfloat16).astype(jnp.float32)
        )
    cols = cols_ref[...]
    modw_ref[...] = lax.dot_general(
        act_ref[...], cols, (((0,), (0,)), ((), ())),
        precision=PRECISE, preferred_element_type=jnp.float32,
    )
    modb_ref[...] = column_sum(cols).reshape(columns)
    start = columns + 16
    qgain_ref[...] = gains[:, start : start + HD].reshape(HD)
    kgain_ref[...] = gains[:, start + HD : start + 2 * HD].reshape(HD)
    part = dot_exact(cols, weight_ref[...], ((1,), (0,)))
    send_ref[...] = jnp.broadcast_to(part[None], send_ref.shape)


def table_kernel(scalars, got_ref, cond_ref, bucket_ref, out_ref):
    total = jnp.sum(got_ref[...], axis=0)
    cond = cond_ref[...]
    sigma = sigmoid(cond)
    grad = total * (sigma * (1.0 + cond * (1.0 - sigma)))
    lines = out_ref.shape[0]
    line = lax.broadcasted_iota(jnp.int32, (lines, 1), 0) + scalars[0] * lines
    out = jnp.zeros(out_ref.shape, jnp.float32)
    for image in range(4):
        hot = line.astype(jnp.float32) == bucket_ref[image : image + 1, 0:1]
        out = out + jnp.where(hot, grad[image : image + 1, :], 0.0)
    out_ref[...] = out


def attend_back_kernel(
    attg_ref, qkv_ref, log_ref, mixed_ref, gain_ref, unit_any, turn_any, order_any,
    back_ref, gsum_ref, kt_ref, up_ref, upt_ref, grad_ref, unit_ref, turn_ref, order_ref, sems,
):
    blocks, _, tokens = attg_ref.shape
    heads = HEADS // blocks
    everyone = blocks * tokens
    lines, chunk = log_ref.shape[1:]
    scale = HD ** (-0.5)
    late = [
        pltpu.make_async_copy(source, target, sems.at[index])
        for index, (source, target) in enumerate(
            ((unit_any, unit_ref), (turn_any, turn_ref), (order_any, order_ref))
        )
    ]
    for copy in late:
        copy.start()
    query_gain, key_gain = gain_ref[0:1, :], gain_ref[1:2, :]
    for head in range(heads):
        kt_ref[head] = qkv_ref[heads + head].T
        grad_ref[heads + head] = jnp.zeros((everyone, LANES), jnp.float32)
        grad_ref[2 * heads + head] = jnp.zeros((everyone, LANES), jnp.float32)
        for block in range(blocks):
            piece = jnp.concatenate(
                [
                    attg_ref[block, HD * head : HD * (head + 1), :],
                    jnp.zeros((LANES - HD, tokens), jnp.bfloat16),
                ],
                axis=0,
            )
            upt_ref[head, :, tokens * block : tokens * (block + 1)] = piece
        up_ref[head] = upt_ref[head].T

    def attend(index, carry):
        rows = pl.ds(pl.multiple_of(index * chunk, chunk), chunk)
        for head in range(heads):
            query = qkv_ref[head, rows, :]
            upstream = up_ref[head, rows, :]
            turned = upt_ref[head, :, rows]
            delta = column_sum(turned.astype(jnp.float32) * mixed_ref[head, :, rows])
            probs = jnp.exp2(
                dot_nt(qkv_ref[heads + head], query) - log_ref[head, pl.ds(index, 1), :]
            )
            score_grad = (probs * (dot_nn(qkv_ref[2 * heads + head], turned) - delta)).astype(
                jnp.bfloat16
            )
            grad_ref[2 * heads + head] += dot_nn(probs.astype(jnp.bfloat16), upstream)
            grad_ref[heads + head] += dot_nn(score_grad, query)
            grad_ref[head, rows, :] = dot_nn(kt_ref[head], score_grad).T
        return carry

    lax.fori_loop(0, lines, attend, 0, unroll=2)
    gsum_ref[...] = jnp.zeros_like(gsum_ref)
    step = tokens
    for copy in late:
        copy.wait()

    def finish(index, carry):
        rows = pl.ds(pl.multiple_of(index * step, step), step)
        turn_cos = turn_ref[0, rows, :]
        turn_sin = turn_ref[1, rows, :]
        parts = []
        for part in range(2 * heads):
            gain = query_gain if part < heads else key_gain
            grad = grad_ref[part, rows, :] * (scale if part < heads else math.log(2.0))
            turned = grad * turn_cos - pltpu.roll(grad, LANES // 2, 1) * turn_sin
            unit = unit_ref[part, rows, :]
            rate = unit[:, LANES - 1 : LANES]
            line = 0 if part < heads else 1
            product = turned * unit
            gsum_ref[line : line + 1, :] += column_sum(product)
            mean = jnp.sum(product * gain, axis=-1, keepdims=True) * (1.0 / HD)
            parts.append((rate * (turned * gain - unit * mean)).astype(jnp.bfloat16))
        for part in range(2 * heads, 3 * heads):
            parts.append(grad_ref[part, rows, :].astype(jnp.bfloat16))
        back_ref[index] = dot_nt(order_ref[...], jnp.concatenate(parts, axis=1)).astype(
            jnp.bfloat16
        )
        return carry

    lax.fori_loop(0, everyone // step, finish, 0, unroll=2)


def qkv_weights_kernel(hid_ref, back_ref, grad_ref):
    blocks = back_ref.shape[0]
    back = jnp.concatenate([back_ref[index] for index in range(blocks)], axis=1)
    grad = dot_nn(back, hid_ref[...]).astype(jnp.bfloat16).T
    columns = grad.shape[1]
    grad_ref[:, :, LANES * (columns // LANES) :] = jnp.zeros(
        (*grad_ref.shape[:2], grad_ref.shape[2] - LANES * (columns // LANES)), jnp.bfloat16
    )
    grad_ref[:, :, 0:columns] = grad.reshape(*grad_ref.shape[:2], columns)


def out_weights_kernel(images, scalars, *refs):
    pieces, refs = refs[:8], refs[8:]
    att_ref, ograd_ref, low_ref, sems = refs
    tokens, width = pieces[0].shape
    mine = scalars[0]
    copies = block_copies(
        pieces,
        low_ref,
        lambda index: pl.multiple_of((mine ^ index) * tokens, tokens),
        tokens,
        sems,
    )
    for copy in copies:
        copy.start()
    for copy in copies:
        copy.wait()
    attended = jnp.concatenate([att_ref[index] for index in range(att_ref.shape[0])], axis=1)
    outw = dot_nn(attended, low_ref[...]).astype(jnp.bfloat16)
    share = width // images
    for image in range(images):
        ograd_ref[image] = outw[:, share * image : share * (image + 1)]


def join_kernel(scalars, grad_ref, ograd_ref, *refs):
    targets, (out_ref, sems) = refs[:4], refs[4:]
    images = out_ref.shape[0]
    blocks = grad_ref.shape[0]
    span = HD * HEADS // blocks
    whole = jnp.concatenate(
        [
            grad_ref[index][:, span * side : span * (side + 1)]
            for side in range(3)
            for index in range(blocks)
        ],
        axis=1,
    )
    share = whole.shape[1] // images
    for image in range(images):
        out_ref[image] = jnp.concatenate(
            [whole[:, share * image : share * (image + 1)], ograd_ref[image]], axis=1
        )
    deal(out_ref, scalars[1], targets, sems)


def input_kernel(
    back_ref, weight_ref, x_ref, mgrad_ref, mod_ref, grad_ref, insum_ref, acc_ref,
):
    step = pl.program_id(0)
    blocks = back_ref.shape[0]
    span = HD * HEADS // blocks
    width = x_ref.shape[1]

    rows = pl.ds(pl.multiple_of(span * step, 16), span)
    natural = jnp.concatenate([back_ref[index, rows, :] for index in range(blocks)], axis=0)
    part = lax.dot_general(
        natural, weight_ref[...], (((0,), (1,)), ((), ())), preferred_element_type=jnp.float32
    )

    @pl.when(step == 0)
    def _():
        acc_ref[...] = part

    @pl.when(step > 0)
    def _():
        acc_ref[...] += part

    @pl.when(step == 2)
    def _():
        x = x_ref[...]
        back = acc_ref[...]
        inverse = lax.rsqrt(jnp.mean(x * x, axis=-1, keepdims=True) + EPS)
        unit = x * inverse
        lifted = back * (1.0 + mod_ref[1:2, :])
        grad_ref[...] = mgrad_ref[...] + inverse * (
            lifted - unit * jnp.mean(lifted * unit, axis=-1, keepdims=True)
        )
        insum_ref[...] = jnp.zeros_like(insum_ref)
        insum_ref[0:1, :] = column_sum(back)
        insum_ref[1:2, :] = column_sum(back * unit)


def whole_spec(shape):
    return pl.BlockSpec(tuple(shape), lambda *_, n=len(shape): (0,) * n)


ANY = pl.BlockSpec(memory_space=pl.ANY)
SMEM = pl.BlockSpec(memory_space=pltpu.SMEM)


def call(
    kernel, operands, outs, scratch=(), scalars=None, name=None, micros=5, specs=None, grid=(1,),
    out_specs=None,
):
    return pl.pallas_call(
        kernel,
        out_shape=outs,
        grid_spec=pltpu.PrefetchScalarGridSpec(
            num_scalar_prefetch=0 if scalars is None else 1,
            grid=grid,
            in_specs=[
                (specs or {}).get(index) or whole_spec(a.shape) for index, a in enumerate(operands)
            ],
            out_specs=[
                (out_specs or {}).get(index) or whole_spec(o.shape) for index, o in enumerate(outs)
            ],
            scratch_shapes=list(scratch),
        ),
        cost_estimate=pl.CostEstimate(
            flops=int(micros * 1e9), transcendentals=0, bytes_accessed=int(micros * 1e6)
        ),
        name=name,
    )(*(() if scalars is None else (scalars,)), *operands)


def struct(shape, dtype=jnp.float32):
    return jax.ShapeDtypeStruct(shape, dtype)


PLANE = ("ty", "tx")


def swap(value, bit):
    return lax.ppermute(value, PLANE, [(index, index ^ bit) for index in range(8)])


def first_round(value):
    return swap(value, 2), swap(value, 1), swap(value, 4)


def split_round(xn, yn, half):
    d1 = swap(xn[:half], 4)
    cx = swap(xn, 2)
    d2 = swap(yn[half:], 1)
    return d1, d2, cx, swap(yn, 2)


def second_round(xn, yn):
    return swap(xn, 4), swap(xn, 2), swap(yn, 2)


def tie(*values):
    return lax.optimization_barrier(values)


def exchange(value, axes=PLANE):
    return lax.all_to_all(value, axes, split_axis=0, concat_axis=0, tiled=True)


def shift(value, pairs):
    return lax.ppermute(value, "img", pairs)


def onward(value, step):
    return shift(value, [(i, (i + step) % 4) for i in range(4)])


def add(left, right):
    return (left.astype(jnp.float32) + right.astype(jnp.float32)).astype(jnp.bfloat16)


def line_first(shares):
    return shift(shares[3], [(0, 1), (3, 2)]), shift(shares[3], [(1, 2), (2, 1)])


def line_second(shares, way):
    return (
        shift(add(shares[2], way), [(1, 3), (2, 0)]),
        shift(shares[2], [(0, 2), (3, 1)]),
        shift(shares[1], [(0, 1), (1, 0), (2, 3), (3, 2)]),
    )


def on_plane(
    images,
    block_in,
    bucket,
    tile_anchor,
    cond_table,
    mod_weight,
    mod_bias,
    qkv_weight,
    query_gain,
    key_gain,
    out_weight,
    gate_up_weight,
    down_weight,
    cotangent,
):
    blocks = 8
    _, tile_rows, tile_cols, width = block_in.shape
    tokens = tile_rows * tile_cols
    everyone = blocks * tokens
    hidden_units = down_weight.shape[0]
    units = hidden_units // blocks
    run = units // 2
    lanes = width // units
    heads = HEADS // blocks
    span = heads * HD
    columns = mod_weight.shape[1]
    wide = 3 * heads * LANES
    packed = -(-3 * span // LANES) * LANES
    bf16 = jnp.bfloat16
    image = lax.axis_index("img")
    mine = lax.axis_index("ty") * 2 + lax.axis_index("tx")
    where = jnp.stack([mine, image]).astype(jnp.int32)
    share = width // images
    x = block_in.reshape(tokens, width)
    cot = cotangent.reshape(tokens, width)
    half = tokens // 2
    pay, low_cot = call(
        open_kernel,
        (bucket, tile_anchor.reshape(2), x, cond_table, mod_weight.T, mod_bias, cot),
        (struct((tokens + EXTRA, width), bf16), struct((tokens, width), bf16)),
        [pltpu.VMEM((8, width), jnp.float32)],
        name="open",
        specs={0: SMEM, 1: SMEM},
    )
    core, xn, yn = first_round(pay)
    spread, order, offsets, gains = call(
        functools.partial(ready_kernel, blocks, tile_cols),
        (*[qkv_weight] * 6, query_gain, key_gain),
        (
            struct((width, wide), bf16),
            struct((3 * span, wide), bf16),
            struct((3, tokens, LANES)),
            struct((8, LANES)),
        ),
        [pltpu.VMEM((width, wide), bf16), pltpu.VMEM((wide, wide), bf16)],
        where,
        "ready",
        specs={
            2 * side + n: pl.BlockSpec(
                (width, LANES), lambda i, s, c=side * width // LANES + n: (0, c + s[0])
            )
            for side in range(3)
            for n in range(2)
        },
    )
    xn, yn, spread, order, offsets, gains = tie(xn, yn, spread, order, offsets, gains)
    d1, d2, cx, cy = split_round(xn, yn, half)
    late_gate, late_table, spread, cx = tie(gate_up_weight, cond_table, spread, cx)
    own_gate, own_up, table_share, modw_share = call(
        layout_kernel,
        (*[late_gate] * 4, late_table, mod_weight.T),
        (
            struct((width, units), bf16),
            struct((width, units), bf16),
            struct((cond_table.shape[0], share)),
            struct((columns, share), bf16),
        ),
        scalars=where,
        name="layout",
        specs={
            n: pl.BlockSpec((width, units), lambda i, s, n=n: (0, n * 4 + s[0] // 2))
            for n in range(4)
        },
    )
    d1, d2, cy, own_gate = tie(d1, d2, cy, own_gate)
    pieces = (pay, xn, core, cx, yn, d1, d2, cy, swap(d1, 2), swap(d2, 2))
    c_core, c_xn, c_yn = first_round(low_cot)
    att, hid, qkv, unit, turn, mod, logs, mixed = call(
        functools.partial(attend_kernel, blocks),
        (*pieces, spread, offsets, gains),
        (
            struct((blocks, span, tokens), bf16),
            struct((everyone, width), bf16),
            struct((3 * heads, everyone, LANES), bf16),
            struct((2 * heads, everyone, LANES)),
            struct((2, everyone, LANES)),
            struct((8, width)),
            struct((heads, everyone // (2 * tokens), 2 * tokens)),
            struct((heads, LANES, everyone)),
        ),
        [
            pltpu.VMEM((everyone, width), bf16),
            pltpu.VMEM((blocks, EXTRA, width), bf16),
            pltpu.VMEM((8, width), jnp.float32),
            pltpu.VMEM((1, 6 * width), jnp.float32),
            pltpu.VMEM((2, 8, LANES), jnp.float32),
            pltpu.VMEM((heads, LANES, everyone), bf16),
            pltpu.VMEM((everyone, width), bf16),
            pltpu.VMEM((3 * heads, everyone, LANES), bf16),
            pltpu.VMEM((2 * heads, everyone, LANES), jnp.float32),
            pltpu.VMEM((2, everyone, LANES), jnp.float32),
            pltpu.SemaphoreType.DMA((10,)),
            pltpu.SemaphoreType.DMA((blocks,)),
            pltpu.SemaphoreType.DMA((4,)),
        ],
        where,
        "attend",
        15,
        {index: ANY for index in range(10)},
        out_specs={index: ANY for index in range(1, 5)},
    )
    att, c_core, c_xn, c_yn = tie(att, c_core, c_xn, c_yn)
    att_all = exchange(att)
    c_dn, c_cx, c_cy = second_round(c_xn, c_yn)
    mlp_steps = 4
    step_units = hidden_units // mlp_steps
    (act_grad,) = call(
        act_grad_kernel,
        (down_weight, cot, mod),
        (struct((tokens, hidden_units)),),
        [pltpu.VMEM((tokens, width), bf16)],
        name="act_grad",
        specs={0: pl.BlockSpec((step_units, width), lambda f: (f, 0))},
        out_specs={0: pl.BlockSpec((tokens, step_units), lambda f: (0, f))},
        grid=(mlp_steps,),
    )
    att_all, c_dn, c_cx, c_cy, act_grad = tie(att_all, c_dn, c_cx, c_cy, act_grad)
    cot_pieces = (low_cot, c_xn, c_core, c_cx, c_yn, c_dn, c_cy, swap(c_dn, 2))
    attn_out, middle, hidden_mid = call(
        middle_kernel,
        (att_all, out_weight, x, mod),
        (struct((tokens, width)), struct((tokens, width)), struct((tokens, width), bf16)),
        name="middle",
    )
    h_core, h_xn, h_yn = first_round(hidden_mid)
    early = mlp_steps // 2
    slab = pl.BlockSpec((tokens, step_units), lambda f: (0, f))
    act_first, back_first = call(
        mlp_first_kernel,
        (gate_up_weight, gate_up_weight, hidden_mid, act_grad),
        (struct((tokens, early * step_units), bf16), struct((tokens, width))),
        name="mlp_first",
        micros=7,
        specs={
            0: pl.BlockSpec((width, step_units), lambda f: (0, f)),
            1: pl.BlockSpec((width, step_units), lambda f: (0, mlp_steps + f)),
            3: slab,
        },
        out_specs={0: slab},
        grid=(early,),
    )
    back_first, h_core, h_xn, h_yn = tie(back_first, h_core, h_xn, h_yn)
    h_dn, h_cx, h_cy = second_round(h_xn, h_yn)
    act_second, middle_grad, attn_grad, attg, sums = call(
        mlp_kernel,
        (
            gate_up_weight, gate_up_weight, out_weight, hidden_mid, middle, attn_out, cot, act_grad,
            mod, back_first,
        ),
        (
            struct((tokens, hidden_units - early * step_units), bf16),
            struct((tokens, width)),
            struct((tokens, width), bf16),
            struct((blocks, span, tokens), bf16),
            struct((8, width)),
        ),
        [pltpu.VMEM((tokens, width), jnp.float32)],
        name="mlp",
        micros=8,
        specs={
            0: pl.BlockSpec((width, step_units), lambda f: (0, early + f)),
            1: pl.BlockSpec((width, step_units), lambda f: (0, mlp_steps + early + f)),
            7: pl.BlockSpec((tokens, step_units), lambda f: (0, early + f)),
        },
        out_specs={0: slab},
        grid=(mlp_steps - early,),
    )
    attg, h_dn, h_cx, h_cy = tie(attg, h_dn, h_cx, h_cy)
    attg_all = exchange(attg)
    hid_pieces = (hidden_mid, h_xn, h_core, h_cx, h_yn, h_dn, h_cy, swap(h_dn, 2))
    zrows = run * lanes + width // images
    a_core, a_xn, a_yn = first_round(attn_grad)
    shares = call(
        mlp_weights_kernel,
        (*hid_pieces, *cot_pieces, own_gate, own_up, down_weight, down_weight, mod),
        (struct((zrows, units), bf16),) * 4,
        [
            pltpu.VMEM((everyone, width), bf16),
            pltpu.VMEM((everyone, width), bf16),
            pltpu.VMEM((3, everyone, units), bf16),
            pltpu.VMEM((units, width), bf16),
            pltpu.VMEM((images, zrows, units), bf16),
            pltpu.SemaphoreType.DMA((2, blocks)),
            pltpu.SemaphoreType.DMA((4,)),
        ],
        where,
        "mlp_weights",
        12,
        {
            **{index: ANY for index in range(16)},
            18: pl.BlockSpec((run, width), lambda i, s: (s[0], 0)),
            19: pl.BlockSpec((run, width), lambda i, s: (8 + s[0], 0)),
        },
        out_specs={index: ANY for index in range(4)},
    )
    attg_all, a_core, a_xn, a_yn, *shares = tie(attg_all, a_core, a_xn, a_yn, *shares)
    way, mid = line_first(shares)
    a_dn, a_cx, a_cy = second_round(a_xn, a_yn)
    back, gain_sums = call(
        attend_back_kernel,
        (attg_all, qkv, logs, mixed, gains, unit, turn, order),
        (struct((blocks, 3 * span, tokens), bf16), struct((8, LANES))),
        [
            pltpu.VMEM((heads, LANES, everyone), bf16),
            pltpu.VMEM((heads, everyone, LANES), bf16),
            pltpu.VMEM((heads, LANES, everyone), bf16),
            pltpu.VMEM((3 * heads, everyone, LANES), jnp.float32),
            pltpu.VMEM(unit.shape, jnp.float32),
            pltpu.VMEM(turn.shape, jnp.float32),
            pltpu.VMEM(order.shape, bf16),
            pltpu.SemaphoreType.DMA((3,)),
        ],
        specs={5: ANY, 6: ANY, 7: ANY},
        name="attend_back",
        micros=15,
    )
    back, way, mid, a_dn, a_cx, a_cy = tie(back, way, mid, a_dn, a_cx, a_cy)
    back_all = exchange(back)
    a_cd = swap(a_dn, 2)
    own_back, a_cd, way = tie(back, a_cd, way)
    other, two, near = line_second(shares, way)
    grad_pieces = (attn_grad, a_xn, a_core, a_cx, a_yn, a_dn, a_cy, a_cd)
    (qkv_part,) = call(
        qkv_weights_kernel,
        (hid, own_back),
        (struct((blocks, width // blocks, packed), bf16),),
        name="qkv_weights",
    )
    qkv_part, att = tie(qkv_part, att)
    qkv_rows = exchange(qkv_part)
    (outw_part,) = call(
        functools.partial(out_weights_kernel, images),
        (*grad_pieces, att),
        (struct((images, span, width // images), bf16),),
        [pltpu.VMEM((everyone, width), bf16), pltpu.SemaphoreType.DMA((blocks,))],
        where,
        "out_weights",
        specs={index: ANY for index in range(blocks)},
    )
    back_all, outw_part = tie(back_all, outw_part)
    in_grad, insum = call(
        input_kernel,
        (back_all, qkv_weight, x, middle_grad, mod),
        (struct((tokens, width)), struct((8, width))),
        [pltpu.VMEM((tokens, width), jnp.float32)],
        name="input",
        micros=7,
        specs={1: pl.BlockSpec((width, width), lambda s: (0, s))},
        grid=(3,),
    )
    output, send = call(
        mlp_out_kernel,
        (
            act_first, act_second, down_weight, down_weight, middle, cot, mod, sums, insum,
            gain_sums, bucket,
        ),
        (struct((tokens, width)), struct((images * blocks, 8, LANES))),
        [
            pltpu.VMEM((tokens, width), jnp.float32),
            pltpu.VMEM((1, 6 * width), jnp.float32),
            pltpu.VMEM((blocks, 1024), jnp.float32),
        ],
        name="mlp_out",
        micros=5,
        specs={
            0: slab,
            1: slab,
            2: pl.BlockSpec((step_units, width), lambda f: (f, 0)),
            3: pl.BlockSpec((step_units, width), lambda f: (early + f, 0)),
            10: SMEM,
        },
        grid=(early,),
    )
    send, qkv_rows = tie(send, qkv_rows)
    everywhere = exchange(send, ("img", "ty", "tx"))
    joined = call(
        join_kernel,
        (qkv_rows, outw_part),
        (struct((width // blocks, 4 * share), bf16),) * 4,
        [
            pltpu.VMEM((images, width // blocks, 4 * share), bf16),
            pltpu.SemaphoreType.DMA((4,)),
        ],
        where,
        "join",
        out_specs={index: ANY for index in range(4)},
    )
    way, j_mid = line_first(joined)
    other, way, j_mid = tie(other, way, j_mid)
    j_other, j_two, j_near = line_second(joined, way)
    send_gateup, first, second = call(
        turn_kernel,
        (shares[0], mid, near, two, other),
        (
            struct((blocks, width // blocks, run), bf16),
            struct((share, run), bf16),
            struct((share, run), bf16),
        ),
        scalars=where,
        name="turn",
    )
    modw_total, modb_total, qgain_total, kgain_total, act_send, condition, buckets = call(
        tail_kernel,
        (everywhere, table_share, modw_share),
        (
            struct((share, columns)),
            struct((columns,)),
            struct((HD,)),
            struct((HD,)),
            struct((blocks, 8, share)),
            struct((8, share)),
            struct((8, LANES)),
        ),
        [pltpu.VMEM((8, columns), jnp.float32), pltpu.VMEM((8, share), jnp.float32)],
        name="tail",
    )
    act_parts = exchange(act_send)
    act_parts, send_gateup = tie(act_parts, send_gateup)
    gateup_rows = exchange(send_gateup)
    first = lax.ppermute(first, PLANE, [(t, t // 2 + 4 * (t % 2)) for t in range(8)])
    second = lax.ppermute(second, PLANE, [(t, t // 2 + 4 * (1 - t % 2)) for t in range(8)])
    act_parts, j_other = tie(act_parts, j_other)
    (table_total,) = call(
        table_kernel,
        (act_parts, condition, buckets),
        (struct((cond_table.shape[0] // blocks, share)),),
        scalars=where,
        name="table",
    )
    gateup_rows, table_total = tie(gateup_rows, table_total)
    gateup_total, down_total, qkv_total, outw_total = call(
        lay_kernel,
        (gateup_rows, first, second, joined[0], j_mid, j_near, j_two, j_other),
        (
            struct((width // blocks, blocks * run)),
            struct((share, units)),
            struct((width // blocks, 3 * share)),
            struct((width // blocks, share)),
        ),
        scalars=where,
        name="lay",
    )
    return (
        output.reshape(block_in.shape),
        in_grad.reshape(block_in.shape),
        table_total,
        modw_total,
        modb_total,
        qkv_total,
        qgain_total,
        kgain_total,
        outw_total,
        gateup_total,
        down_total.T,
    )


def solution(mesh):
    sizes = mesh.shape
    fits = sizes["ty"] == 4 and sizes["tx"] == 2 and sizes["img"] == 4
    return jax.shard_map(
        functools.partial(on_plane, sizes["img"]) if fits else on_device,
        mesh=mesh,
        in_specs=(
            P("img", "ty", "tx", None),
            P("img"),
            P("img", "ty", "tx", None),
            P(),
            P(None, ("ty", "tx")),
            P(("ty", "tx")),
            P(),
            P(),
            P(),
            P(),
            P(),
            P(),
            P("img", "ty", "tx", None),
        ),
        out_specs=(
            P("img", "ty", "tx", None),
            P("img", "ty", "tx", None),
            P(("ty", "tx"), "img"),
            P("img", ("ty", "tx")),
            P(("ty", "tx")),
            P(("ty", "tx"), "img"),
            P(),
            P(),
            P(("ty", "tx"), "img"),
            P(("ty", "tx"), "img"),
            P(("ty", "tx"), "img"),
        ),
        check_vma=False,
    )
```
